32 devices in a mesh: groups: 2 (over y), seq: 16 (over z, x, core), mp: 1.
Axes of the slice: x: 2, y: 2, z: 4, core: 2. Of those that a mesh axis runs over, the one named last changes fastest.
Arguments:
- hidden: bfloat16 [7200, 5120], P(('groups', 'seq'), 'mp'), parts along dimension 0, may hold values from -6 to 6
- modulation: float32 [4, 5120], P('groups', 'mp'), parts along dimension 0, may hold values from -3 to 3
- head_weight: bfloat16 [5120, 64], P('mp'), may hold values from -0.078125 to 0.078125
- head_bias: float32 [64], P('mp'), may hold values from -3 to 3
- residual: float32 [64, 7200], P('mp', ('groups', 'seq')), parts along dimension 1, may hold values from -4 to 4
- latent: float32 [64, 7200], P('mp', ('groups', 'seq')), parts along dimension 1, may hold values from -6 to 6
- band_gain: float32 [2, 16], P(None, 'mp'), may hold values from 0.5 to 2
- cut_rows: int32 [2], P('groups'), parts along dimension 0, may hold values from 0 to 45
- cut_cols: int32 [2], P('groups'), parts along dimension 0, may hold values from 0 to 80
- skip_flags: int32 [100], P('groups'), parts along dimension 0, may hold values 0 or 1
- step_index: int32 [2], P('groups'), parts along dimension 0, may hold values from 0 to 49
Outputs:
- velocity: float32 [64, 7200], P('mp', ('groups', 'seq')), parts along dimension 1
- latent_next: float32 [64, 7200], P('mp', ('groups', 'seq')), parts along dimension 1
The draws below stay inside these ranges and needn't reach their ends.
There are 2 independent parts, one for each index of `groups`. The reference program is written for one: setup_inputs(seed, part) draws one part's arguments, and reference() takes and returns one part's arrays. A program takes and returns all parts, laid end to end along the dimension named above; an argument that names none is the same for every part. Nothing has to cross between parts.
Inputs may be any that keep to these rules, and one draw needn't show every extreme that they name: cut_rows[f] and cut_cols[f] belong to frame f.
All inputs are finite; a program needn't handle non-finite values.
Results may differ from the reference program's by a relative error of at most 0.0019.
Values sent between devices are 32-bit elements; how exact they have to be, the bound alone decides.
No kernel may reach another device: no remote copies, remote signals or barrier semaphores. Data moves between devices by JAX's collectives and lax.ppermute only.
A program may use at most 64 MiB of HBM per device.

```python
import math
import jax
import jax.numpy as jnp
from jax import lax

D = 5120
OUTC = 16
PCH = 64
H = 90
W = 160
PH = 45
PW = 80
NSTEP = 50
TOKENS = 3600
FRAMES = 1


def plant(drawn, own_key, smallest, top_value):
    place = [jax.random.randint(jax.random.fold_in(own_key, axis), (), 0, length) for axis, length in enumerate(drawn.shape)]
    main_axis = drawn.shape.index(max(drawn.shape))
    neighbour = place[:main_axis] + [(place[main_axis] + 1) % drawn.shape[main_axis]] + place[main_axis + 1:]
    return drawn.at[tuple(place)].set(smallest).at[tuple(neighbour)].set(top_value)


def shard_levels(stream_key, dims, shards, least, top_value):
    level = 1.0
    for dim, shards_of in shards:
        heights = jax.random.uniform(jax.random.fold_in(jax.random.fold_in(stream_key, 6), dim), (shards_of,), jnp.float32, least / len(shards), top_value / len(shards))
        level = level * jnp.repeat(jnp.exp(heights), dims[dim] // shards_of).reshape((-1,) + (1,) * (len(dims) - 1 - dim))
    return level


def centred(stream_key, extent, width, limit, pieces=(), kind=jnp.bfloat16):
    values = jax.random.normal(stream_key, extent, jnp.float32) * width
    if len(pieces) > 0:
        values = shard_levels(stream_key, extent, pieces, -0.22, 0.18) * values
    return jnp.clip(values, min=-limit, max=limit).astype(kind)


def setup_inputs(seed: int = 0, part: int = 0) -> dict:
    seeds = jax.random.split(jax.random.key(seed), 12)
    part_splits = jax.random.split(jax.random.fold_in(seeds[11], part), 12)
    return {
        "hidden": centred(part_splits[0], (TOKENS, D), 1.0, 6.0, ((0, 16),)),
        "modulation": centred(part_splits[1], (2, D), 0.5, 3.0, (), jnp.float32),
        "head_weight": centred(seeds[2], (D, PCH), D ** -0.5, 0.078125),
        "head_bias": centred(seeds[3], (PCH,), 0.5, 3.0, (), jnp.float32),
        "residual": centred(part_splits[4], (PCH, TOKENS), 0.3, 4.0, ((1, 16),), jnp.float32),
        "latent": centred(part_splits[5], (PCH, TOKENS), 1.0, 6.0, ((1, 16),), jnp.float32),
        "band_gain": jnp.clip(jnp.exp(jax.random.uniform(seeds[6], (2, OUTC), jnp.float32, math.log(0.5), math.log(2.0))), 0.5, 2.0),
        "cut_rows": jax.random.randint(part_splits[7], (FRAMES,), 0, PH + 1).astype(jnp.int32),
        "cut_cols": jax.random.randint(part_splits[8], (FRAMES,), 0, PW + 1).astype(jnp.int32),
        "skip_flags": plant((jax.random.randint(part_splits[9], (NSTEP,), 0, 2) < 1).astype(jnp.int32), jax.random.fold_in(part_splits[9], 1), 0, 1),
        "step_index": jax.random.randint(part_splits[10], (1,), 0, NSTEP).astype(jnp.int32),
    }


EPSILON = 1e-06
GUIDE_EXTRA = 4.0
SHIFT_FACTOR = 5.0

def sigma_at(step_number):
    remain = 1.0 - step_number.astype(jnp.float32) / NSTEP
    return SHIFT_FACTOR * remain / (1.0 + (SHIFT_FACTOR - 1.0) * remain)

def band_weights(skip_flags, step_index, band_gain):
    current = step_index[0]
    counter = jnp.arange(NSTEP, dtype=jnp.int32)
    computed = (skip_flags == 0) & (counter <= current)
    last_full = jnp.max(jnp.where(computed, counter, -1))
    spacing = (current - last_full).astype(jnp.float32)
    gap_ratio = spacing / (spacing + 2.0)
    return (band_gain[0] * (1.0 + gap_ratio), band_gain[1] * (1.0 - 0.5 * gap_ratio))

def reference(hidden, modulation, head_weight, head_bias, residual, latent, band_gain, cut_rows, cut_cols, skip_flags, step_index):
    frame_tokens = PH * PW

    def head_frame(frame_block):
        values = frame_block.astype(jnp.float32)
        average = lax.optimization_barrier(jnp.sum(values, axis=1)) / D
        second = lax.optimization_barrier(jnp.sum(values * values, axis=1)) / D
        scale_inv = lax.rsqrt(second - average * average + EPSILON)
        normed = ((values - average[:, None]) * scale_inv[:, None] * (1.0 + modulation[1]) + modulation[0]).astype(jnp.bfloat16)
        return jnp.dot(normed, head_weight, preferred_element_type=jnp.float32)
    head_frames = lax.map(head_frame, hidden.reshape(FRAMES, frame_tokens, D))
    conditional = head_frames.reshape(TOKENS, PCH).T + head_bias[:, None]
    planes = residual.reshape(OUTC, 2, 2, FRAMES, PH, PW).transpose(3, 0, 4, 1, 5, 2).reshape(FRAMES, OUTC, H, W)
    row_range = jnp.arange(H, dtype=jnp.int32)
    col_range = jnp.arange(W, dtype=jnp.int32)
    rows_freq = jnp.minimum(row_range, H - row_range)
    cols_freq = jnp.minimum(col_range, W - col_range)
    keep_rows = rows_freq[None, :] <= cut_rows[:, None]
    keep_cols = cols_freq[None, :] <= cut_cols[:, None]
    kept_modes = (keep_rows[:, :, None] & keep_cols[:, None, :]).astype(jnp.float32)
    spectrum = jnp.fft.fft2(planes)
    low_planes = jnp.real(jnp.fft.ifft2(spectrum * kept_modes[:, None, :, :])).astype(jnp.float32)
    low_band = low_planes.reshape(FRAMES, OUTC, PH, 2, PW, 2).transpose(1, 3, 5, 0, 2, 4).reshape(PCH, TOKENS)
    high_band = residual - low_band
    w_low, w_high = band_weights(skip_flags, step_index, band_gain)
    row_low = jnp.repeat(w_low, 4)[:, None]
    row_high = jnp.repeat(w_high, 4)[:, None]
    velocity = conditional + GUIDE_EXTRA * (row_low * low_band + row_high * high_band)
    current = step_index[0]
    latent_next = latent + (sigma_at(current + 1) - sigma_at(current)) * velocity
    return (velocity, latent_next)
```

```python
import functools
import math

import jax
import jax.numpy as jnp
from jax import lax
from jax.experimental import pallas as pl
from jax.experimental.pallas import tpu as pltpu
from jax.sharding import PartitionSpec as P

D = 5120
H = 90
W = 160
PH = 45
PW = 80
NSTEP = 50

EPSILON = 1e-06
GUIDE_EXTRA = 4.0
SHIFT_FACTOR = 5.0
HIGHEST = lax.Precision.HIGHEST
LANES = 128


def sigma_at(step_number):
    remain = 1.0 - step_number.astype(jnp.float32) / NSTEP
    return SHIFT_FACTOR * remain / (1.0 + (SHIFT_FACTOR - 1.0) * remain)


def band_weights(skip_flags, step_index, band_gain):
    current = step_index[0]
    counter = jnp.arange(NSTEP, dtype=jnp.int32)
    computed = (skip_flags == 0) & (counter <= current)
    last_full = jnp.max(jnp.where(computed, counter, -1))
    spacing = (current - last_full).astype(jnp.float32)
    gap_ratio = spacing / (spacing + 2.0)
    return (band_gain[0] * (1.0 + gap_ratio), band_gain[1] * (1.0 - 0.5 * gap_ratio))


def band_matrix(rows, cols, length, cutoff):
    modes = jnp.arange(length // 2 + 1, dtype=jnp.int32)
    weight = jnp.where((modes == 0) | (2 * modes == length), 1.0, 2.0) / length
    kept = jnp.where(modes <= cutoff, weight, 0.0)

    def tables(places):
        turns = (places[:, None] * modes[None, :] % length).astype(jnp.float32)
        angles = 2.0 * math.pi / length * turns
        return jnp.cos(angles), jnp.sin(angles)

    row_cos, row_sin = tables(rows)
    col_cos, col_sin = tables(cols)
    return jnp.dot(row_cos * kept, col_cos.T, precision=HIGHEST) + jnp.dot(
        row_sin * kept, col_sin.T, precision=HIGHEST
    )


def split(value):
    high = value.astype(jnp.bfloat16)
    return high, (value - high.astype(jnp.float32)).astype(jnp.bfloat16)


def dot3(left, right):
    lh, ll = left
    rh, rl = right
    dot = functools.partial(jnp.dot, preferred_element_type=jnp.float32)
    return dot(lh, rh) + (dot(ll, rh) + dot(lh, rl))


def mix_kernel(far, near, span, *refs):
    shifts, row_filter, col_filter = refs[:3]
    sources = refs[3 : 3 + far]
    outs = refs[3 + far : 3 + far + near]
    window, lines, rows_even, rows_odd, mixed_even, mixed_odd = refs[3 + far + near :]
    local_rows, local_tokens = sources[0].shape
    channels = local_rows // 4
    width = window.shape[1]
    wide = far * span * 2
    tall = near * span * 2
    window[...] = jnp.zeros_like(window)
    for k in range(far):
        window[:, :local_tokens] = sources[k][...]
        turned = pltpu.roll(window[...], shifts[k], 1)
        for r in range(span):
            lines[r] = pltpu.roll(turned, (width - r * PW) % width, 1)[:, :LANES]
        for r in range(span):
            for dy in range(2):
                place = pl.ds(k * span * 2 + r * 2 + dy, channels, stride=wide)
                rows_even[place, :] = lines[r, pl.ds(2 * dy, channels, stride=4), :]
                rows_odd[place, :] = lines[r, pl.ds(2 * dy + 1, channels, stride=4), :]
    filters = split(col_filter[...])
    even_left = split(rows_even[...])
    odd_left = split(rows_odd[...])
    done = []
    for dx in range(2):
        columns = slice(dx * LANES, (dx + 1) * LANES)
        done.append(
            dot3(even_left, [f[:LANES, columns] for f in filters])
            + dot3(odd_left, [f[LANES:, columns] for f in filters])
        )
    row_left = split(row_filter[...])
    for c in range(channels):
        block = slice(c * wide, (c + 1) * wide)
        place = slice(c * tall, (c + 1) * tall)
        mixed_even[place, :] = dot3(row_left, split(done[0][block]))
        mixed_odd[place, :] = dot3(row_left, split(done[1][block]))
    blank = jnp.zeros((local_rows, width - LANES), jnp.float32)
    for m in range(near):
        for r in range(span):
            for dy in range(2):
                place = pl.ds(m * span * 2 + r * 2 + dy, channels, stride=tall)
                lines[r, pl.ds(2 * dy, channels, stride=4), :] = mixed_even[place, :]
                lines[r, pl.ds(2 * dy + 1, channels, stride=4), :] = mixed_odd[place, :]
        total = jnp.concatenate([lines[0], blank], axis=1)
        for r in range(1, span):
            total += pltpu.roll(jnp.concatenate([lines[r], blank], axis=1), r * PW, 1)
        total = pltpu.roll(total, (width - shifts[far + m]) % width, 1)
        outs[m][...] = total[:, :local_tokens]


def mix(shifts, row_filter, col_filter, sources, near, span):
    far = len(sources)
    local_rows, local_tokens = sources[0].shape
    channels = local_rows // 4
    width = pl.cdiv(span * PW, LANES) * LANES
    wide = channels * far * span * 2
    tall = channels * near * span * 2
    vmem = pl.BlockSpec(memory_space=pltpu.VMEM)
    return pl.pallas_call(
        functools.partial(mix_kernel, far, near, span),
        out_shape=[jax.ShapeDtypeStruct((local_rows, local_tokens), jnp.float32)] * near,
        in_specs=[pl.BlockSpec(memory_space=pltpu.SMEM)] + [vmem] * (2 + far),
        out_specs=[vmem] * near,
        scratch_shapes=[
            pltpu.VMEM((local_rows, width), jnp.float32),
            pltpu.VMEM((span, local_rows, LANES), jnp.float32),
            pltpu.VMEM((wide, LANES), jnp.float32),
            pltpu.VMEM((wide, LANES), jnp.float32),
            pltpu.VMEM((tall, LANES), jnp.float32),
            pltpu.VMEM((tall, LANES), jnp.float32),
        ],
        name="mix",
    )(shifts, row_filter, col_filter, *sources)


def body(
    hidden,
    modulation,
    head_weight,
    head_bias,
    residual,
    latent,
    band_gain,
    cut_rows,
    cut_cols,
    skip_flags,
    step_index,
):
    local_rows, local_tokens = residual.shape
    frame_tokens = PH * PW
    members = frame_tokens // local_tokens
    bits = members.bit_length() - 1
    near = 1 << (bits // 2)
    far = members // near
    places = lax.axis_size("seq")
    seq_index = lax.axis_index("seq")
    position = seq_index % members
    frame_index = seq_index // members

    def exchange(value, mask):
        return lax.ppermute(value, "seq", [(s, s ^ mask) for s in range(places)])

    sources = [residual] + [exchange(residual, k * near) for k in range(1, far)]

    span = max(
        (p * local_tokens % PW + local_tokens + PW - 1) // PW for p in range(members)
    )
    givers = jnp.stack([position ^ (k * near) for k in range(far)])
    takers = jnp.stack([position ^ m for m in range(near)])
    shifts = jnp.concatenate([givers, takers]) * local_tokens % PW

    def pixel_rows(owners):
        first = 2 * (owners * local_tokens // PW)
        return (first[:, None] + jnp.arange(2 * span, dtype=jnp.int32)).reshape(-1)

    row_filter = band_matrix(
        pixel_rows(takers), pixel_rows(givers), H, cut_rows[frame_index]
    )
    columns = jnp.arange(W, dtype=jnp.int32).reshape(PW, 2).T.reshape(-1)
    col_filter = band_matrix(columns, columns, W, cut_cols[frame_index])
    gap = LANES - PW
    col_filter = jnp.pad(
        col_filter.reshape(2, PW, 2, PW), ((0, 0), (0, gap), (0, 0), (0, gap))
    ).reshape(2 * LANES, 2 * LANES)

    values = hidden.astype(jnp.float32)
    moments = lax.psum((jnp.sum(values, axis=1), jnp.sum(values * values, axis=1)), "mp")
    average = moments[0] / D
    scale_inv = lax.rsqrt(moments[1] / D - average * average + EPSILON)
    normed = (
        (values - average[:, None]) * scale_inv[:, None] * (1.0 + modulation[1]) + modulation[0]
    ).astype(jnp.bfloat16)
    conditional = (
        lax.psum_scatter(
            lax.dot_general(
                head_weight, normed, (((0,), (1,)), ((), ())), preferred_element_type=jnp.float32
            ),
            "mp",
            scatter_dimension=0,
            tiled=True,
        )
        + head_bias[:, None]
    )
    w_low, w_high = band_weights(skip_flags, step_index, band_gain)
    row_high = GUIDE_EXTRA * jnp.repeat(w_high, 4)[:, None]
    row_low = GUIDE_EXTRA * jnp.repeat(w_low - w_high, 4)[:, None]
    base = conditional + row_high * residual
    current = step_index[0]
    step = sigma_at(current + 1) - sigma_at(current)

    parts = mix(shifts, row_filter, col_filter, sources, near, span)
    low_band = parts[0]
    for m in range(1, near):
        low_band = low_band + exchange(parts[m], m)
    velocity = base + row_low * low_band
    latent_next = latent + step * velocity
    return (velocity, latent_next)


def solution(mesh):
    in_specs = (
        P(("groups", "seq"), "mp"),
        P("groups", "mp"),
        P("mp", None),
        P("mp"),
        P("mp", ("groups", "seq")),
        P("mp", ("groups", "seq")),
        P(None, "mp"),
        P("groups"),
        P("groups"),
        P("groups"),
        P("groups"),
    )
    out_specs = (P("mp", ("groups", "seq")), P("mp", ("groups", "seq")))
    return jax.shard_map(body, mesh=mesh, in_specs=in_specs, out_specs=out_specs, check_vma=False)
```

```python
import functools
import math

import jax
import jax.numpy as jnp
from jax import lax
from jax.experimental import pallas as pl
from jax.experimental.pallas import tpu as pltpu
from jax.sharding import PartitionSpec as P

D = 5120
H = 90
W = 160
PH = 45
PW = 80
NSTEP = 50

EPSILON = 1e-06
GUIDE_EXTRA = 4.0
SHIFT_FACTOR = 5.0
HIGHEST = lax.Precision.HIGHEST
LANES = 128


def sigma_at(step_number):
    remain = 1.0 - step_number.astype(jnp.float32) / NSTEP
    return SHIFT_FACTOR * remain / (1.0 + (SHIFT_FACTOR - 1.0) * remain)


def band_weights(skip_flags, step_index, band_gain):
    current = step_index[0]
    counter = jnp.arange(NSTEP, dtype=jnp.int32)
    computed = (skip_flags == 0) & (counter <= current)
    last_full = jnp.max(jnp.where(computed, counter, -1))
    spacing = (current - last_full).astype(jnp.float32)
    gap_ratio = spacing / (spacing + 2.0)
    return (band_gain[0] * (1.0 + gap_ratio), band_gain[1] * (1.0 - 0.5 * gap_ratio))


def band_matrix(rows, cols, length, cutoff):
    modes = jnp.arange(length // 2 + 1, dtype=jnp.int32)
    weight = jnp.where((modes == 0) | (2 * modes == length), 1.0, 2.0) / length
    kept = jnp.where(modes <= cutoff, weight, 0.0)

    def tables(places):
        turns = (places[:, None] * modes[None, :] % length).astype(jnp.float32)
        angles = 2.0 * math.pi / length * turns
        return jnp.cos(angles), jnp.sin(angles)

    row_cos, row_sin = tables(rows)
    col_cos, col_sin = tables(cols)
    return jnp.dot(row_cos * kept, col_cos.T, precision=HIGHEST) + jnp.dot(
        row_sin * kept, col_sin.T, precision=HIGHEST
    )


def split(value):
    high = value.astype(jnp.bfloat16)
    return high, (value - high.astype(jnp.float32)).astype(jnp.bfloat16)


def dot3(left, right):
    lh, ll = left
    rh, rl = right
    dot = functools.partial(jnp.dot, preferred_element_type=jnp.float32)
    return dot(lh, rh) + (dot(ll, rh) + dot(lh, rl))


def mix_kernel(far, near, span, *refs):
    shifts, row_filter, col_filter = refs[:3]
    sources = refs[3 : 3 + far]
    outs = refs[3 + far : 3 + far + near]
    window, lines, rows_even, rows_odd, mixed_even, mixed_odd = refs[3 + far + near :]
    local_rows, local_tokens = sources[0].shape
    channels = local_rows // 4
    width = window.shape[1]
    wide = far * span * 2
    tall = near * span * 2
    window[...] = jnp.zeros_like(window)
    for k in range(far):
        window[:, :local_tokens] = sources[k][...]
        turned = pltpu.roll(window[...], shifts[k], 1)
        for r in range(span):
            lines[r] = pltpu.roll(turned, (width - r * PW) % width, 1)[:, :LANES]
        for r in range(span):
            for dy in range(2):
                place = pl.ds(k * span * 2 + r * 2 + dy, channels, stride=wide)
                rows_even[place, :] = lines[r, pl.ds(2 * dy, channels, stride=4), :]
                rows_odd[place, :] = lines[r, pl.ds(2 * dy + 1, channels, stride=4), :]
    filters = split(col_filter[...])
    even_left = split(rows_even[...])
    odd_left = split(rows_odd[...])
    done = []
    for dx in range(2):
        columns = slice(dx * LANES, (dx + 1) * LANES)
        done.append(
            dot3(even_left, [f[:LANES, columns] for f in filters])
            + dot3(odd_left, [f[LANES:, columns] for f in filters])
        )
    row_left = split(row_filter[...])
    for c in range(channels):
        block = slice(c * wide, (c + 1) * wide)
        place = slice(c * tall, (c + 1) * tall)
        mixed_even[place, :] = dot3(row_left, split(done[0][block]))
        mixed_odd[place, :] = dot3(row_left, split(done[1][block]))
    blank = jnp.zeros((local_rows, width - LANES), jnp.float32)
    for m in range(near):
        for r in range(span):
            for dy in range(2):
                place = pl.ds(m * span * 2 + r * 2 + dy, channels, stride=tall)
                lines[r, pl.ds(2 * dy, channels, stride=4), :] = mixed_even[place, :]
                lines[r, pl.ds(2 * dy + 1, channels, stride=4), :] = mixed_odd[place, :]
        total = jnp.concatenate([lines[0], blank], axis=1)
        for r in range(1, span):
            total += pltpu.roll(jnp.concatenate([lines[r], blank], axis=1), r * PW, 1)
        total = pltpu.roll(total, (width - shifts[far + m]) % width, 1)
        outs[m][...] = total[:, :local_tokens]


def mix(shifts, row_filter, col_filter, sources, near, span):
    far = len(sources)
    local_rows, local_tokens = sources[0].shape
    channels = local_rows // 4
    width = pl.cdiv(span * PW, LANES) * LANES
    wide = channels * far * span * 2
    tall = channels * near * span * 2
    vmem = pl.BlockSpec(memory_space=pltpu.VMEM)
    return pl.pallas_call(
        functools.partial(mix_kernel, far, near, span),
        out_shape=[jax.ShapeDtypeStruct((local_rows, local_tokens), jnp.float32)] * near,
        in_specs=[pl.BlockSpec(memory_space=pltpu.SMEM)] + [vmem] * (2 + far),
        out_specs=[vmem] * near,
        scratch_shapes=[
            pltpu.VMEM((local_rows, width), jnp.float32),
            pltpu.VMEM((span, local_rows, LANES), jnp.float32),
            pltpu.VMEM((wide, LANES), jnp.float32),
            pltpu.VMEM((wide, LANES), jnp.float32),
            pltpu.VMEM((tall, LANES), jnp.float32),
            pltpu.VMEM((tall, LANES), jnp.float32),
        ],
        compiler_params=pltpu.CompilerParams(vmem_limit_bytes=8 * 2**20),
        name="mix",
    )(shifts, row_filter, col_filter, *sources)


def body(
    hidden,
    modulation,
    head_weight,
    head_bias,
    residual,
    latent,
    band_gain,
    cut_rows,
    cut_cols,
    skip_flags,
    step_index,
):
    local_rows, local_tokens = residual.shape
    frame_tokens = PH * PW
    members = frame_tokens // local_tokens
    bits = members.bit_length() - 1
    near = 1 << (bits // 2)
    far = members // near
    places = lax.axis_size("seq")
    seq_index = lax.axis_index("seq")
    position = seq_index % members
    frame_index = seq_index // members

    def exchange(value, mask):
        return lax.ppermute(value, "seq", [(s, s ^ mask) for s in range(places)])

    sources = [residual] + [exchange(residual, k * near) for k in range(1, far)]

    span = max(
        (p * local_tokens % PW + local_tokens + PW - 1) // PW for p in range(members)
    )
    givers = jnp.stack([position ^ (k * near) for k in range(far)])
    takers = jnp.stack([position ^ m for m in range(near)])
    shifts = jnp.concatenate([givers, takers]) * local_tokens % PW

    def pixel_rows(owners):
        first = 2 * (owners * local_tokens // PW)
        return (first[:, None] + jnp.arange(2 * span, dtype=jnp.int32)).reshape(-1)

    row_filter = band_matrix(
        pixel_rows(takers), pixel_rows(givers), H, cut_rows[frame_index]
    )
    columns = jnp.arange(W, dtype=jnp.int32).reshape(PW, 2).T.reshape(-1)
    col_filter = band_matrix(columns, columns, W, cut_cols[frame_index])
    gap = LANES - PW
    col_filter = jnp.pad(
        col_filter.reshape(2, PW, 2, PW), ((0, 0), (0, gap), (0, 0), (0, gap))
    ).reshape(2 * LANES, 2 * LANES)

    values = hidden.astype(jnp.float32)
    moments = lax.psum((jnp.sum(values, axis=1), jnp.sum(values * values, axis=1)), "mp")
    average = moments[0] / D
    scale_inv = lax.rsqrt(moments[1] / D - average * average + EPSILON)
    normed = (
        (values - average[:, None]) * scale_inv[:, None] * (1.0 + modulation[1]) + modulation[0]
    ).astype(jnp.bfloat16)
    conditional = (
        lax.psum_scatter(
            lax.dot_general(
                head_weight, normed, (((0,), (1,)), ((), ())), preferred_element_type=jnp.float32
            ),
            "mp",
            scatter_dimension=0,
            tiled=True,
        )
        + head_bias[:, None]
    )
    w_low, w_high = band_weights(skip_flags, step_index, band_gain)
    row_high = GUIDE_EXTRA * jnp.repeat(w_high, 4)[:, None]
    row_low = GUIDE_EXTRA * jnp.repeat(w_low - w_high, 4)[:, None]
    base = conditional + row_high * residual
    current = step_index[0]
    step = sigma_at(current + 1) - sigma_at(current)

    parts = mix(shifts, row_filter, col_filter, sources, near, span)
    low_band = parts[0]
    for m in range(1, near):
        low_band = low_band + exchange(parts[m], m)
    velocity = base + row_low * low_band
    latent_next = latent + step * velocity
    return (velocity, latent_next)


def solution(mesh):
    in_specs = (
        P(("groups", "seq"), "mp"),
        P("groups", "mp"),
        P("mp", None),
        P("mp"),
        P("mp", ("groups", "seq")),
        P("mp", ("groups", "seq")),
        P(None, "mp"),
        P("groups"),
        P("groups"),
        P("groups"),
        P("groups"),
    )
    out_specs = (P("mp", ("groups", "seq")), P("mp", ("groups", "seq")))
    return jax.shard_map(body, mesh=mesh, in_specs=in_specs, out_specs=out_specs, check_vma=False)
```

```python
import functools
import math

import jax
import jax.numpy as jnp
from jax import lax
from jax.experimental import pallas as pl
from jax.experimental.pallas import tpu as pltpu
from jax.sharding import PartitionSpec as P


D = 5120
H = 90
W = 160
PH = 45
PW = 80
NSTEP = 50

EPSILON = 1e-06
GUIDE_EXTRA = 4.0
SHIFT_FACTOR = 5.0
LANES = 128


def sigma_at(step_number):
    remain = 1.0 - step_number.astype(jnp.float32) / NSTEP
    return SHIFT_FACTOR * remain / (1.0 + (SHIFT_FACTOR - 1.0) * remain)


def band_weights(skip_flags, step_index, band_gain):
    current = step_index[0]
    counter = jnp.arange(NSTEP, dtype=jnp.int32)
    computed = (skip_flags == 0) & (counter <= current)
    last_full = jnp.max(jnp.where(computed, counter, -1))
    spacing = (current - last_full).astype(jnp.float32)
    gap_ratio = spacing / (spacing + 2.0)
    return (band_gain[0] * (1.0 + gap_ratio), band_gain[1] * (1.0 - 0.5 * gap_ratio))


def split(value):
    high = value.astype(jnp.bfloat16)
    return high, (value - high.astype(jnp.float32)).astype(jnp.bfloat16)


def dot3(left, right, contract=((1,), (0,))):
    (lh, ll), (rh, rl) = left, right

    def dot(one, other):
        return lax.dot_general(
            one, other, (contract, ((), ())), preferred_element_type=jnp.float32
        )

    return dot(lh, rh) + (dot(ll, rh) + dot(lh, rl))


def iota(shape, axis):
    return lax.broadcasted_iota(jnp.int32, shape, axis)


class Layout:
    def __init__(self, local_rows, local_tokens):
        self.rows = local_rows
        self.tokens = local_tokens
        self.channels = local_rows // 4
        self.members = PH * PW // local_tokens
        bits = self.members.bit_length() - 1
        self.near = 1 << (bits // 2)
        self.far = self.members // self.near
        self.span = max(
            (p * local_tokens % PW + local_tokens + PW - 1) // PW
            for p in range(self.members)
        )
        self.lines = 2 * self.span
        self.groups = pl.cdiv(self.span * PW, LANES)

    def owners(self, position):
        givers = [position ^ (k * self.near) for k in range(self.far)]
        takers = [position ^ m for m in range(self.near)]
        return givers, takers

    def offset(self, owner):
        return lax.rem(owner * self.tokens, PW)

    def first_line(self, owner):
        return 2 * (owner * self.tokens // PW)


def wave_tables(places, length, cutoff):
    modes = iota(places.shape, 1)
    turns = lax.rem(places * modes, length).astype(jnp.float32)
    angles = turns * (2.0 * math.pi / length)
    table = jnp.concatenate([jnp.cos(angles), jnp.sin(angles)], axis=1)
    weight = jnp.where((modes == 0) | (2 * modes == length), 1.0, 2.0) / length
    kept = jnp.where((modes <= cutoff) & (2 * modes <= length), weight, 0.0)
    return table, jnp.concatenate([kept, kept], axis=1)


def bands_kernel(layout, cut_rows, cut_cols, col_high, col_low, row_high, row_low):
    seq_index = lax.axis_index("seq")
    position = lax.rem(seq_index, layout.members)
    frame = seq_index // layout.members
    shape = (2 * LANES, LANES)
    line = iota(shape, 0)
    odd = line >= LANES
    column = jnp.where(odd, line - LANES, line)
    table, kept = wave_tables(2 * column + odd.astype(jnp.int32), W, cut_cols[frame])
    table = jnp.where(jnp.concatenate([column, column], axis=1) < PW, table, 0.0)
    high, low = split(dot3(split(table * kept), split(table), ((1,), (1,))))
    col_high[...] = high
    col_low[...] = low

    def tables(owners):
        shape = (len(owners) * layout.lines, LANES)
        line = iota(shape, 0)
        places = line
        for n, owner in enumerate(owners):
            start = layout.first_line(owner) - n * layout.lines
            places = jnp.where(line >= n * layout.lines, line + start, places)
        return wave_tables(places, H, cut_rows[frame])

    givers, takers = layout.owners(position)
    given, kept = tables(givers)
    taken, _ = tables(takers)
    small = dot3(split(taken), split(given * kept), ((1,), (1,)))
    wide = given.shape[0]
    size = wide * layout.channels
    spread = (iota((wide, size), 1) // layout.channels == iota((wide, size), 0)).astype(
        jnp.bfloat16
    )
    shape = (layout.channels, size)
    same = lax.rem(iota(shape, 1), layout.channels) == iota(shape, 0)
    for part, out in zip(split(small), (row_high, row_low)):
        repeated = jnp.dot(part, spread, preferred_element_type=jnp.float32)
        for n in range(taken.shape[0]):
            block = jnp.where(same, repeated[n : n + 1], 0.0)
            place = slice(n * layout.channels, (n + 1) * layout.channels)
            out[place, :] = block.astype(jnp.bfloat16)


def mix_kernel(layout, *refs):
    far, near, span, groups = layout.far, layout.near, layout.span, layout.groups
    channels, tokens = layout.channels, layout.tokens
    col_high, col_low, row_high, row_low = refs[:4]
    sources = refs[4 : 4 + far]
    outs = refs[4 + far : 4 + far + near]
    window, lines, data_high, data_low = refs[4 + far + near :]
    givers, takers = layout.owners(lax.rem(lax.axis_index("seq"), layout.members))
    lane = iota((layout.rows, LANES), 1)
    chunks = window.shape[1] // LANES
    blank = jnp.zeros((layout.rows, LANES), jnp.float32)
    window[...] = jnp.zeros_like(window)
    for k in range(far):
        window[:, :tokens] = sources[k][...]
        offset = layout.offset(givers[k])
        turned = [
            pltpu.roll(window[:, g * LANES : (g + 1) * LANES], offset, 1) for g in range(chunks)
        ]
        turned = [blank] + turned + [blank] * (groups - chunks)
        placed = [jnp.where(lane >= offset, turned[g + 1], turned[g]) for g in range(groups)]
        for r in range(span):
            group, start = divmod(r * PW, LANES)
            if start == 0:
                line = placed[group]
            else:
                line = pltpu.roll(placed[group], LANES - start, 1)
                if start + PW > LANES:
                    rest = pltpu.roll(placed[group + 1], LANES - start, 1)
                    line = jnp.where(lane < LANES - start, line, rest)
            lines[r] = line
        for r in range(span):
            for dy in range(2):
                first = ((k * span + r) * 2 + dy) * channels
                for dx in range(2):
                    high, low = split(lines[r, pl.ds(2 * dy + dx, channels, stride=4), :])
                    place = (slice(first, first + channels), slice(dx * LANES, (dx + 1) * LANES))
                    data_high[place] = high
                    data_low[place] = low
    mixed = dot3((data_high[...], data_low[...]), (col_high[...], col_low[...]))
    mixed = dot3((row_high[...], row_low[...]), split(mixed))
    lane = iota((channels, LANES), 1)
    for m in range(near):
        offset = layout.offset(takers[m])
        back = lax.rem(LANES - offset, LANES)
        for dy in range(2):
            for dx in range(2):
                placed = [None] * (groups + 1)

                def put(group, value):
                    old = placed[group]
                    placed[group] = value if old is None else old + value

                for r in range(span):
                    first = ((m * span + r) * 2 + dy) * channels
                    line = mixed[first : first + channels, dx * LANES : (dx + 1) * LANES]
                    group, start = divmod(r * PW, LANES)
                    if start:
                        line = pltpu.roll(line, start, 1)
                    if start + PW <= LANES:
                        put(group, line)
                    else:
                        put(group, jnp.where(lane >= start, line, 0.0))
                        put(group + 1, jnp.where(lane < start, line, 0.0))
                turned = [pltpu.roll(p, back, 1) for p in placed[:groups]]
                first = (dy * 2 + dx) * channels
                for g in range(pl.cdiv(tokens, LANES)):
                    value = jnp.where(lane < LANES - offset, turned[g], turned[g + 1])
                    last = min(tokens, (g + 1) * LANES)
                    outs[m][first : first + channels, g * LANES : last] = value[
                        :, : last - g * LANES
                    ]


def finish_kernel(layout, *refs):
    near, channels, tokens = layout.near, layout.channels, layout.tokens
    parts = refs[:near]
    base, row_low, step, latent, velocity, latent_next, total = refs[near:]
    for g in range(total.shape[0]):
        last = min(tokens, (g + 1) * LANES)
        columns = slice(g * LANES, last)
        width = slice(0, last - g * LANES)
        low_band = parts[0][:, columns]
        for m in range(1, near):
            low_band += parts[m][:, columns]
        total[g, :, width] = low_band
        for c in range(channels):
            rows = slice(4 * c, 4 * c + 4)
            low_band = total[g, pl.ds(c, 4, stride=channels), :][:, width]
            value = base[rows, columns] + row_low[rows, columns] * low_band
            velocity[rows, columns] = value
            latent_next[rows, columns] = latent[rows, columns] + step[rows, columns] * value


VMEM = pl.BlockSpec(memory_space=pltpu.VMEM)
SMEM = pl.BlockSpec(memory_space=pltpu.SMEM)


def bands(layout, cut_rows, cut_cols):
    wide = layout.far * layout.lines * layout.channels
    tall = layout.near * layout.lines * layout.channels
    col = jax.ShapeDtypeStruct((2 * LANES, 2 * LANES), jnp.bfloat16)
    row = jax.ShapeDtypeStruct((tall, wide), jnp.bfloat16)
    return pl.pallas_call(
        functools.partial(bands_kernel, layout),
        out_shape=[col, col, row, row],
        in_specs=[SMEM, SMEM],
        out_specs=[VMEM] * 4,
        compiler_params=pltpu.CompilerParams(vmem_limit_bytes=8 * 2**20),
        cost_estimate=pl.CostEstimate(flops=10**8, bytes_accessed=10**6, transcendentals=0),
        name="bands",
    )(cut_rows, cut_cols)


def mix(layout, filters, sources):
    wide = layout.far * layout.lines * layout.channels
    shape = (layout.rows, layout.tokens)
    data = pltpu.VMEM((wide, 2 * LANES), jnp.bfloat16)
    return pl.pallas_call(
        functools.partial(mix_kernel, layout),
        out_shape=[jax.ShapeDtypeStruct(shape, jnp.float32)] * layout.near,
        in_specs=[VMEM] * (4 + layout.far),
        out_specs=[VMEM] * layout.near,
        scratch_shapes=[
            pltpu.VMEM((layout.rows, pl.cdiv(layout.tokens, LANES) * LANES), jnp.float32),
            pltpu.VMEM((layout.span, layout.rows, LANES), jnp.float32),
            data,
            data,
        ],
        compiler_params=pltpu.CompilerParams(vmem_limit_bytes=8 * 2**20),
        cost_estimate=pl.CostEstimate(flops=10**9, bytes_accessed=10**6, transcendentals=0),
        name="mix",
    )(*filters, *sources)


def finish(layout, parts, base, row_low, step, latent):
    shape = jax.ShapeDtypeStruct((layout.rows, layout.tokens), jnp.float32)
    return pl.pallas_call(
        functools.partial(finish_kernel, layout),
        out_shape=[shape, shape],
        in_specs=[VMEM] * (layout.near + 4),
        out_specs=[VMEM, VMEM],
        scratch_shapes=[
            pltpu.VMEM((pl.cdiv(layout.tokens, LANES), layout.rows, LANES), jnp.float32)
        ],
        compiler_params=pltpu.CompilerParams(vmem_limit_bytes=8 * 2**20),
        name="finish",
    )(*parts, base, row_low, step, latent)


def body(
    hidden,
    modulation,
    head_weight,
    head_bias,
    residual,
    latent,
    band_gain,
    cut_rows,
    cut_cols,
    skip_flags,
    step_index,
):
    layout = Layout(*residual.shape)
    places = lax.axis_size("seq")

    def exchange(values, unit):
        swapped = [values[0]] * len(values)
        for n in [*range(2, len(values)), 1]:
            pairs = [(s, s ^ (n * unit)) for s in range(places)]
            swapped[n] = lax.ppermute(values[n], "seq", pairs)
        return swapped

    sources = exchange([residual] * layout.far, layout.near)
    filters = bands(layout, cut_rows, cut_cols)
    values = hidden.astype(jnp.float32)
    moments = lax.psum((jnp.sum(values, axis=1), jnp.sum(values * values, axis=1)), "mp")
    average = moments[0] / D
    scale_inv = lax.rsqrt(moments[1] / D - average * average + EPSILON)
    normed = (
        (values - average[:, None]) * scale_inv[:, None] * (1.0 + modulation[1]) + modulation[0]
    ).astype(jnp.bfloat16)
    conditional = (
        lax.psum_scatter(
            lax.dot_general(
                head_weight, normed, (((0,), (1,)), ((), ())), preferred_element_type=jnp.float32
            ),
            "mp",
            scatter_dimension=0,
            tiled=True,
        )
        + head_bias[:, None]
    )
    w_low, w_high = band_weights(skip_flags, step_index, band_gain)
    row_high = GUIDE_EXTRA * jnp.repeat(w_high, 4)[:, None]
    row_low = GUIDE_EXTRA * jnp.repeat(w_low - w_high, 4)[:, None]
    base = conditional + row_high * residual
    current = step_index[0]
    step = sigma_at(current + 1) - sigma_at(current)

    parts = mix(layout, filters, sources)
    parts = exchange(parts, 1)
    shape = residual.shape
    return finish(
        layout,
        parts,
        base,
        jnp.broadcast_to(row_low, shape),
        jnp.broadcast_to(step, shape),
        latent,
    )


def solution(mesh):
    in_specs = (
        P(("groups", "seq"), "mp"),
        P("groups", "mp"),
        P("mp", None),
        P("mp"),
        P("mp", ("groups", "seq")),
        P("mp", ("groups", "seq")),
        P(None, "mp"),
        P("groups"),
        P("groups"),
        P("groups"),
        P("groups"),
    )
    out_specs = (P("mp", ("groups", "seq")), P("mp", ("groups", "seq")))
    return jax.shard_map(body, mesh=mesh, in_specs=in_specs, out_specs=out_specs, check_vma=False)
```

```python
import functools
import math

import jax
import jax.numpy as jnp
from jax import lax
from jax.experimental import pallas as pl
from jax.experimental.pallas import tpu as pltpu
from jax.sharding import PartitionSpec as P


D = 5120
H = 90
W = 160
PH = 45
PW = 80
NSTEP = 50

EPSILON = 1e-06
GUIDE_EXTRA = 4.0
SHIFT_FACTOR = 5.0
LANES = 128


def sigma_at(step_number):
    remain = 1.0 - step_number.astype(jnp.float32) / NSTEP
    return SHIFT_FACTOR * remain / (1.0 + (SHIFT_FACTOR - 1.0) * remain)


def band_weights(skip_flags, step_index, band_gain):
    current = step_index[0]
    counter = jnp.arange(NSTEP, dtype=jnp.int32)
    computed = (skip_flags == 0) & (counter <= current)
    last_full = jnp.max(jnp.where(computed, counter, -1))
    spacing = (current - last_full).astype(jnp.float32)
    gap_ratio = spacing / (spacing + 2.0)
    return (band_gain[0] * (1.0 + gap_ratio), band_gain[1] * (1.0 - 0.5 * gap_ratio))


def split(value):
    high = value.astype(jnp.bfloat16)
    return high, (value - high.astype(jnp.float32)).astype(jnp.bfloat16)


def dot3(left, right, contract=((1,), (0,))):
    (lh, ll), (rh, rl) = left, right

    def dot(one, other):
        return lax.dot_general(
            one, other, (contract, ((), ())), preferred_element_type=jnp.float32
        )

    return dot(lh, rh) + (dot(ll, rh) + dot(lh, rl))


def iota(shape, axis):
    return lax.broadcasted_iota(jnp.int32, shape, axis)


class Layout:
    def __init__(self, local_rows, local_tokens):
        self.rows = local_rows
        self.tokens = local_tokens
        self.channels = local_rows // 4
        self.members = PH * PW // local_tokens
        bits = self.members.bit_length() - 1
        self.near = 1 << (bits // 2)
        self.far = self.members // self.near
        self.span = max(
            (p * local_tokens % PW + local_tokens + PW - 1) // PW
            for p in range(self.members)
        )
        self.lines = 2 * self.span
        self.groups = pl.cdiv(self.span * PW, LANES)

    def owners(self, position):
        givers = [position ^ (k * self.near) for k in self.order(self.far)]
        takers = [position ^ m for m in range(self.near)]
        return givers, takers

    def order(self, count):
        return [0, *range(2, count), 1][:count]

    def offset(self, owner):
        return lax.rem(owner * self.tokens, PW)

    def first_line(self, owner):
        return 2 * (owner * self.tokens // PW)


def wave_tables(places, length, cutoff):
    modes = iota(places.shape, 1)
    turns = lax.rem(places * modes, length).astype(jnp.float32)
    angles = turns * (2.0 * math.pi / length)
    table = jnp.concatenate([jnp.cos(angles), jnp.sin(angles)], axis=1)
    weight = jnp.where((modes == 0) | (2 * modes == length), 1.0, 2.0) / length
    kept = jnp.where((modes <= cutoff) & (2 * modes <= length), weight, 0.0)
    return table, jnp.concatenate([kept, kept], axis=1)


def bands_kernel(layout, cut_rows, cut_cols, col_high, col_low, row_high, row_low):
    seq_index = lax.axis_index("seq")
    position = lax.rem(seq_index, layout.members)
    frame = seq_index // layout.members
    shape = (2 * LANES, LANES)
    line = iota(shape, 0)
    odd = line >= LANES
    column = jnp.where(odd, line - LANES, line)
    table, kept = wave_tables(2 * column + odd.astype(jnp.int32), W, cut_cols[frame])
    table = jnp.where(jnp.concatenate([column, column], axis=1) < PW, table, 0.0)
    high, low = split(dot3(split(table * kept), split(table), ((1,), (1,))))
    col_high[...] = high
    col_low[...] = low

    def tables(owners):
        shape = (len(owners) * layout.lines, LANES)
        line = iota(shape, 0)
        places = line
        for n, owner in enumerate(owners):
            start = layout.first_line(owner) - n * layout.lines
            places = jnp.where(line >= n * layout.lines, line + start, places)
        return wave_tables(places, H, cut_rows[frame])

    givers, takers = layout.owners(position)
    given, kept = tables(givers)
    taken, _ = tables(takers)
    small = dot3(split(taken), split(given * kept), ((1,), (1,)))
    wide = given.shape[0]
    size = wide * layout.channels
    spread = (iota((wide, size), 1) // layout.channels == iota((wide, size), 0)).astype(
        jnp.bfloat16
    )
    shape = (layout.channels, size)
    same = lax.rem(iota(shape, 1), layout.channels) == iota(shape, 0)
    for part, out in zip(split(small), (row_high, row_low)):
        repeated = jnp.dot(part, spread, preferred_element_type=jnp.float32)
        for n in range(taken.shape[0]):
            block = jnp.where(same, repeated[n : n + 1], 0.0)
            place = slice(n * layout.channels, (n + 1) * layout.channels)
            out[place, :] = block.astype(jnp.bfloat16)


def filtered(layout, slots, sources, filters, scratch):
    span, groups, channels, tokens = layout.span, layout.groups, layout.channels, layout.tokens
    col_high, col_low, row_high, row_low = filters
    window, lines, data_high, data_low = scratch
    givers, _ = layout.owners(lax.rem(lax.axis_index("seq"), layout.members))
    lane = iota((layout.rows, LANES), 1)
    chunks = window.shape[1] // LANES
    blank = jnp.zeros((layout.rows, LANES), jnp.float32)
    window[...] = jnp.zeros_like(window)
    for k, (slot, source) in enumerate(zip(slots, sources)):
        window[:, :tokens] = source[...]
        offset = layout.offset(givers[slot])
        turned = [
            pltpu.roll(window[:, g * LANES : (g + 1) * LANES], offset, 1) for g in range(chunks)
        ]
        turned = [blank] + turned + [blank] * (groups - chunks)
        placed = [jnp.where(lane >= offset, turned[g + 1], turned[g]) for g in range(groups)]
        for r in range(span):
            group, start = divmod(r * PW, LANES)
            if start == 0:
                line = placed[group]
            else:
                line = pltpu.roll(placed[group], LANES - start, 1)
                if start + PW > LANES:
                    rest = pltpu.roll(placed[group + 1], LANES - start, 1)
                    line = jnp.where(lane < LANES - start, line, rest)
            lines[r] = line
        for r in range(span):
            for dy in range(2):
                first = ((k * span + r) * 2 + dy) * channels
                for dx in range(2):
                    high, low = split(lines[r, pl.ds(2 * dy + dx, channels, stride=4), :])
                    place = (slice(first, first + channels), slice(dx * LANES, (dx + 1) * LANES))
                    data_high[place] = high
                    data_low[place] = low
    mixed = dot3((data_high[...], data_low[...]), (col_high[...], col_low[...]))
    each = layout.lines * channels
    columns = slice(slots[0] * each, (slots[-1] + 1) * each)
    return dot3((row_high[:, columns], row_low[:, columns]), split(mixed))


def early_kernel(layout, slots, *refs):
    sources = refs[4 : 4 + len(slots)]
    carry = refs[4 + len(slots)]
    carry[...] = filtered(layout, slots, sources, refs[:4], refs[5 + len(slots) :])


def mix_kernel(layout, slots, *refs):
    near, span, groups = layout.near, layout.span, layout.groups
    channels, tokens = layout.channels, layout.tokens
    carry = refs[4]
    sources = refs[5 : 5 + len(slots)]
    outs = refs[5 + len(slots) : 5 + len(slots) + near]
    scratch = refs[5 + len(slots) + near :]
    mixed = carry[...] + filtered(layout, slots, sources, refs[:4], scratch)
    _, takers = layout.owners(lax.rem(lax.axis_index("seq"), layout.members))
    lane = iota((channels, LANES), 1)
    for m in range(near):
        offset = layout.offset(takers[m])
        back = lax.rem(LANES - offset, LANES)
        for dy in range(2):
            for dx in range(2):
                placed = [None] * (groups + 1)

                def put(group, value):
                    old = placed[group]
                    placed[group] = value if old is None else old + value

                for r in range(span):
                    first = ((m * span + r) * 2 + dy) * channels
                    line = mixed[first : first + channels, dx * LANES : (dx + 1) * LANES]
                    group, start = divmod(r * PW, LANES)
                    if start:
                        line = pltpu.roll(line, start, 1)
                    if start + PW <= LANES:
                        put(group, line)
                    else:
                        put(group, jnp.where(lane >= start, line, 0.0))
                        put(group + 1, jnp.where(lane < start, line, 0.0))
                turned = [pltpu.roll(p, back, 1) for p in placed[:groups]]
                first = (dy * 2 + dx) * channels
                for g in range(pl.cdiv(tokens, LANES)):
                    value = jnp.where(lane < LANES - offset, turned[g], turned[g + 1])
                    last = min(tokens, (g + 1) * LANES)
                    outs[m][first : first + channels, g * LANES : last] = value[
                        :, : last - g * LANES
                    ]


def head_kernel(
    layout,
    hidden,
    modulation,
    weight,
    bias,
    residual,
    band_gain,
    skip_flags,
    step_index,
    base,
    row_low,
    step,
    normed,
):
    tokens, width = hidden.shape
    tiles = width // LANES
    block = 16

    def norm(rows):
        count = rows.size if isinstance(rows, pl.Slice) else rows.stop - rows.start
        sums = [jnp.zeros((count, LANES), jnp.float32) for _ in range(4)]
        squares = list(sums)
        for t in range(tiles):
            value = hidden[rows, t * LANES : (t + 1) * LANES].astype(jnp.float32)
            sums[t % 4] += value
            squares[t % 4] += value * value
        total = jnp.sum((sums[0] + sums[1]) + (sums[2] + sums[3]), axis=1, keepdims=True)
        square = jnp.sum(
            (squares[0] + squares[1]) + (squares[2] + squares[3]), axis=1, keepdims=True
        )
        average = total / D
        scale_inv = lax.rsqrt(square / D - average * average + EPSILON)
        average = jnp.broadcast_to(average, (count, LANES))
        scale_inv = jnp.broadcast_to(scale_inv, (count, LANES))
        for t in range(tiles):
            columns = slice(t * LANES, (t + 1) * LANES)
            value = hidden[rows, columns].astype(jnp.float32)
            value = (value - average) * scale_inv
            value = value * (1.0 + modulation[1:2, columns]) + modulation[0:1, columns]
            normed[rows, columns] = value.astype(jnp.bfloat16)

    @pl.loop(0, tokens // block)
    def _(n):
        norm(pl.ds(pl.multiple_of(n * block, block), block))

    if tokens % block:
        norm(slice(tokens // block * block, tokens))
    conditional = lax.dot_general(
        normed[...],
        weight[...],
        (((1,), (1,)), ((), ())),
        preferred_element_type=jnp.float32,
    )
    conditional = (conditional + bias[...]).T

    current = jnp.full((1, 1), step_index[0], jnp.int32)
    counter = iota(skip_flags.shape, 1)
    computed = (skip_flags[...] == 0) & (counter <= current)
    last_full = jnp.max(jnp.where(computed, counter, -1), axis=1, keepdims=True)
    spacing = (current - last_full).astype(jnp.float32)
    gap_ratio = spacing / (spacing + 2.0)
    shape = (layout.rows, layout.channels)
    own = iota(shape, 0) // 4 == iota(shape, 1)
    w_low, w_high = (
        jnp.sum(jnp.where(own, band_gain[n : n + 1, :], 0.0), axis=1, keepdims=True) * factor
        for n, factor in enumerate((1.0 + gap_ratio, 1.0 - 0.5 * gap_ratio))
    )
    base[...] = conditional + GUIDE_EXTRA * w_high * residual[...]
    row_low[...] = jnp.broadcast_to(GUIDE_EXTRA * (w_low - w_high), row_low.shape)
    step[...] = jnp.broadcast_to(sigma_at(current + 1) - sigma_at(current), step.shape)


def finish_kernel(layout, *refs):
    near, channels, tokens = layout.near, layout.channels, layout.tokens
    parts = refs[:near]
    base, row_low, step, latent, velocity, latent_next, total = refs[near:]
    for g in range(total.shape[0]):
        last = min(tokens, (g + 1) * LANES)
        columns = slice(g * LANES, last)
        width = slice(0, last - g * LANES)
        low_band = parts[0][:, columns]
        for m in range(1, near):
            low_band += parts[m][:, columns]
        total[g, :, width] = low_band
        for c in range(channels):
            rows = slice(4 * c, 4 * c + 4)
            low_band = total[g, pl.ds(c, 4, stride=channels), :][:, width]
            value = base[rows, columns] + row_low[rows, width] * low_band
            velocity[rows, columns] = value
            latent_next[rows, columns] = latent[rows, columns] + step[:4, width] * value


VMEM = pl.BlockSpec(memory_space=pltpu.VMEM)
SMEM = pl.BlockSpec(memory_space=pltpu.SMEM)


def bands(layout, cut_rows, cut_cols):
    wide = layout.far * layout.lines * layout.channels
    tall = layout.near * layout.lines * layout.channels
    col = jax.ShapeDtypeStruct((2 * LANES, 2 * LANES), jnp.bfloat16)
    row = jax.ShapeDtypeStruct((tall, wide), jnp.bfloat16)
    return pl.pallas_call(
        functools.partial(bands_kernel, layout),
        out_shape=[col, col, row, row],
        in_specs=[SMEM, SMEM],
        out_specs=[VMEM] * 4,
        compiler_params=pltpu.CompilerParams(vmem_limit_bytes=8 * 2**20),
        cost_estimate=pl.CostEstimate(flops=10**8, bytes_accessed=10**6, transcendentals=0),
        name="bands",
    )(cut_rows, cut_cols)


def mix_scratch(layout, count):
    data = pltpu.VMEM((count * layout.lines * layout.channels, 2 * LANES), jnp.bfloat16)
    return [
        pltpu.VMEM((layout.rows, pl.cdiv(layout.tokens, LANES) * LANES), jnp.float32),
        pltpu.VMEM((layout.span, layout.rows, LANES), jnp.float32),
        data,
        data,
    ]


def early(layout, filters, slots, sources):
    tall = layout.near * layout.lines * layout.channels
    return pl.pallas_call(
        functools.partial(early_kernel, layout, slots),
        out_shape=jax.ShapeDtypeStruct((tall, 2 * LANES), jnp.float32),
        in_specs=[VMEM] * (4 + len(slots)),
        out_specs=VMEM,
        scratch_shapes=mix_scratch(layout, len(slots)),
        compiler_params=pltpu.CompilerParams(vmem_limit_bytes=8 * 2**20),
        cost_estimate=pl.CostEstimate(flops=10**9, bytes_accessed=10**6, transcendentals=0),
        name="early",
    )(*filters, *sources)


def mix(layout, filters, carry, slots, sources):
    shape = (layout.rows, layout.tokens)
    return pl.pallas_call(
        functools.partial(mix_kernel, layout, slots),
        out_shape=[jax.ShapeDtypeStruct(shape, jnp.float32)] * layout.near,
        in_specs=[VMEM] * (5 + len(slots)),
        out_specs=[VMEM] * layout.near,
        scratch_shapes=mix_scratch(layout, len(slots)),
        compiler_params=pltpu.CompilerParams(vmem_limit_bytes=8 * 2**20),
        cost_estimate=pl.CostEstimate(flops=10**9, bytes_accessed=10**6, transcendentals=0),
        name="mix",
    )(*filters, carry, *sources)


def head(layout, hidden, modulation, head_weight, head_bias, residual, gain, flags, step_index):
    return pl.pallas_call(
        functools.partial(head_kernel, layout),
        out_shape=[
            jax.ShapeDtypeStruct(residual.shape, jnp.float32),
            jax.ShapeDtypeStruct((layout.rows, LANES), jnp.float32),
            jax.ShapeDtypeStruct((8, LANES), jnp.float32),
        ],
        in_specs=[VMEM] * 7 + [SMEM],
        out_specs=[VMEM] * 3,
        scratch_shapes=[pltpu.VMEM(hidden.shape, jnp.bfloat16)],
        compiler_params=pltpu.CompilerParams(vmem_limit_bytes=16 * 2**20),
        cost_estimate=pl.CostEstimate(
            flops=2 * hidden.size * layout.rows, bytes_accessed=10**7, transcendentals=0
        ),
        name="head",
    )(
        hidden,
        modulation,
        head_weight.T,
        head_bias.reshape(1, -1),
        residual,
        gain,
        flags.reshape(1, -1),
        step_index,
    )


def head_in_parts(
    layout, hidden, modulation, head_weight, head_bias, residual, gain, flags, step_index
):
    values = hidden.astype(jnp.float32)
    moments = lax.psum((jnp.sum(values, axis=1), jnp.sum(values * values, axis=1)), "mp")
    average = moments[0] / D
    scale_inv = lax.rsqrt(moments[1] / D - average * average + EPSILON)
    normed = (
        (values - average[:, None]) * scale_inv[:, None] * (1.0 + modulation[1]) + modulation[0]
    ).astype(jnp.bfloat16)
    conditional = (
        lax.psum_scatter(
            lax.dot_general(
                head_weight, normed, (((0,), (1,)), ((), ())), preferred_element_type=jnp.float32
            ),
            "mp",
            scatter_dimension=0,
            tiled=True,
        )
        + head_bias[:, None]
    )
    w_low, w_high = band_weights(flags, step_index, gain)
    row_high = GUIDE_EXTRA * jnp.repeat(w_high, 4)[:, None]
    row_low = GUIDE_EXTRA * jnp.repeat(w_low - w_high, 4)[:, None]
    current = step_index[0]
    return (
        conditional + row_high * residual,
        jnp.broadcast_to(row_low, (layout.rows, LANES)),
        jnp.broadcast_to(sigma_at(current + 1) - sigma_at(current), (8, LANES)),
    )


def finish(layout, parts, base, row_low, step, latent):
    shape = jax.ShapeDtypeStruct((layout.rows, layout.tokens), jnp.float32)
    return pl.pallas_call(
        functools.partial(finish_kernel, layout),
        out_shape=[shape, shape],
        in_specs=[VMEM] * (layout.near + 4),
        out_specs=[VMEM, VMEM],
        scratch_shapes=[
            pltpu.VMEM((pl.cdiv(layout.tokens, LANES), layout.rows, LANES), jnp.float32)
        ],
        compiler_params=pltpu.CompilerParams(vmem_limit_bytes=8 * 2**20),
        name="finish",
    )(*parts, base, row_low, step, latent)


def body(
    hidden,
    modulation,
    head_weight,
    head_bias,
    residual,
    latent,
    band_gain,
    cut_rows,
    cut_cols,
    skip_flags,
    step_index,
):
    layout = Layout(*residual.shape)
    places = lax.axis_size("seq")

    def exchange(values, unit):
        swapped = [values[0]] * len(values)
        for n in layout.order(len(values))[1:]:
            pairs = [(s, s ^ (n * unit)) for s in range(places)]
            swapped[n] = lax.ppermute(values[n], "seq", pairs)
        return swapped

    sources = exchange([residual] * layout.far, layout.near)
    filters = bands(layout, cut_rows, cut_cols)
    run_head = head if lax.axis_size("mp") == 1 else head_in_parts
    base, row_low, step = run_head(
        layout,
        hidden,
        modulation,
        head_weight,
        head_bias,
        residual,
        band_gain,
        skip_flags,
        step_index,
    )
    sources = [sources[k] for k in layout.order(layout.far)]
    slots = list(range(layout.far))
    half = layout.far // 2
    carry = early(layout, filters, slots[:half], sources[:half])
    parts = exchange(mix(layout, filters, carry, slots[half:], sources[half:]), 1)
    return finish(layout, parts, base, row_low, step, latent)


def solution(mesh):
    in_specs = (
        P(("groups", "seq"), "mp"),
        P("groups", "mp"),
        P("mp", None),
        P("mp"),
        P("mp", ("groups", "seq")),
        P("mp", ("groups", "seq")),
        P(None, "mp"),
        P("groups"),
        P("groups"),
        P("groups"),
        P("groups"),
    )
    out_specs = (P("mp", ("groups", "seq")), P("mp", ("groups", "seq")))
    return jax.shard_map(body, mesh=mesh, in_specs=in_specs, out_specs=out_specs, check_vma=False)
```

```python
import functools
import math

import jax
import jax.numpy as jnp
from jax import lax
from jax.experimental import pallas as pl
from jax.experimental.pallas import tpu as pltpu
from jax.sharding import PartitionSpec as P


D = 5120
H = 90
W = 160
PH = 45
PW = 80
NSTEP = 50

EPSILON = 1e-06
GUIDE_EXTRA = 4.0
SHIFT_FACTOR = 5.0
LANES = 128


def sigma_at(step_number):
    remain = 1.0 - step_number.astype(jnp.float32) / NSTEP
    return SHIFT_FACTOR * remain / (1.0 + (SHIFT_FACTOR - 1.0) * remain)


def band_weights(skip_flags, step_index, band_gain):
    current = step_index[0]
    counter = jnp.arange(NSTEP, dtype=jnp.int32)
    computed = (skip_flags == 0) & (counter <= current)
    last_full = jnp.max(jnp.where(computed, counter, -1))
    spacing = (current - last_full).astype(jnp.float32)
    gap_ratio = spacing / (spacing + 2.0)
    return (band_gain[0] * (1.0 + gap_ratio), band_gain[1] * (1.0 - 0.5 * gap_ratio))


def split(value):
    high = value.astype(jnp.bfloat16)
    return high, (value - high.astype(jnp.float32)).astype(jnp.bfloat16)


def dot3(left, right, contract=((1,), (0,))):
    (lh, ll), (rh, rl) = left, right

    def dot(one, other):
        return lax.dot_general(
            one, other, (contract, ((), ())), preferred_element_type=jnp.float32
        )

    return dot(lh, rh) + (dot(ll, rh) + dot(lh, rl))


def iota(shape, axis):
    return lax.broadcasted_iota(jnp.int32, shape, axis)


class Layout:
    def __init__(self, local_rows, local_tokens):
        self.rows = local_rows
        self.tokens = local_tokens
        self.channels = local_rows // 4
        self.members = PH * PW // local_tokens
        bits = self.members.bit_length() - 1
        self.near = 1 << (bits // 2)
        self.far = self.members // self.near
        self.span = max(
            (p * local_tokens % PW + local_tokens + PW - 1) // PW
            for p in range(self.members)
        )
        self.lines = 2 * self.span
        self.groups = pl.cdiv(self.span * PW, LANES)

    def owners(self, position):
        givers = [position ^ (k * self.near) for k in self.order(self.far)]
        takers = [position ^ m for m in self.order(self.near)]
        return givers, takers

    def order(self, count):
        return [0, *range(2, count), 1][:count]

    def offset(self, owner):
        return lax.rem(owner * self.tokens, PW)

    def first_line(self, owner):
        return 2 * (owner * self.tokens // PW)


def waves(places, length):
    turns = lax.rem(places * iota(places.shape, 1), length).astype(jnp.float32)
    angles = turns * (2.0 * math.pi / length)
    return jnp.concatenate([jnp.cos(angles), jnp.sin(angles)], axis=1)


def kept_modes(shape, length, cutoff):
    modes = iota(shape, 1)
    weight = jnp.where((modes == 0) | (2 * modes == length), 1.0, 2.0) / length
    kept = jnp.where((modes <= cutoff) & (2 * modes <= length), weight, 0.0)
    return jnp.concatenate([kept, kept], axis=1)


def bands_kernel(
    layout,
    cut_rows,
    cut_cols,
    col_high,
    col_low,
    row_high,
    row_low,
):
    seq_index = lax.axis_index("seq")
    position = lax.rem(seq_index, layout.members)
    frame = seq_index // layout.members

    shape = (2 * LANES, LANES)
    line = iota(shape, 0)
    odd = line >= LANES
    column = jnp.where(odd, line - LANES, line)
    table = waves(2 * column + odd.astype(jnp.int32), W)
    table = jnp.where(jnp.concatenate([column, column], axis=1) < PW, table, 0.0)

    def tables(owners):
        line = iota((len(owners) * layout.lines, LANES), 0)
        places = line
        for n, owner in enumerate(owners):
            start = layout.first_line(owner) - n * layout.lines
            places = jnp.where(line >= n * layout.lines, line + start, places)
        return waves(places, H)

    givers, takers = layout.owners(position)
    given = tables(givers)
    taken = tables(takers)
    kept = kept_modes(shape, W, cut_cols[frame])
    high, low = split(dot3(split(table * kept), split(table), ((1,), (1,))))
    col_high[...] = high
    col_low[...] = low
    kept = kept_modes((given.shape[0], LANES), H, cut_rows[frame])
    small = dot3(split(taken), split(given * kept), ((1,), (1,)))
    wide = given.shape[0]
    size = wide * layout.channels
    spread = (iota((wide, size), 1) // layout.channels == iota((wide, size), 0)).astype(
        jnp.bfloat16
    )
    shape = (layout.channels, size)
    same = lax.rem(iota(shape, 1), layout.channels) == iota(shape, 0)
    for part, out in zip(split(small), (row_high, row_low)):
        repeated = jnp.dot(part, spread, preferred_element_type=jnp.float32)
        for n in range(taken.shape[0]):
            block = jnp.where(same, repeated[n : n + 1], 0.0)
            place = slice(n * layout.channels, (n + 1) * layout.channels)
            out[place, :] = block.astype(jnp.bfloat16)


def filtered(layout, slots, sources, filters, scratch):
    span, groups, channels, tokens = layout.span, layout.groups, layout.channels, layout.tokens
    col_high, col_low = filters[:2]
    window, lines, data_high, data_low = scratch
    givers, _ = layout.owners(lax.rem(lax.axis_index("seq"), layout.members))
    lane = iota((layout.rows, LANES), 1)
    chunks = window.shape[1] // LANES
    blank = jnp.zeros((layout.rows, LANES), jnp.float32)
    window[...] = jnp.zeros_like(window)
    for k, (slot, source) in enumerate(zip(slots, sources)):
        window[:, :tokens] = source[...]
        offset = layout.offset(givers[slot])
        turned = [
            pltpu.roll(window[:, g * LANES : (g + 1) * LANES], offset, 1) for g in range(chunks)
        ]
        turned = [blank] + turned + [blank] * (groups - chunks)
        placed = [jnp.where(lane >= offset, turned[g + 1], turned[g]) for g in range(groups)]
        for r in range(span):
            group, start = divmod(r * PW, LANES)
            if start == 0:
                line = placed[group]
            else:
                line = pltpu.roll(placed[group], LANES - start, 1)
                if start + PW > LANES:
                    rest = pltpu.roll(placed[group + 1], LANES - start, 1)
                    line = jnp.where(lane < LANES - start, line, rest)
            lines[r] = line
        for r in range(span):
            for dy in range(2):
                first = ((k * span + r) * 2 + dy) * channels
                for dx in range(2):
                    high, low = split(lines[r, pl.ds(2 * dy + dx, channels, stride=4), :])
                    place = (slice(first, first + channels), slice(dx * LANES, (dx + 1) * LANES))
                    data_high[place] = high
                    data_low[place] = low
    return dot3((data_high[...], data_low[...]), (col_high[...], col_low[...]))


def slots_columns(layout, slots):
    each = layout.lines * layout.channels
    return slice(slots[0] * each, (slots[-1] + 1) * each)


def early_kernel(layout, slots, *refs):
    sources = refs[4 : 4 + len(slots)]
    carry = refs[4 + len(slots)]
    data = filtered(layout, slots, sources, refs[:4], refs[5 + len(slots) :])
    columns = slots_columns(layout, slots)
    carry[...] = dot3([f[:, columns] for f in refs[2:4]], split(data))


def place_part(layout, mixed, taker, out):
    span, groups = layout.span, layout.groups
    channels, tokens = layout.channels, layout.tokens
    lane = iota((channels, LANES), 1)
    offset = layout.offset(taker)
    back = lax.rem(LANES - offset, LANES)
    for dy in range(2):
        for dx in range(2):
            placed = [None] * (groups + 1)

            def put(group, value):
                old = placed[group]
                placed[group] = value if old is None else old + value

            for r in range(span):
                first = (r * 2 + dy) * channels
                line = mixed[first : first + channels, dx * LANES : (dx + 1) * LANES]
                group, start = divmod(r * PW, LANES)
                if start:
                    line = pltpu.roll(line, start, 1)
                if start + PW <= LANES:
                    put(group, line)
                else:
                    put(group, jnp.where(lane >= start, line, 0.0))
                    put(group + 1, jnp.where(lane < start, line, 0.0))
            turned = [pltpu.roll(p, back, 1) for p in placed[:groups]]
            first = (dy * 2 + dx) * channels
            for g in range(pl.cdiv(tokens, LANES)):
                value = jnp.where(lane < LANES - offset, turned[g], turned[g + 1])
                last = min(tokens, (g + 1) * LANES)
                out[first : first + channels, g * LANES : last] = value[:, : last - g * LANES]


def first_kernel(layout, slots, m, *refs):
    filters, carry = refs[:4], refs[4]
    sources = refs[5 : 5 + len(slots)]
    out, data_high, data_low = refs[5 + len(slots) : 8 + len(slots)]
    high, low = split(filtered(layout, slots, sources, filters, refs[8 + len(slots) :]))
    data_high[...] = high
    data_low[...] = low
    each = layout.lines * layout.channels
    _, takers = layout.owners(lax.rem(lax.axis_index("seq"), layout.members))
    rows = slice(m * each, (m + 1) * each)
    columns = slots_columns(layout, slots)
    mixed = carry[rows, :] + dot3([f[rows, columns] for f in filters[2:]], (high, low))
    place_part(layout, mixed, takers[m], out)


def rest_kernel(layout, slots, others, *refs):
    row_high, row_low, carry, data_high, data_low = refs[:5]
    _, takers = layout.owners(lax.rem(lax.axis_index("seq"), layout.members))
    each = layout.lines * layout.channels
    columns = slots_columns(layout, slots)
    for m, out in zip(others, refs[5:]):
        rows = slice(m * each, (m + 1) * each)
        filters = [f[rows, columns] for f in (row_high, row_low)]
        mixed = carry[rows, :] + dot3(filters, (data_high[...], data_low[...]))
        place_part(layout, mixed, takers[m], out)


def norm_kernel(hidden, modulation, normed, scale):
    tokens, width = hidden.shape
    tiles = [slice(t, t + LANES) for t in range(0, width, LANES)]
    block, pair = 16, 2
    scale[...] = 1.0 + modulation[1:2, :]

    def moments(rows, count):
        sums = [jnp.zeros((count, LANES), jnp.float32) for _ in range(2)]
        squares = list(sums)
        for t, columns in enumerate(tiles):
            value = hidden[rows, columns].astype(jnp.float32)
            sums[t % 2] += value
            squares[t % 2] += value * value
        average = jnp.sum(sums[0] + sums[1], axis=1, keepdims=True) / D
        square = jnp.sum(squares[0] + squares[1], axis=1, keepdims=True) / D
        scale_inv = lax.rsqrt(square - average * average + EPSILON)
        return [jnp.broadcast_to(v, (count, LANES)) for v in (average, scale_inv)]

    def norm(rows, average, scale_inv):
        for columns in tiles:
            value = hidden[rows, columns].astype(jnp.float32)
            value = (value - average) * scale_inv
            value = value * scale[:, columns] + modulation[0:1, columns]
            normed[rows, columns] = value.astype(jnp.bfloat16)

    whole = tokens // (block * pair)

    @pl.loop(0, whole)
    def _(n):
        first = pl.multiple_of(n * (block * pair), block)
        rows = [pl.ds(first + p * block, block) for p in range(pair)]
        found = [moments(r, block) for r in rows]
        for r, f in zip(rows, found):
            norm(r, *f)

    for first in range(whole * block * pair, tokens, block):
        last = min(tokens, first + block)
        norm(slice(first, last), *moments(slice(first, last), last - first))


def project_kernel(
    layout,
    normed,
    weight,
    bias,
    residual,
    band_gain,
    skip_flags,
    step_index,
    base,
    row_low,
    step,
):
    conditional = lax.dot_general(
        normed[...],
        weight[...],
        (((1,), (1,)), ((), ())),
        preferred_element_type=jnp.float32,
    )
    conditional = (conditional + bias[...]).T

    current = jnp.full((1, 1), step_index[0], jnp.int32)
    counter = iota(skip_flags.shape, 1)
    computed = (skip_flags[...] == 0) & (counter <= current)
    last_full = jnp.max(jnp.where(computed, counter, -1), axis=1, keepdims=True)
    spacing = (current - last_full).astype(jnp.float32)
    gap_ratio = spacing / (spacing + 2.0)
    shape = (layout.rows, layout.channels)
    own = iota(shape, 0) // 4 == iota(shape, 1)
    w_low, w_high = (
        jnp.sum(jnp.where(own, band_gain[n : n + 1, :], 0.0), axis=1, keepdims=True) * factor
        for n, factor in enumerate((1.0 + gap_ratio, 1.0 - 0.5 * gap_ratio))
    )
    base[...] = conditional + GUIDE_EXTRA * w_high * residual[...]
    row_low[...] = jnp.broadcast_to(GUIDE_EXTRA * (w_low - w_high), row_low.shape)
    step[...] = jnp.broadcast_to(sigma_at(current + 1) - sigma_at(current), step.shape)


def finish_kernel(layout, *refs):
    near, channels, tokens = layout.near, layout.channels, layout.tokens
    parts = refs[:near]
    base, row_low, step, latent, velocity, latent_next, total = refs[near:]
    for g in range(total.shape[0]):
        last = min(tokens, (g + 1) * LANES)
        columns = slice(g * LANES, last)
        width = slice(0, last - g * LANES)
        low_band = parts[0][:, columns]
        for m in range(1, near):
            low_band += parts[m][:, columns]
        total[g, :, width] = low_band
        for c in range(channels):
            rows = slice(4 * c, 4 * c + 4)
            low_band = total[g, pl.ds(c, 4, stride=channels), :][:, width]
            value = base[rows, columns] + row_low[rows, width] * low_band
            velocity[rows, columns] = value
            latent_next[rows, columns] = latent[rows, columns] + step[:4, width] * value


VMEM = pl.BlockSpec(memory_space=pltpu.VMEM)
SMEM = pl.BlockSpec(memory_space=pltpu.SMEM)


def bands(layout, cut_rows, cut_cols):
    wide = layout.far * layout.lines * layout.channels
    tall = layout.near * layout.lines * layout.channels
    col = jax.ShapeDtypeStruct((2 * LANES, 2 * LANES), jnp.bfloat16)
    row = jax.ShapeDtypeStruct((tall, wide), jnp.bfloat16)
    return pl.pallas_call(
        functools.partial(bands_kernel, layout),
        out_shape=[col, col, row, row],
        in_specs=[SMEM, SMEM],
        out_specs=[VMEM] * 4,
        compiler_params=pltpu.CompilerParams(vmem_limit_bytes=8 * 2**20),
        cost_estimate=pl.CostEstimate(flops=10**9, bytes_accessed=2 * 10**7, transcendentals=0),
        name="bands",
    )(cut_rows, cut_cols)


def mix_scratch(layout, count):
    data = pltpu.VMEM((count * layout.lines * layout.channels, 2 * LANES), jnp.bfloat16)
    return [
        pltpu.VMEM((layout.rows, pl.cdiv(layout.tokens, LANES) * LANES), jnp.float32),
        pltpu.VMEM((layout.span, layout.rows, LANES), jnp.float32),
        data,
        data,
    ]


def early(layout, filters, slots, sources):
    tall = layout.near * layout.lines * layout.channels
    return pl.pallas_call(
        functools.partial(early_kernel, layout, slots),
        out_shape=jax.ShapeDtypeStruct((tall, 2 * LANES), jnp.float32),
        in_specs=[VMEM] * (4 + len(slots)),
        out_specs=VMEM,
        scratch_shapes=mix_scratch(layout, len(slots)),
        compiler_params=pltpu.CompilerParams(vmem_limit_bytes=8 * 2**20),
        cost_estimate=pl.CostEstimate(flops=10**9, bytes_accessed=10**6, transcendentals=0),
        name="early",
    )(*filters, *sources)


def mix_first(layout, filters, carry, slots, sources, m):
    wide = len(slots) * layout.lines * layout.channels
    data = jax.ShapeDtypeStruct((wide, 2 * LANES), jnp.bfloat16)
    return pl.pallas_call(
        functools.partial(first_kernel, layout, slots, m),
        out_shape=[jax.ShapeDtypeStruct((layout.rows, layout.tokens), jnp.float32), data, data],
        in_specs=[VMEM] * (5 + len(slots)),
        out_specs=[VMEM] * 3,
        scratch_shapes=mix_scratch(layout, len(slots)),
        compiler_params=pltpu.CompilerParams(vmem_limit_bytes=8 * 2**20),
        cost_estimate=pl.CostEstimate(flops=10**9, bytes_accessed=10**6, transcendentals=0),
        name="mix_first",
    )(*filters, carry, *sources)


def mix_rest(layout, filters, carry, slots, data, others):
    shape = jax.ShapeDtypeStruct((layout.rows, layout.tokens), jnp.float32)
    return pl.pallas_call(
        functools.partial(rest_kernel, layout, slots, others),
        out_shape=[shape] * len(others),
        in_specs=[VMEM] * 5,
        out_specs=[VMEM] * len(others),
        compiler_params=pltpu.CompilerParams(vmem_limit_bytes=8 * 2**20),
        cost_estimate=pl.CostEstimate(flops=10**9, bytes_accessed=10**6, transcendentals=0),
        name="mix_rest",
    )(*filters[2:], carry, *data)


def head(layout, hidden, modulation, head_weight, head_bias, residual, gain, flags, step_index):
    normed = pl.pallas_call(
        norm_kernel,
        out_shape=jax.ShapeDtypeStruct(hidden.shape, jnp.bfloat16),
        in_specs=[VMEM] * 2,
        out_specs=VMEM,
        scratch_shapes=[pltpu.VMEM((1, hidden.shape[1]), jnp.float32)],
        compiler_params=pltpu.CompilerParams(vmem_limit_bytes=8 * 2**20),
        cost_estimate=pl.CostEstimate(
            flops=10 * hidden.size, bytes_accessed=10**7, transcendentals=0
        ),
        name="norm",
    )(hidden, modulation)
    return pl.pallas_call(
        functools.partial(project_kernel, layout),
        out_shape=[
            jax.ShapeDtypeStruct(residual.shape, jnp.float32),
            jax.ShapeDtypeStruct((layout.rows, LANES), jnp.float32),
            jax.ShapeDtypeStruct((8, LANES), jnp.float32),
        ],
        in_specs=[VMEM] * 6 + [SMEM],
        out_specs=[VMEM] * 3,
        compiler_params=pltpu.CompilerParams(vmem_limit_bytes=8 * 2**20),
        cost_estimate=pl.CostEstimate(
            flops=2 * hidden.size * layout.rows, bytes_accessed=3 * 10**6, transcendentals=0
        ),
        name="project",
    )(
        normed,
        head_weight.T,
        head_bias.reshape(1, -1),
        residual,
        gain,
        flags.reshape(1, -1),
        step_index,
    )


def head_in_parts(
    layout, hidden, modulation, head_weight, head_bias, residual, gain, flags, step_index
):
    values = hidden.astype(jnp.float32)
    moments = lax.psum((jnp.sum(values, axis=1), jnp.sum(values * values, axis=1)), "mp")
    average = moments[0] / D
    scale_inv = lax.rsqrt(moments[1] / D - average * average + EPSILON)
    normed = (
        (values - average[:, None]) * scale_inv[:, None] * (1.0 + modulation[1]) + modulation[0]
    ).astype(jnp.bfloat16)
    conditional = (
        lax.psum_scatter(
            lax.dot_general(
                head_weight, normed, (((0,), (1,)), ((), ())), preferred_element_type=jnp.float32
            ),
            "mp",
            scatter_dimension=0,
            tiled=True,
        )
        + head_bias[:, None]
    )
    w_low, w_high = band_weights(flags, step_index, gain)
    row_high = GUIDE_EXTRA * jnp.repeat(w_high, 4)[:, None]
    row_low = GUIDE_EXTRA * jnp.repeat(w_low - w_high, 4)[:, None]
    current = step_index[0]
    return (
        conditional + row_high * residual,
        jnp.broadcast_to(row_low, (layout.rows, LANES)),
        jnp.broadcast_to(sigma_at(current + 1) - sigma_at(current), (8, LANES)),
    )


def finish(layout, parts, base, row_low, step, latent):
    shape = jax.ShapeDtypeStruct((layout.rows, layout.tokens), jnp.float32)
    return pl.pallas_call(
        functools.partial(finish_kernel, layout),
        out_shape=[shape, shape],
        in_specs=[VMEM] * (layout.near + 4),
        out_specs=[VMEM, VMEM],
        scratch_shapes=[
            pltpu.VMEM((pl.cdiv(layout.tokens, LANES), layout.rows, LANES), jnp.float32)
        ],
        compiler_params=pltpu.CompilerParams(vmem_limit_bytes=8 * 2**20),
        name="finish",
    )(*parts, base, row_low, step, latent)


def body(
    hidden,
    modulation,
    head_weight,
    head_bias,
    residual,
    latent,
    band_gain,
    cut_rows,
    cut_cols,
    skip_flags,
    step_index,
):
    layout = Layout(*residual.shape)
    places = lax.axis_size("seq")

    def exchange(values, unit):
        swapped = [values[0]]
        for turn, n in enumerate(layout.order(len(values))[1:]):
            pairs = [(s, s ^ (n * unit)) for s in range(places)]
            swapped.append(lax.ppermute(values[turn + 1], "seq", pairs))
        return swapped

    sources = exchange([residual] * layout.far, layout.near)
    filters = bands(layout, cut_rows, cut_cols)
    run_head = head if lax.axis_size("mp") == 1 else head_in_parts
    base, row_low, step = run_head(
        layout,
        hidden,
        modulation,
        head_weight,
        head_bias,
        residual,
        band_gain,
        skip_flags,
        step_index,
    )
    slots = list(range(layout.far))
    half = layout.far // 2
    carry = early(layout, filters, slots[:half], sources[:half])
    late, others = slots[half:], [0, *range(2, layout.near)]
    part, *data = mix_first(layout, filters, carry, late, sources[half:], 1)
    own, *rest = mix_rest(layout, filters, carry, late, data, others)
    parts = exchange([own, part, *rest], 1)
    return finish(layout, parts, base, row_low, step, latent)


def solution(mesh):
    in_specs = (
        P(("groups", "seq"), "mp"),
        P("groups", "mp"),
        P("mp", None),
        P("mp"),
        P("mp", ("groups", "seq")),
        P("mp", ("groups", "seq")),
        P(None, "mp"),
        P("groups"),
        P("groups"),
        P("groups"),
        P("groups"),
    )
    out_specs = (P("mp", ("groups", "seq")), P("mp", ("groups", "seq")))
    return jax.shard_map(body, mesh=mesh, in_specs=in_specs, out_specs=out_specs, check_vma=False)
```

```python
import functools
import math

import jax
import jax.numpy as jnp
from jax import lax
from jax.experimental import pallas as pl
from jax.experimental.pallas import tpu as pltpu
from jax.sharding import PartitionSpec as P


D = 5120
H = 90
W = 160
PH = 45
PW = 80
NSTEP = 50

EPSILON = 1e-06
GUIDE_EXTRA = 4.0
SHIFT_FACTOR = 5.0
LANES = 128


def sigma_at(step_number):
    remain = 1.0 - step_number.astype(jnp.float32) / NSTEP
    return SHIFT_FACTOR * remain / (1.0 + (SHIFT_FACTOR - 1.0) * remain)


def band_weights(skip_flags, step_index, band_gain):
    current = step_index[0]
    counter = jnp.arange(NSTEP, dtype=jnp.int32)
    computed = (skip_flags == 0) & (counter <= current)
    last_full = jnp.max(jnp.where(computed, counter, -1))
    spacing = (current - last_full).astype(jnp.float32)
    gap_ratio = spacing / (spacing + 2.0)
    return (band_gain[0] * (1.0 + gap_ratio), band_gain[1] * (1.0 - 0.5 * gap_ratio))


def split(value):
    high = value.astype(jnp.bfloat16)
    return high, (value - high.astype(jnp.float32)).astype(jnp.bfloat16)


def dot3(left, right, contract=((1,), (0,))):
    (lh, ll), (rh, rl) = left, right

    def dot(one, other):
        return lax.dot_general(
            one, other, (contract, ((), ())), preferred_element_type=jnp.float32
        )

    return dot(lh, rh) + (dot(ll, rh) + dot(lh, rl))


def iota(shape, axis):
    return lax.broadcasted_iota(jnp.int32, shape, axis)


class Layout:
    def __init__(self, local_rows, local_tokens):
        self.rows = local_rows
        self.tokens = local_tokens
        self.channels = local_rows // 4
        self.members = PH * PW // local_tokens
        bits = self.members.bit_length() - 1
        self.near = 1 << (bits // 2)
        self.far = self.members // self.near
        self.span = max(
            (p * local_tokens % PW + local_tokens + PW - 1) // PW
            for p in range(self.members)
        )
        self.lines = 2 * self.span
        self.groups = pl.cdiv(self.span * PW, LANES)

    def owners(self, position):
        givers = [position ^ (k * self.near) for k in self.order(self.far)]
        takers = [position ^ m for m in self.order(self.near)]
        return givers, takers

    def order(self, count):
        return [0, *range(2, count), 1][:count]

    def offset(self, owner):
        return lax.rem(owner * self.tokens, PW)

    def first_line(self, owner):
        return 2 * (owner * self.tokens // PW)


def cosine_of_turns(turns):
    angle = 2.0 * math.pi * (0.25 - jnp.abs(turns - 0.5))
    square = angle * angle
    series = jnp.full_like(square, -1.0 / math.factorial(11))
    for power in (9, 7, 5, 3, 1):
        series = series * square + (-1.0) ** (power // 2) / math.factorial(power)
    return -angle * series


def waves(places, length):
    phase = (places * iota(places.shape, 1)).astype(jnp.float32)
    phase = phase - length * jnp.floor((phase + 0.5) * (1.0 / length))
    turns = phase * (1.0 / length)
    later = jnp.where(turns < 0.25, turns + 0.75, turns - 0.25)
    return jnp.concatenate([cosine_of_turns(turns), cosine_of_turns(later)], axis=1)


def kept_modes(shape, length, cutoff):
    modes = iota(shape, 1)
    weight = jnp.where((modes == 0) | (2 * modes == length), 1.0, 2.0) / length
    kept = jnp.where((modes <= cutoff) & (2 * modes <= length), weight, 0.0)
    return jnp.concatenate([kept, kept], axis=1)


def bands_kernel(layout, cut_rows, cut_cols, col_filter, *row_filters):
    seq_index = lax.axis_index("seq")
    position = lax.rem(seq_index, layout.members)
    frame = seq_index // layout.members

    column = iota((PW, LANES), 0)
    gap = jnp.zeros((LANES - PW, 2 * LANES), jnp.float32)
    table = jnp.concatenate([waves(2 * column, W), gap, waves(2 * column + 1, W), gap], axis=0)

    def tables(owners):
        line = iota((len(owners) * layout.lines, LANES), 0)
        places = line
        for n, owner in enumerate(owners):
            start = layout.first_line(owner) - n * layout.lines
            places = jnp.where(line >= n * layout.lines, line + start, places)
        return waves(places, H)

    givers, takers = layout.owners(position)
    given = tables(givers)
    taken = tables(takers)
    kept = kept_modes((2 * LANES, LANES), W, cut_cols[frame])
    high, low = split(dot3(split(table * kept), split(table), ((1,), (1,))))
    for n, part in enumerate((high, high, low)):
        col_filter[n * 2 * LANES : (n + 1) * 2 * LANES, :] = part
    kept = kept_modes((given.shape[0], LANES), H, cut_rows[frame])
    small = dot3(split(taken), split(given * kept), ((1,), (1,)))
    wide = given.shape[0]
    size = wide * layout.channels
    spread = (iota((wide, size), 1) // layout.channels == iota((wide, size), 0)).astype(
        jnp.bfloat16
    )
    shape = (layout.channels, size)
    same = lax.rem(iota(shape, 1), layout.channels) == iota(shape, 0)
    each = size // len(row_filters)
    for part, spots in zip(split(small), ((0, 2), (1,))):
        repeated = jnp.dot(part, spread, preferred_element_type=jnp.float32)
        for n in range(taken.shape[0]):
            block = jnp.where(same, repeated[n : n + 1], 0.0).astype(jnp.bfloat16)
            place = slice(n * layout.channels, (n + 1) * layout.channels)
            for half, out in enumerate(row_filters):
                for spot in spots:
                    out[place, spot * each : (spot + 1) * each] = block[
                        :, half * each : (half + 1) * each
                    ]


def product(left, right):
    return jnp.dot(left, right, preferred_element_type=jnp.float32)


def filtered(layout, slots, sources, col_filter, scratch):
    span, groups, channels, tokens = layout.span, layout.groups, layout.channels, layout.tokens
    window, lines, data = scratch
    givers, _ = layout.owners(lax.rem(lax.axis_index("seq"), layout.members))
    lane = iota((layout.rows, LANES), 1)
    chunks = window.shape[1] // LANES
    blank = jnp.zeros((layout.rows, LANES), jnp.float32)
    window[...] = jnp.zeros_like(window)
    for k, (slot, source) in enumerate(zip(slots, sources)):
        window[:, :tokens] = source[...]
        offset = layout.offset(givers[slot])
        turned = [
            pltpu.roll(window[:, g * LANES : (g + 1) * LANES], offset, 1) for g in range(chunks)
        ]
        turned = [blank] + turned + [blank] * (groups - chunks)
        placed = [jnp.where(lane >= offset, turned[g + 1], turned[g]) for g in range(groups)]
        for r in range(span):
            group, start = divmod(r * PW, LANES)
            if start == 0:
                line = placed[group]
            else:
                line = pltpu.roll(placed[group], LANES - start, 1)
                if start + PW > LANES:
                    rest = pltpu.roll(placed[group + 1], LANES - start, 1)
                    line = jnp.where(lane < LANES - start, line, rest)
            lines[r] = line
        for r in range(span):
            for dy in range(2):
                first = ((k * span + r) * 2 + dy) * channels
                for dx in range(2):
                    high, low = split(lines[r, pl.ds(2 * dy + dx, channels, stride=4), :])
                    for n, part in enumerate((high, low, high)):
                        left = (2 * n + dx) * LANES
                        data[first : first + channels, left : left + LANES] = part
    high, low = split(product(data[...], col_filter[...]))
    return jnp.concatenate([high, high, low], axis=0)


def early_kernel(layout, slots, col_filter, row_filter, *refs):
    sources, carry = refs[: len(slots)], refs[len(slots)]
    data = filtered(layout, slots, sources, col_filter, refs[len(slots) + 1 :])
    carry[...] = product(row_filter[...], data)


def place_part(layout, mixed, taker, out):
    span, groups = layout.span, layout.groups
    channels, tokens = layout.channels, layout.tokens
    lane = iota((channels, LANES), 1)
    offset = layout.offset(taker)
    back = lax.rem(LANES - offset, LANES)
    for dy in range(2):
        for dx in range(2):
            placed = [None] * (groups + 1)

            def put(group, value):
                old = placed[group]
                placed[group] = value if old is None else old + value

            for r in range(span):
                first = (r * 2 + dy) * channels
                line = mixed[first : first + channels, dx * LANES : (dx + 1) * LANES]
                group, start = divmod(r * PW, LANES)
                if start:
                    line = pltpu.roll(line, start, 1)
                if start + PW <= LANES:
                    put(group, line)
                else:
                    put(group, jnp.where(lane >= start, line, 0.0))
                    put(group + 1, jnp.where(lane < start, line, 0.0))
            turned = [pltpu.roll(p, back, 1) for p in placed[:groups]]
            first = (dy * 2 + dx) * channels
            for g in range(pl.cdiv(tokens, LANES)):
                value = jnp.where(lane < LANES - offset, turned[g], turned[g + 1])
                last = min(tokens, (g + 1) * LANES)
                out[first : first + channels, g * LANES : last] = value[:, : last - g * LANES]


def first_kernel(layout, slots, m, col_filter, row_filter, carry, *refs):
    sources = refs[: len(slots)]
    out, data = refs[len(slots) : len(slots) + 2]
    found = filtered(layout, slots, sources, col_filter, refs[len(slots) + 2 :])
    data[...] = found
    each = layout.lines * layout.channels
    _, takers = layout.owners(lax.rem(lax.axis_index("seq"), layout.members))
    rows = slice(m * each, (m + 1) * each)
    place_part(layout, carry[rows, :] + product(row_filter[rows, :], found), takers[m], out)


def rest_kernel(layout, others, row_filter, carry, data, *outs):
    _, takers = layout.owners(lax.rem(lax.axis_index("seq"), layout.members))
    each = layout.lines * layout.channels
    for m, out in zip(others, outs):
        rows = slice(m * each, (m + 1) * each)
        mixed = carry[rows, :] + product(row_filter[rows, :], data[...])
        place_part(layout, mixed, takers[m], out)


def norm_rows(hidden, modulation, scale, normed, start, stop):
    tiles = [slice(t, t + LANES) for t in range(0, hidden.shape[1], LANES)]
    block, pair = 16, 2
    scale[...] = 1.0 + modulation[1:2, :]

    def moments(rows, count):
        sums = [jnp.zeros((count, LANES), jnp.float32) for _ in range(2)]
        squares = list(sums)
        for t, columns in enumerate(tiles):
            value = hidden[rows, columns].astype(jnp.float32)
            sums[t % 2] += value
            squares[t % 2] += value * value
        average = jnp.sum(sums[0] + sums[1], axis=1, keepdims=True) / D
        square = jnp.sum(squares[0] + squares[1], axis=1, keepdims=True) / D
        scale_inv = lax.rsqrt(square - average * average + EPSILON)
        return [jnp.broadcast_to(v, (count, LANES)) for v in (average, scale_inv)]

    def norm(rows, place, average, scale_inv):
        for columns in tiles:
            value = hidden[rows, columns].astype(jnp.float32)
            value = (value - average) * scale_inv
            value = value * scale[:, columns] + modulation[0:1, columns]
            normed[place, columns] = value.astype(jnp.bfloat16)

    whole = (stop - start) // (block * pair)

    @pl.loop(0, whole)
    def _(n):
        first = pl.multiple_of(n * (block * pair), block)
        rows = [pl.ds(start + first + p * block, block) for p in range(pair)]
        found = [moments(r, block) for r in rows]
        for p in range(pair):
            norm(rows[p], pl.ds(first + p * block, block), *found[p])

    for first in range(start + whole * block * pair, stop, block):
        rows = slice(first, min(stop, first + block))
        found = moments(rows, rows.stop - first)
        norm(rows, slice(first - start, rows.stop - start), *found)


def norm_kernel(hidden, modulation, normed, scale):
    norm_rows(hidden, modulation, scale, normed, 0, normed.shape[0])


def project_kernel(
    layout,
    early_normed,
    hidden,
    modulation,
    weight,
    bias,
    residual,
    band_gain,
    skip_flags,
    step_index,
    base,
    row_low,
    step,
    normed,
    scale,
):
    tokens, first = hidden.shape[0], early_normed.shape[0]
    current = jnp.full((1, 1), step_index[0], jnp.int32)
    counter = iota(skip_flags.shape, 1)
    computed = (skip_flags[...] == 0) & (counter <= current)
    last_full = jnp.max(jnp.where(computed, counter, -1), axis=1, keepdims=True)
    spacing = (current - last_full).astype(jnp.float32)
    gap_ratio = spacing / (spacing + 2.0)
    shape = (layout.rows, layout.channels)
    own = iota(shape, 0) // 4 == iota(shape, 1)
    w_low, w_high = (
        jnp.sum(jnp.where(own, band_gain[n : n + 1, :], 0.0), axis=1, keepdims=True) * factor
        for n, factor in enumerate((1.0 + gap_ratio, 1.0 - 0.5 * gap_ratio))
    )

    def project(rows, columns):
        conditional = lax.dot_general(
            rows[...], weight[...], (((1,), (1,)), ((), ())), preferred_element_type=jnp.float32
        )
        conditional = (conditional + bias[...]).T
        base[:, columns] = conditional + GUIDE_EXTRA * w_high * residual[:, columns]

    if first:
        project(early_normed, slice(0, first))
    norm_rows(hidden, modulation, scale, normed, first, tokens)
    project(normed, slice(first, tokens))
    row_low[...] = jnp.broadcast_to(GUIDE_EXTRA * (w_low - w_high), row_low.shape)
    step[...] = jnp.broadcast_to(sigma_at(current + 1) - sigma_at(current), step.shape)


def finish_kernel(layout, *refs):
    near, channels, tokens = layout.near, layout.channels, layout.tokens
    parts = refs[:near]
    base, row_low, step, latent, velocity, latent_next, total = refs[near:]
    for g in range(total.shape[0]):
        last = min(tokens, (g + 1) * LANES)
        columns = slice(g * LANES, last)
        width = slice(0, last - g * LANES)
        low_band = parts[0][:, columns]
        for m in range(1, near):
            low_band += parts[m][:, columns]
        total[g, :, width] = low_band
        for c in range(channels):
            rows = slice(4 * c, 4 * c + 4)
            low_band = total[g, pl.ds(c, 4, stride=channels), :][:, width]
            value = base[rows, columns] + row_low[rows, width] * low_band
            velocity[rows, columns] = value
            latent_next[rows, columns] = latent[rows, columns] + step[:4, width] * value


VMEM = pl.BlockSpec(memory_space=pltpu.VMEM)
SMEM = pl.BlockSpec(memory_space=pltpu.SMEM)


def bands(layout, cut_rows, cut_cols):
    wide = layout.far * layout.lines * layout.channels
    tall = layout.near * layout.lines * layout.channels
    col = jax.ShapeDtypeStruct((6 * LANES, 2 * LANES), jnp.bfloat16)
    row = jax.ShapeDtypeStruct((tall, 3 * wide // 2), jnp.bfloat16)
    return pl.pallas_call(
        functools.partial(bands_kernel, layout),
        out_shape=[col, row, row],
        in_specs=[SMEM, SMEM],
        out_specs=[VMEM] * 3,
        compiler_params=pltpu.CompilerParams(vmem_limit_bytes=8 * 2**20),
        cost_estimate=pl.CostEstimate(flops=10**9, bytes_accessed=2 * 10**7, transcendentals=0),
        name="bands",
    )(cut_rows, cut_cols)


def mix_scratch(layout, count):
    return [
        pltpu.VMEM((layout.rows, pl.cdiv(layout.tokens, LANES) * LANES), jnp.float32),
        pltpu.VMEM((layout.span, layout.rows, LANES), jnp.float32),
        pltpu.VMEM((count * layout.lines * layout.channels, 6 * LANES), jnp.bfloat16),
    ]


def early(layout, filters, slots, sources):
    tall = layout.near * layout.lines * layout.channels
    return pl.pallas_call(
        functools.partial(early_kernel, layout, slots),
        out_shape=jax.ShapeDtypeStruct((tall, 2 * LANES), jnp.float32),
        in_specs=[VMEM] * (2 + len(slots)),
        out_specs=VMEM,
        scratch_shapes=mix_scratch(layout, len(slots)),
        compiler_params=pltpu.CompilerParams(vmem_limit_bytes=8 * 2**20),
        cost_estimate=pl.CostEstimate(flops=10**9, bytes_accessed=10**6, transcendentals=0),
        name="early",
    )(*filters, *sources)


def mix_first(layout, filters, carry, slots, sources, m):
    wide = len(slots) * layout.lines * layout.channels
    return pl.pallas_call(
        functools.partial(first_kernel, layout, slots, m),
        out_shape=[
            jax.ShapeDtypeStruct((layout.rows, layout.tokens), jnp.float32),
            jax.ShapeDtypeStruct((3 * wide, 2 * LANES), jnp.bfloat16),
        ],
        in_specs=[VMEM] * (3 + len(slots)),
        out_specs=[VMEM] * 2,
        scratch_shapes=mix_scratch(layout, len(slots)),
        compiler_params=pltpu.CompilerParams(vmem_limit_bytes=8 * 2**20),
        cost_estimate=pl.CostEstimate(flops=10**9, bytes_accessed=10**6, transcendentals=0),
        name="mix_first",
    )(*filters, carry, *sources)


def mix_rest(layout, row_filter, carry, data, others):
    shape = jax.ShapeDtypeStruct((layout.rows, layout.tokens), jnp.float32)
    return pl.pallas_call(
        functools.partial(rest_kernel, layout, others),
        out_shape=[shape] * len(others),
        in_specs=[VMEM] * 3,
        out_specs=[VMEM] * len(others),
        compiler_params=pltpu.CompilerParams(vmem_limit_bytes=8 * 2**20),
        cost_estimate=pl.CostEstimate(flops=10**9, bytes_accessed=10**6, transcendentals=0),
        name="mix_rest",
    )(row_filter, carry, data)


def head(layout, hidden, modulation, head_weight, head_bias, residual, gain, flags, step_index):
    first = hidden.shape[0] // LANES * LANES
    scale = pltpu.VMEM((1, hidden.shape[1]), jnp.float32)
    normed = pl.pallas_call(
        norm_kernel,
        out_shape=jax.ShapeDtypeStruct((first, hidden.shape[1]), jnp.bfloat16),
        in_specs=[VMEM] * 2,
        out_specs=VMEM,
        scratch_shapes=[scale],
        compiler_params=pltpu.CompilerParams(vmem_limit_bytes=8 * 2**20),
        cost_estimate=pl.CostEstimate(
            flops=10 * hidden.size, bytes_accessed=10**7, transcendentals=0
        ),
        name="norm",
    )(hidden, modulation)
    return pl.pallas_call(
        functools.partial(project_kernel, layout),
        out_shape=[
            jax.ShapeDtypeStruct(residual.shape, jnp.float32),
            jax.ShapeDtypeStruct((layout.rows, LANES), jnp.float32),
            jax.ShapeDtypeStruct((8, LANES), jnp.float32),
        ],
        in_specs=[VMEM] * 8 + [SMEM],
        out_specs=[VMEM] * 3,
        scratch_shapes=[
            pltpu.VMEM((hidden.shape[0] - first, hidden.shape[1]), jnp.bfloat16),
            scale,
        ],
        compiler_params=pltpu.CompilerParams(vmem_limit_bytes=8 * 2**20),
        cost_estimate=pl.CostEstimate(
            flops=2 * hidden.size * layout.rows, bytes_accessed=3 * 10**6, transcendentals=0
        ),
        name="project",
    )(
        normed,
        hidden,
        modulation,
        head_weight.T,
        head_bias.reshape(1, -1),
        residual,
        gain,
        flags.reshape(1, -1),
        step_index,
    )


def head_in_parts(
    layout, hidden, modulation, head_weight, head_bias, residual, gain, flags, step_index
):
    values = hidden.astype(jnp.float32)
    moments = lax.psum((jnp.sum(values, axis=1), jnp.sum(values * values, axis=1)), "mp")
    average = moments[0] / D
    scale_inv = lax.rsqrt(moments[1] / D - average * average + EPSILON)
    normed = (
        (values - average[:, None]) * scale_inv[:, None] * (1.0 + modulation[1]) + modulation[0]
    ).astype(jnp.bfloat16)
    conditional = (
        lax.psum_scatter(
            lax.dot_general(
                head_weight, normed, (((0,), (1,)), ((), ())), preferred_element_type=jnp.float32
            ),
            "mp",
            scatter_dimension=0,
            tiled=True,
        )
        + head_bias[:, None]
    )
    w_low, w_high = band_weights(flags, step_index, gain)
    row_high = GUIDE_EXTRA * jnp.repeat(w_high, 4)[:, None]
    row_low = GUIDE_EXTRA * jnp.repeat(w_low - w_high, 4)[:, None]
    current = step_index[0]
    return (
        conditional + row_high * residual,
        jnp.broadcast_to(row_low, (layout.rows, LANES)),
        jnp.broadcast_to(sigma_at(current + 1) - sigma_at(current), (8, LANES)),
    )


def finish(layout, parts, base, row_low, step, latent):
    shape = jax.ShapeDtypeStruct((layout.rows, layout.tokens), jnp.float32)
    return pl.pallas_call(
        functools.partial(finish_kernel, layout),
        out_shape=[shape, shape],
        in_specs=[VMEM] * (layout.near + 4),
        out_specs=[VMEM, VMEM],
        scratch_shapes=[
            pltpu.VMEM((pl.cdiv(layout.tokens, LANES), layout.rows, LANES), jnp.float32)
        ],
        compiler_params=pltpu.CompilerParams(vmem_limit_bytes=8 * 2**20),
        name="finish",
    )(*parts, base, row_low, step, latent)


def body(
    hidden,
    modulation,
    head_weight,
    head_bias,
    residual,
    latent,
    band_gain,
    cut_rows,
    cut_cols,
    skip_flags,
    step_index,
):
    layout = Layout(*residual.shape)
    places = lax.axis_size("seq")

    def exchange(values, unit):
        swapped = [values[0]]
        for turn, n in enumerate(layout.order(len(values))[1:]):
            pairs = [(s, s ^ (n * unit)) for s in range(places)]
            swapped.append(lax.ppermute(values[turn + 1], "seq", pairs))
        return swapped

    sources = exchange([residual] * layout.far, layout.near)
    col_filter, row_early, row_late = bands(layout, cut_rows, cut_cols)
    run_head = head if lax.axis_size("mp") == 1 else head_in_parts
    base, row_low, step = run_head(
        layout,
        hidden,
        modulation,
        head_weight,
        head_bias,
        residual,
        band_gain,
        skip_flags,
        step_index,
    )
    slots = list(range(layout.far))
    half = layout.far // 2
    carry = early(layout, (col_filter, row_early), slots[:half], sources[:half])
    filters = (col_filter, row_late)
    part, data = mix_first(layout, filters, carry, slots[half:], sources[half:], 1)
    own, *rest = mix_rest(layout, row_late, carry, data, [0, *range(2, layout.near)])
    parts = exchange([own, part, *rest], 1)
    return finish(layout, parts, base, row_low, step, latent)


def solution(mesh):
    in_specs = (
        P(("groups", "seq"), "mp"),
        P("groups", "mp"),
        P("mp", None),
        P("mp"),
        P("mp", ("groups", "seq")),
        P("mp", ("groups", "seq")),
        P(None, "mp"),
        P("groups"),
        P("groups"),
        P("groups"),
        P("groups"),
    )
    out_specs = (P("mp", ("groups", "seq")), P("mp", ("groups", "seq")))
    return jax.shard_map(body, mesh=mesh, in_specs=in_specs, out_specs=out_specs, check_vma=False)
```

```python
import functools
import math

import jax
import jax.numpy as jnp
from jax import lax
from jax.experimental import pallas as pl
from jax.experimental.pallas import tpu as pltpu
from jax.sharding import PartitionSpec as P


D = 5120
H = 90
W = 160
PH = 45
PW = 80
NSTEP = 50

EPSILON = 1e-06
GUIDE_EXTRA = 4.0
SHIFT_FACTOR = 5.0
LANES = 128


def sigma_at(step_number):
    remain = 1.0 - step_number.astype(jnp.float32) / NSTEP
    return SHIFT_FACTOR * remain / (1.0 + (SHIFT_FACTOR - 1.0) * remain)


def band_weights(skip_flags, step_index, band_gain):
    current = step_index[0]
    counter = jnp.arange(NSTEP, dtype=jnp.int32)
    computed = (skip_flags == 0) & (counter <= current)
    last_full = jnp.max(jnp.where(computed, counter, -1))
    spacing = (current - last_full).astype(jnp.float32)
    gap_ratio = spacing / (spacing + 2.0)
    return (band_gain[0] * (1.0 + gap_ratio), band_gain[1] * (1.0 - 0.5 * gap_ratio))


def split(value):
    high = value.astype(jnp.bfloat16)
    return high, (value - high.astype(jnp.float32)).astype(jnp.bfloat16)


def dot3(left, right, contract=((1,), (0,))):
    (lh, ll), (rh, rl) = left, right

    def dot(one, other):
        return lax.dot_general(
            one, other, (contract, ((), ())), preferred_element_type=jnp.float32
        )

    return dot(lh, rh) + (dot(ll, rh) + dot(lh, rl))


def iota(shape, axis):
    return lax.broadcasted_iota(jnp.int32, shape, axis)


class Layout:
    def __init__(self, local_rows, local_tokens):
        self.rows = local_rows
        self.tokens = local_tokens
        self.channels = local_rows // 4
        self.members = PH * PW // local_tokens
        bits = self.members.bit_length() - 1
        self.near = 1 << (bits // 2)
        self.far = self.members // self.near
        self.span = max(
            (p * local_tokens % PW + local_tokens + PW - 1) // PW
            for p in range(self.members)
        )
        self.lines = 2 * self.span
        self.groups = pl.cdiv(self.span * PW, LANES)

    def owners(self, position):
        givers = [position ^ (k * self.near) for k in self.far_order()]
        takers = [position ^ m for m in self.near_order()]
        return givers, takers

    def far_order(self):
        return [0, *range(2, self.far), 1][: self.far]

    def near_order(self):
        return [0, *range(self.near - 1, 0, -1)]

    def offset(self, owner):
        return lax.rem(owner * self.tokens, PW)

    def first_line(self, owner):
        return 2 * (owner * self.tokens // PW)


def cosine_of_turns(turns):
    angle = 2.0 * math.pi * (0.25 - jnp.abs(turns - 0.5))
    square = angle * angle
    series = jnp.full_like(square, -1.0 / math.factorial(11))
    for power in (9, 7, 5, 3, 1):
        series = series * square + (-1.0) ** (power // 2) / math.factorial(power)
    return -angle * series


def waves(places, length):
    phase = (places * iota(places.shape, 1)).astype(jnp.float32)
    phase = phase - length * jnp.floor((phase + 0.5) * (1.0 / length))
    turns = phase * (1.0 / length)
    later = jnp.where(turns < 0.25, turns + 0.75, turns - 0.25)
    return jnp.concatenate([cosine_of_turns(turns), cosine_of_turns(later)], axis=1)


def kept_modes(shape, length, cutoff):
    modes = iota(shape, 1)
    weight = jnp.where((modes == 0) | (2 * modes == length), 1.0, 2.0) / length
    kept = jnp.where((modes <= cutoff) & (2 * modes <= length), weight, 0.0)
    return jnp.concatenate([kept, kept], axis=1)


def bands_kernel(layout, cut_rows, cut_cols, col_filter, *row_filters):
    seq_index = lax.axis_index("seq")
    position = lax.rem(seq_index, layout.members)
    frame = seq_index // layout.members

    column = iota((PW, LANES), 0)
    gap = jnp.zeros((LANES - PW, 2 * LANES), jnp.float32)
    table = jnp.concatenate([waves(2 * column, W), gap, waves(2 * column + 1, W), gap], axis=0)

    def tables(owners):
        line = iota((len(owners) * layout.lines, LANES), 0)
        places = line
        for n, owner in enumerate(owners):
            start = layout.first_line(owner) - n * layout.lines
            places = jnp.where(line >= n * layout.lines, line + start, places)
        return waves(places, H)

    givers, takers = layout.owners(position)
    given = tables(givers)
    taken = tables(takers)
    kept = kept_modes((2 * LANES, LANES), W, cut_cols[frame])
    high, low = split(dot3(split(table * kept), split(table), ((1,), (1,))))
    for n, part in enumerate((high, high, low)):
        col_filter[n * 2 * LANES : (n + 1) * 2 * LANES, :] = part
    kept = kept_modes((given.shape[0], LANES), H, cut_rows[frame])
    small = dot3(split(taken), split(given * kept), ((1,), (1,)))
    wide = given.shape[0]
    size = wide * layout.channels
    spread = (iota((wide, size), 1) // layout.channels == iota((wide, size), 0)).astype(
        jnp.bfloat16
    )
    shape = (layout.channels, size)
    same = lax.rem(iota(shape, 1), layout.channels) == iota(shape, 0)
    each = size // len(row_filters)
    for part, spots in zip(split(small), ((0, 2), (1,))):
        repeated = jnp.dot(part, spread, preferred_element_type=jnp.float32)
        for n in range(taken.shape[0]):
            block = jnp.where(same, repeated[n : n + 1], 0.0).astype(jnp.bfloat16)
            place = slice(n * layout.channels, (n + 1) * layout.channels)
            for half, out in enumerate(row_filters):
                for spot in spots:
                    out[place, spot * each : (spot + 1) * each] = block[
                        :, half * each : (half + 1) * each
                    ]


def product(left, right):
    return jnp.dot(left, right, preferred_element_type=jnp.float32)


def filtered(layout, slots, sources, col_filter, scratch):
    span, groups, channels, tokens = layout.span, layout.groups, layout.channels, layout.tokens
    window, lines, data = scratch
    givers, _ = layout.owners(lax.rem(lax.axis_index("seq"), layout.members))
    lane = iota((layout.rows, LANES), 1)
    chunks = window.shape[1] // LANES
    blank = jnp.zeros((layout.rows, LANES), jnp.float32)
    window[...] = jnp.zeros_like(window)
    for k, (slot, source) in enumerate(zip(slots, sources)):
        window[:, :tokens] = source[...]
        offset = layout.offset(givers[slot])
        turned = [
            pltpu.roll(window[:, g * LANES : (g + 1) * LANES], offset, 1) for g in range(chunks)
        ]
        turned = [blank] + turned + [blank] * (groups - chunks)
        placed = [jnp.where(lane >= offset, turned[g + 1], turned[g]) for g in range(groups)]
        for r in range(span):
            group, start = divmod(r * PW, LANES)
            if start == 0:
                line = placed[group]
            else:
                line = pltpu.roll(placed[group], LANES - start, 1)
                if start + PW > LANES:
                    rest = pltpu.roll(placed[group + 1], LANES - start, 1)
                    line = jnp.where(lane < LANES - start, line, rest)
            lines[r] = line
        for r in range(span):
            for dy in range(2):
                first = ((k * span + r) * 2 + dy) * channels
                for dx in range(2):
                    high, low = split(lines[r, pl.ds(2 * dy + dx, channels, stride=4), :])
                    for n, part in enumerate((high, low, high)):
                        left = (2 * n + dx) * LANES
                        data[first : first + channels, left : left + LANES] = part
    high, low = split(product(data[...], col_filter[...]))
    return jnp.concatenate([high, high, low], axis=0)


def early_kernel(layout, slots, col_filter, row_filter, *refs):
    sources, carry = refs[: len(slots)], refs[len(slots)]
    data = filtered(layout, slots, sources, col_filter, refs[len(slots) + 1 :])
    carry[...] = product(row_filter[...], data)


def place_part(layout, mixed, taker, out):
    span, groups = layout.span, layout.groups
    channels, tokens = layout.channels, layout.tokens
    lane = iota((channels, LANES), 1)
    offset = layout.offset(taker)
    back = lax.rem(LANES - offset, LANES)
    for dy in range(2):
        for dx in range(2):
            placed = [None] * (groups + 1)

            def put(group, value):
                old = placed[group]
                placed[group] = value if old is None else old + value

            for r in range(span):
                first = (r * 2 + dy) * channels
                line = mixed[first : first + channels, dx * LANES : (dx + 1) * LANES]
                group, start = divmod(r * PW, LANES)
                if start:
                    line = pltpu.roll(line, start, 1)
                if start + PW <= LANES:
                    put(group, line)
                else:
                    put(group, jnp.where(lane >= start, line, 0.0))
                    put(group + 1, jnp.where(lane < start, line, 0.0))
            turned = [pltpu.roll(p, back, 1) for p in placed[:groups]]
            first = (dy * 2 + dx) * channels
            for g in range(pl.cdiv(tokens, LANES)):
                value = jnp.where(lane < LANES - offset, turned[g], turned[g + 1])
                last = min(tokens, (g + 1) * LANES)
                out[first : first + channels, g * LANES : last] = value[:, : last - g * LANES]


def first_kernel(layout, slots, m, col_filter, row_filter, carry, *refs):
    sources = refs[: len(slots)]
    out, data = refs[len(slots) : len(slots) + 2]
    found = filtered(layout, slots, sources, col_filter, refs[len(slots) + 2 :])
    data[...] = found
    each = layout.lines * layout.channels
    _, takers = layout.owners(lax.rem(lax.axis_index("seq"), layout.members))
    rows = slice(m * each, (m + 1) * each)
    place_part(layout, carry[rows, :] + product(row_filter[rows, :], found), takers[m], out)


def rest_kernel(layout, others, row_filter, carry, data, *outs):
    _, takers = layout.owners(lax.rem(lax.axis_index("seq"), layout.members))
    each = layout.lines * layout.channels
    for m, out in zip(others, outs):
        rows = slice(m * each, (m + 1) * each)
        mixed = carry[rows, :] + product(row_filter[rows, :], data[...])
        place_part(layout, mixed, takers[m], out)


def norm_rows(hidden, modulation, scale, normed, start, stop, unroll=False):
    tiles = [slice(t, t + LANES) for t in range(0, hidden.shape[1], LANES)]
    block, pair = 16, 2
    scale[...] = 1.0 + modulation[1:2, :]

    def moments(rows, count):
        sums = [jnp.zeros((count, LANES), jnp.float32) for _ in range(2)]
        squares = list(sums)
        for t, columns in enumerate(tiles):
            value = hidden[rows, columns].astype(jnp.float32)
            sums[t % 2] += value
            squares[t % 2] += value * value
        average = jnp.sum(sums[0] + sums[1], axis=1, keepdims=True) / D
        square = jnp.sum(squares[0] + squares[1], axis=1, keepdims=True) / D
        scale_inv = lax.rsqrt(square - average * average + EPSILON)
        return [jnp.broadcast_to(v, (count, LANES)) for v in (average, scale_inv)]

    def norm(rows, place, average, scale_inv):
        for columns in tiles:
            value = hidden[rows, columns].astype(jnp.float32)
            value = (value - average) * scale_inv
            value = value * scale[:, columns] + modulation[0:1, columns]
            normed[place, columns] = value.astype(jnp.bfloat16)

    whole = (stop - start) // (block * pair)

    @pl.loop(0, whole, unroll=unroll)
    def _(n):
        first = pl.multiple_of(n * (block * pair), block)
        rows = [pl.ds(start + first + p * block, block) for p in range(pair)]
        found = [moments(r, block) for r in rows]
        for p in range(pair):
            norm(rows[p], pl.ds(first + p * block, block), *found[p])

    for first in range(start + whole * block * pair, stop, block):
        rows = slice(first, min(stop, first + block))
        found = moments(rows, rows.stop - first)
        norm(rows, slice(first - start, rows.stop - start), *found)


def norm_kernel(hidden, modulation, normed, scale):
    norm_rows(hidden, modulation, scale, normed, 0, normed.shape[0])


def project_kernel(
    layout,
    early_normed,
    hidden,
    modulation,
    weight,
    bias,
    residual,
    band_gain,
    skip_flags,
    step_index,
    base,
    row_low,
    step,
    normed,
    scale,
):
    tokens, first = hidden.shape[0], early_normed.shape[0]
    current = jnp.full((1, 1), step_index[0], jnp.int32)
    counter = iota(skip_flags.shape, 1)
    computed = (skip_flags[...] == 0) & (counter <= current)
    last_full = jnp.max(jnp.where(computed, counter, -1), axis=1, keepdims=True)
    spacing = (current - last_full).astype(jnp.float32)
    gap_ratio = spacing / (spacing + 2.0)
    shape = (layout.rows, layout.channels)
    own = iota(shape, 0) // 4 == iota(shape, 1)
    w_low, w_high = (
        jnp.sum(jnp.where(own, band_gain[n : n + 1, :], 0.0), axis=1, keepdims=True) * factor
        for n, factor in enumerate((1.0 + gap_ratio, 1.0 - 0.5 * gap_ratio))
    )

    def project(rows, columns):
        conditional = lax.dot_general(
            rows[...], weight[...], (((1,), (1,)), ((), ())), preferred_element_type=jnp.float32
        )
        conditional = (conditional + bias[...]).T
        base[:, columns] = conditional + GUIDE_EXTRA * w_high * residual[:, columns]

    if first:
        project(early_normed, slice(0, first))
    norm_rows(hidden, modulation, scale, normed, first, tokens, unroll=True)
    project(normed, slice(first, tokens))
    row_low[...] = jnp.broadcast_to(GUIDE_EXTRA * (w_low - w_high), row_low.shape)
    step[...] = jnp.broadcast_to(sigma_at(current + 1) - sigma_at(current), step.shape)


def finish_kernel(layout, *refs):
    near, channels, tokens = layout.near, layout.channels, layout.tokens
    parts = refs[:near]
    base, row_low, step, latent, velocity, latent_next, total = refs[near:]
    for g in range(total.shape[0]):
        last = min(tokens, (g + 1) * LANES)
        columns = slice(g * LANES, last)
        width = slice(0, last - g * LANES)
        low_band = parts[0][:, columns]
        for m in range(1, near):
            low_band += parts[m][:, columns]
        total[g, :, width] = low_band
        for c in range(channels):
            rows = slice(4 * c, 4 * c + 4)
            low_band = total[g, pl.ds(c, 4, stride=channels), :][:, width]
            value = base[rows, columns] + row_low[rows, width] * low_band
            velocity[rows, columns] = value
            latent_next[rows, columns] = latent[rows, columns] + step[:4, width] * value


VMEM = pl.BlockSpec(memory_space=pltpu.VMEM)
SMEM = pl.BlockSpec(memory_space=pltpu.SMEM)


def bands(layout, cut_rows, cut_cols):
    wide = layout.far * layout.lines * layout.channels
    tall = layout.near * layout.lines * layout.channels
    col = jax.ShapeDtypeStruct((6 * LANES, 2 * LANES), jnp.bfloat16)
    row = jax.ShapeDtypeStruct((tall, 3 * wide // 2), jnp.bfloat16)
    return pl.pallas_call(
        functools.partial(bands_kernel, layout),
        out_shape=[col, row, row],
        in_specs=[SMEM, SMEM],
        out_specs=[VMEM] * 3,
        compiler_params=pltpu.CompilerParams(vmem_limit_bytes=8 * 2**20),
        cost_estimate=pl.CostEstimate(flops=10**9, bytes_accessed=2 * 10**7, transcendentals=0),
        name="bands",
    )(cut_rows, cut_cols)


def mix_scratch(layout, count):
    return [
        pltpu.VMEM((layout.rows, pl.cdiv(layout.tokens, LANES) * LANES), jnp.float32),
        pltpu.VMEM((layout.span, layout.rows, LANES), jnp.float32),
        pltpu.VMEM((count * layout.lines * layout.channels, 6 * LANES), jnp.bfloat16),
    ]


def early(layout, filters, slots, sources):
    tall = layout.near * layout.lines * layout.channels
    return pl.pallas_call(
        functools.partial(early_kernel, layout, slots),
        out_shape=jax.ShapeDtypeStruct((tall, 2 * LANES), jnp.float32),
        in_specs=[VMEM] * (2 + len(slots)),
        out_specs=VMEM,
        scratch_shapes=mix_scratch(layout, len(slots)),
        compiler_params=pltpu.CompilerParams(vmem_limit_bytes=8 * 2**20),
        cost_estimate=pl.CostEstimate(flops=10**9, bytes_accessed=10**6, transcendentals=0),
        name="early",
    )(*filters, *sources)


def mix_first(layout, filters, carry, slots, sources, m):
    wide = len(slots) * layout.lines * layout.channels
    return pl.pallas_call(
        functools.partial(first_kernel, layout, slots, m),
        out_shape=[
            jax.ShapeDtypeStruct((layout.rows, layout.tokens), jnp.float32),
            jax.ShapeDtypeStruct((3 * wide, 2 * LANES), jnp.bfloat16),
        ],
        in_specs=[VMEM] * (3 + len(slots)),
        out_specs=[VMEM] * 2,
        scratch_shapes=mix_scratch(layout, len(slots)),
        compiler_params=pltpu.CompilerParams(vmem_limit_bytes=8 * 2**20),
        cost_estimate=pl.CostEstimate(flops=10**9, bytes_accessed=10**6, transcendentals=0),
        name="mix_first",
    )(*filters, carry, *sources)


def mix_rest(layout, row_filter, carry, data, others):
    shape = jax.ShapeDtypeStruct((layout.rows, layout.tokens), jnp.float32)
    return pl.pallas_call(
        functools.partial(rest_kernel, layout, others),
        out_shape=[shape] * len(others),
        in_specs=[VMEM] * 3,
        out_specs=[VMEM] * len(others),
        compiler_params=pltpu.CompilerParams(vmem_limit_bytes=8 * 2**20),
        cost_estimate=pl.CostEstimate(flops=10**9, bytes_accessed=10**6, transcendentals=0),
        name="mix_rest",
    )(row_filter, carry, data)


def head(layout, hidden, modulation, head_weight, head_bias, residual, gain, flags, step_index):
    first = hidden.shape[0] // LANES * LANES
    scale = pltpu.VMEM((1, hidden.shape[1]), jnp.float32)
    normed = pl.pallas_call(
        norm_kernel,
        out_shape=jax.ShapeDtypeStruct((first, hidden.shape[1]), jnp.bfloat16),
        in_specs=[VMEM] * 2,
        out_specs=VMEM,
        scratch_shapes=[scale],
        compiler_params=pltpu.CompilerParams(vmem_limit_bytes=8 * 2**20),
        cost_estimate=pl.CostEstimate(
            flops=10 * hidden.size, bytes_accessed=10**7, transcendentals=0
        ),
        name="norm",
    )(hidden, modulation)
    return pl.pallas_call(
        functools.partial(project_kernel, layout),
        out_shape=[
            jax.ShapeDtypeStruct(residual.shape, jnp.float32),
            jax.ShapeDtypeStruct((layout.rows, LANES), jnp.float32),
            jax.ShapeDtypeStruct((8, LANES), jnp.float32),
        ],
        in_specs=[VMEM] * 8 + [SMEM],
        out_specs=[VMEM] * 3,
        scratch_shapes=[
            pltpu.VMEM((hidden.shape[0] - first, hidden.shape[1]), jnp.bfloat16),
            scale,
        ],
        compiler_params=pltpu.CompilerParams(vmem_limit_bytes=8 * 2**20),
        cost_estimate=pl.CostEstimate(
            flops=2 * hidden.size * layout.rows, bytes_accessed=3 * 10**6, transcendentals=0
        ),
        name="project",
    )(
        normed,
        hidden,
        modulation,
        head_weight.T,
        head_bias.reshape(1, -1),
        residual,
        gain,
        flags.reshape(1, -1),
        step_index,
    )


def head_in_parts(
    layout, hidden, modulation, head_weight, head_bias, residual, gain, flags, step_index
):
    values = hidden.astype(jnp.float32)
    moments = lax.psum((jnp.sum(values, axis=1), jnp.sum(values * values, axis=1)), "mp")
    average = moments[0] / D
    scale_inv = lax.rsqrt(moments[1] / D - average * average + EPSILON)
    normed = (
        (values - average[:, None]) * scale_inv[:, None] * (1.0 + modulation[1]) + modulation[0]
    ).astype(jnp.bfloat16)
    conditional = (
        lax.psum_scatter(
            lax.dot_general(
                head_weight, normed, (((0,), (1,)), ((), ())), preferred_element_type=jnp.float32
            ),
            "mp",
            scatter_dimension=0,
            tiled=True,
        )
        + head_bias[:, None]
    )
    w_low, w_high = band_weights(flags, step_index, gain)
    row_high = GUIDE_EXTRA * jnp.repeat(w_high, 4)[:, None]
    row_low = GUIDE_EXTRA * jnp.repeat(w_low - w_high, 4)[:, None]
    current = step_index[0]
    return (
        conditional + row_high * residual,
        jnp.broadcast_to(row_low, (layout.rows, LANES)),
        jnp.broadcast_to(sigma_at(current + 1) - sigma_at(current), (8, LANES)),
    )


def finish(layout, parts, base, row_low, step, latent):
    shape = jax.ShapeDtypeStruct((layout.rows, layout.tokens), jnp.float32)
    return pl.pallas_call(
        functools.partial(finish_kernel, layout),
        out_shape=[shape, shape],
        in_specs=[VMEM] * (layout.near + 4),
        out_specs=[VMEM, VMEM],
        scratch_shapes=[
            pltpu.VMEM((pl.cdiv(layout.tokens, LANES), layout.rows, LANES), jnp.float32)
        ],
        compiler_params=pltpu.CompilerParams(vmem_limit_bytes=8 * 2**20),
        name="finish",
    )(*parts, base, row_low, step, latent)


def body(
    hidden,
    modulation,
    head_weight,
    head_bias,
    residual,
    latent,
    band_gain,
    cut_rows,
    cut_cols,
    skip_flags,
    step_index,
):
    layout = Layout(*residual.shape)
    places = lax.axis_size("seq")

    def exchange(values, masks):
        swapped = [values[0]]
        for turn, mask in enumerate(masks[1:]):
            pairs = [(s, s ^ mask) for s in range(places)]
            swapped.append(lax.ppermute(values[turn + 1], "seq", pairs))
        return swapped

    masks = [k * layout.near for k in layout.far_order()]
    sources = exchange([residual] * layout.far, masks)
    col_filter, row_early, row_late = bands(layout, cut_rows, cut_cols)
    run_head = head if lax.axis_size("mp") == 1 else head_in_parts
    base, row_low, step = run_head(
        layout,
        hidden,
        modulation,
        head_weight,
        head_bias,
        residual,
        band_gain,
        skip_flags,
        step_index,
    )
    slots = list(range(layout.far))
    half = layout.far // 2
    carry = early(layout, (col_filter, row_early), slots[:half], sources[:half])
    filters = (col_filter, row_late)
    part, data = mix_first(layout, filters, carry, slots[half:], sources[half:], 1)
    own, *rest = mix_rest(layout, row_late, carry, data, [0, *range(2, layout.near)])
    parts = exchange([own, part, *rest], layout.near_order())
    return finish(layout, parts, base, row_low, step, latent)


def solution(mesh):
    in_specs = (
        P(("groups", "seq"), "mp"),
        P("groups", "mp"),
        P("mp", None),
        P("mp"),
        P("mp", ("groups", "seq")),
        P("mp", ("groups", "seq")),
        P(None, "mp"),
        P("groups"),
        P("groups"),
        P("groups"),
        P("groups"),
    )
    out_specs = (P("mp", ("groups", "seq")), P("mp", ("groups", "seq")))
    return jax.shard_map(body, mesh=mesh, in_specs=in_specs, out_specs=out_specs, check_vma=False)
```

```python
import functools
import math

import jax
import jax.numpy as jnp
from jax import lax
from jax.experimental import pallas as pl
from jax.experimental.pallas import tpu as pltpu
from jax.sharding import PartitionSpec as P


D = 5120
H = 90
W = 160
PH = 45
PW = 80
NSTEP = 50

EPSILON = 1e-06
GUIDE_EXTRA = 4.0
SHIFT_FACTOR = 5.0
LANES = 128


def sigma_at(step_number):
    remain = 1.0 - step_number.astype(jnp.float32) / NSTEP
    return SHIFT_FACTOR * remain / (1.0 + (SHIFT_FACTOR - 1.0) * remain)


def band_weights(skip_flags, step_index, band_gain):
    current = step_index[0]
    counter = jnp.arange(NSTEP, dtype=jnp.int32)
    computed = (skip_flags == 0) & (counter <= current)
    last_full = jnp.max(jnp.where(computed, counter, -1))
    spacing = (current - last_full).astype(jnp.float32)
    gap_ratio = spacing / (spacing + 2.0)
    return (band_gain[0] * (1.0 + gap_ratio), band_gain[1] * (1.0 - 0.5 * gap_ratio))


def split(value):
    high = value.astype(jnp.bfloat16)
    return high, (value - high.astype(jnp.float32)).astype(jnp.bfloat16)


def dot3(left, right, contract=((1,), (0,))):
    (lh, ll), (rh, rl) = left, right

    def dot(one, other):
        return lax.dot_general(
            one, other, (contract, ((), ())), preferred_element_type=jnp.float32
        )

    return dot(lh, rh) + (dot(ll, rh) + dot(lh, rl))


def iota(shape, axis):
    return lax.broadcasted_iota(jnp.int32, shape, axis)


class Layout:
    def __init__(self, local_rows, local_tokens):
        self.rows = local_rows
        self.tokens = local_tokens
        self.channels = local_rows // 4
        self.members = PH * PW // local_tokens
        bits = self.members.bit_length() - 1
        self.near = 1 << (bits // 2)
        self.far = self.members // self.near
        self.span = max(
            (p * local_tokens % PW + local_tokens + PW - 1) // PW
            for p in range(self.members)
        )
        self.lines = 2 * self.span
        self.groups = pl.cdiv(self.span * PW, LANES)

    def owners(self, position):
        givers = [position ^ (k * self.near) for k in self.far_order()]
        takers = [position ^ m for m in self.near_order()]
        return givers, takers

    def far_order(self):
        return [0, *range(2, self.far), 1][: self.far]

    def near_order(self):
        return [0, *range(self.near - 1, 0, -1)]

    def offset(self, owner):
        return lax.rem(owner * self.tokens, PW)

    def first_line(self, owner):
        return 2 * (owner * self.tokens // PW)


def cosine_of_turns(turns):
    angle = 2.0 * math.pi * (0.25 - jnp.abs(turns - 0.5))
    square = angle * angle
    series = jnp.full_like(square, -1.0 / math.factorial(11))
    for power in (9, 7, 5, 3, 1):
        series = series * square + (-1.0) ** (power // 2) / math.factorial(power)
    return -angle * series


def waves(places, length):
    phase = (places * iota(places.shape, 1)).astype(jnp.float32)
    phase = phase - length * jnp.floor((phase + 0.5) * (1.0 / length))
    turns = phase * (1.0 / length)
    later = jnp.where(turns < 0.25, turns + 0.75, turns - 0.25)
    return jnp.concatenate([cosine_of_turns(turns), cosine_of_turns(later)], axis=1)


def kept_modes(shape, length, cutoff):
    modes = iota(shape, 1)
    weight = jnp.where((modes == 0) | (2 * modes == length), 1.0, 2.0) / length
    kept = jnp.where((modes <= cutoff) & (2 * modes <= length), weight, 0.0)
    return jnp.concatenate([kept, kept], axis=1)


def bands_kernel(layout, cut_rows, cut_cols, col_filter, *row_filters):
    seq_index = lax.axis_index("seq")
    position = lax.rem(seq_index, layout.members)
    frame = seq_index // layout.members

    column = iota((PW, LANES), 0)
    gap = jnp.zeros((LANES - PW, 2 * LANES), jnp.float32)
    table = jnp.concatenate([waves(2 * column, W), gap, waves(2 * column + 1, W), gap], axis=0)

    def tables(owners):
        line = iota((len(owners) * layout.lines, LANES), 0)
        places = line
        for n, owner in enumerate(owners):
            start = layout.first_line(owner) - n * layout.lines
            places = jnp.where(line >= n * layout.lines, line + start, places)
        return waves(places, H)

    givers, takers = layout.owners(position)
    given = tables(givers)
    taken = tables(takers)
    kept = kept_modes((2 * LANES, LANES), W, cut_cols[frame])
    high, low = split(dot3(split(table * kept), split(table), ((1,), (1,))))
    for n, part in enumerate((high, high, low)):
        col_filter[n * 2 * LANES : (n + 1) * 2 * LANES, :] = part
    kept = kept_modes((given.shape[0], LANES), H, cut_rows[frame])
    small = dot3(split(taken), split(given * kept), ((1,), (1,)))
    wide = given.shape[0]
    size = wide * layout.channels
    spread = (iota((wide, size), 1) // layout.channels == iota((wide, size), 0)).astype(
        jnp.bfloat16
    )
    shape = (layout.channels, size)
    same = lax.rem(iota(shape, 1), layout.channels) == iota(shape, 0)
    each = size // len(row_filters)
    for part, spots in zip(split(small), ((0, 2), (1,))):
        repeated = jnp.dot(part, spread, preferred_element_type=jnp.float32)
        for n in range(taken.shape[0]):
            block = jnp.where(same, repeated[n : n + 1], 0.0).astype(jnp.bfloat16)
            place = slice(n * layout.channels, (n + 1) * layout.channels)
            for half, out in enumerate(row_filters):
                for spot in spots:
                    out[place, spot * each : (spot + 1) * each] = block[
                        :, half * each : (half + 1) * each
                    ]


def product(left, right):
    return jnp.dot(left, right, preferred_element_type=jnp.float32)


def filtered(layout, slots, sources, col_filter, scratch):
    span, groups, channels, tokens = layout.span, layout.groups, layout.channels, layout.tokens
    window, lines, data = scratch
    givers, _ = layout.owners(lax.rem(lax.axis_index("seq"), layout.members))
    lane = iota((layout.rows, LANES), 1)
    chunks = window.shape[1] // LANES
    blank = jnp.zeros((layout.rows, LANES), jnp.float32)
    window[...] = jnp.zeros_like(window)
    for k, (slot, source) in enumerate(zip(slots, sources)):
        window[:, :tokens] = source[...]
        offset = layout.offset(givers[slot])
        turned = [
            pltpu.roll(window[:, g * LANES : (g + 1) * LANES], offset, 1) for g in range(chunks)
        ]
        turned = [blank] + turned + [blank] * (groups - chunks)
        placed = [jnp.where(lane >= offset, turned[g + 1], turned[g]) for g in range(groups)]
        for r in range(span):
            group, start = divmod(r * PW, LANES)
            if start == 0:
                line = placed[group]
            else:
                line = pltpu.roll(placed[group], LANES - start, 1)
                if start + PW > LANES:
                    rest = pltpu.roll(placed[group + 1], LANES - start, 1)
                    line = jnp.where(lane < LANES - start, line, rest)
            lines[r] = line
        for r in range(span):
            for dy in range(2):
                first = ((k * span + r) * 2 + dy) * channels
                for dx in range(2):
                    high, low = split(lines[r, pl.ds(2 * dy + dx, channels, stride=4), :])
                    for n, part in enumerate((high, low, high)):
                        left = (2 * n + dx) * LANES
                        data[first : first + channels, left : left + LANES] = part
    each = layout.lines * channels
    halves = [
        split(product(data[k * each : (k + 1) * each, :], col_filter[...]))
        for k in range(len(slots))
    ]
    high, low = (jnp.concatenate(h, axis=0) for h in zip(*halves))
    return jnp.concatenate([high, high, low], axis=0)


def early_kernel(layout, slots, col_filter, row_filter, *refs):
    sources, carry = refs[: len(slots)], refs[len(slots)]
    data = filtered(layout, slots, sources, col_filter, refs[len(slots) + 1 :])
    carry[...] = product(row_filter[...], data)


def place_part(layout, mixed, taker, out):
    span, groups = layout.span, layout.groups
    channels, tokens = layout.channels, layout.tokens
    lane = iota((channels, LANES), 1)
    offset = layout.offset(taker)
    back = lax.rem(LANES - offset, LANES)
    for dy in range(2):
        for dx in range(2):
            placed = [None] * (groups + 1)

            def put(group, value):
                old = placed[group]
                placed[group] = value if old is None else old + value

            for r in range(span):
                first = (r * 2 + dy) * channels
                line = mixed[first : first + channels, dx * LANES : (dx + 1) * LANES]
                group, start = divmod(r * PW, LANES)
                if start:
                    line = pltpu.roll(line, start, 1)
                if start + PW <= LANES:
                    put(group, line)
                else:
                    put(group, jnp.where(lane >= start, line, 0.0))
                    put(group + 1, jnp.where(lane < start, line, 0.0))
            turned = [pltpu.roll(p, back, 1) for p in placed[:groups]]
            first = (dy * 2 + dx) * channels
            for g in range(pl.cdiv(tokens, LANES)):
                value = jnp.where(lane < LANES - offset, turned[g], turned[g + 1])
                last = min(tokens, (g + 1) * LANES)
                out[first : first + channels, g * LANES : last] = value[:, : last - g * LANES]


def first_kernel(layout, slots, m, col_filter, row_filter, carry, *refs):
    sources = refs[: len(slots)]
    out, data = refs[len(slots) : len(slots) + 2]
    found = filtered(layout, slots, sources, col_filter, refs[len(slots) + 2 :])
    data[...] = found
    each = layout.lines * layout.channels
    _, takers = layout.owners(lax.rem(lax.axis_index("seq"), layout.members))
    rows = slice(m * each, (m + 1) * each)
    place_part(layout, carry[rows, :] + product(row_filter[rows, :], found), takers[m], out)


def rest_kernel(layout, others, row_filter, carry, data, *outs):
    _, takers = layout.owners(lax.rem(lax.axis_index("seq"), layout.members))
    each = layout.lines * layout.channels
    for m, out in zip(others, outs):
        rows = slice(m * each, (m + 1) * each)
        mixed = carry[rows, :] + product(row_filter[rows, :], data[...])
        place_part(layout, mixed, takers[m], out)


def norm_rows(hidden, modulation, scale, normed, start, stop, unroll=False):
    tiles = [slice(t, t + LANES) for t in range(0, hidden.shape[1], LANES)]
    block, pair = 16, 2
    scale[...] = 1.0 + modulation[1:2, :]

    def moments(rows, count):
        sums = [jnp.zeros((count, LANES), jnp.float32) for _ in range(2)]
        squares = list(sums)
        for t, columns in enumerate(tiles):
            value = hidden[rows, columns].astype(jnp.float32)
            sums[t % 2] += value
            squares[t % 2] += value * value
        average = jnp.sum(sums[0] + sums[1], axis=1, keepdims=True) / D
        square = jnp.sum(squares[0] + squares[1], axis=1, keepdims=True) / D
        scale_inv = lax.rsqrt(square - average * average + EPSILON)
        return [jnp.broadcast_to(v, (count, LANES)) for v in (average, scale_inv)]

    def norm(rows, place, average, scale_inv):
        for columns in tiles:
            value = hidden[rows, columns].astype(jnp.float32)
            value = (value - average) * scale_inv
            value = value * scale[:, columns] + modulation[0:1, columns]
            normed[place, columns] = value.astype(jnp.bfloat16)

    whole = (stop - start) // (block * pair)

    @pl.loop(0, whole, unroll=unroll)
    def _(n):
        first = pl.multiple_of(n * (block * pair), block)
        rows = [pl.ds(start + first + p * block, block) for p in range(pair)]
        found = [moments(r, block) for r in rows]
        for p in range(pair):
            norm(rows[p], pl.ds(first + p * block, block), *found[p])

    for first in range(start + whole * block * pair, stop, block):
        rows = slice(first, min(stop, first + block))
        found = moments(rows, rows.stop - first)
        norm(rows, slice(first - start, rows.stop - start), *found)


def norm_kernel(hidden, modulation, normed, scale):
    norm_rows(hidden, modulation, scale, normed, 0, normed.shape[0], unroll=True)


def project_kernel(
    layout,
    early_normed,
    hidden,
    modulation,
    weight,
    bias,
    residual,
    band_gain,
    skip_flags,
    step_index,
    base,
    row_low,
    step,
    normed,
    scale,
):
    tokens, first = hidden.shape[0], early_normed.shape[0]
    current = jnp.full((1, 1), step_index[0], jnp.int32)
    counter = iota(skip_flags.shape, 1)
    computed = (skip_flags[...] == 0) & (counter <= current)
    last_full = jnp.max(jnp.where(computed, counter, -1), axis=1, keepdims=True)
    spacing = (current - last_full).astype(jnp.float32)
    gap_ratio = spacing / (spacing + 2.0)
    shape = (layout.rows, layout.channels)
    own = iota(shape, 0) // 4 == iota(shape, 1)
    w_low, w_high = (
        jnp.sum(jnp.where(own, band_gain[n : n + 1, :], 0.0), axis=1, keepdims=True) * factor
        for n, factor in enumerate((1.0 + gap_ratio, 1.0 - 0.5 * gap_ratio))
    )

    def project(rows, columns):
        conditional = lax.dot_general(
            rows[...], weight[...], (((1,), (1,)), ((), ())), preferred_element_type=jnp.float32
        )
        conditional = (conditional + bias[...]).T
        base[:, columns] = conditional + GUIDE_EXTRA * w_high * residual[:, columns]

    if first:
        project(early_normed, slice(0, first))
    norm_rows(hidden, modulation, scale, normed, first, tokens, unroll=True)
    project(normed, slice(first, tokens))
    row_low[...] = jnp.broadcast_to(GUIDE_EXTRA * (w_low - w_high), row_low.shape)
    step[...] = jnp.broadcast_to(sigma_at(current + 1) - sigma_at(current), step.shape)


def finish_kernel(layout, *refs):
    near, channels, tokens = layout.near, layout.channels, layout.tokens
    parts = refs[:near]
    base, row_low, step, latent, velocity, latent_next, total = refs[near:]
    for g in range(total.shape[0]):
        last = min(tokens, (g + 1) * LANES)
        columns = slice(g * LANES, last)
        width = slice(0, last - g * LANES)
        low_band = parts[0][:, columns]
        for m in range(1, near):
            low_band += parts[m][:, columns]
        total[g, :, width] = low_band
        for c in range(channels):
            rows = slice(4 * c, 4 * c + 4)
            low_band = total[g, pl.ds(c, 4, stride=channels), :][:, width]
            value = base[rows, columns] + row_low[rows, width] * low_band
            velocity[rows, columns] = value
            latent_next[rows, columns] = latent[rows, columns] + step[:4, width] * value


VMEM = pl.BlockSpec(memory_space=pltpu.VMEM)
SMEM = pl.BlockSpec(memory_space=pltpu.SMEM)


def bands(layout, cut_rows, cut_cols):
    wide = layout.far * layout.lines * layout.channels
    tall = layout.near * layout.lines * layout.channels
    col = jax.ShapeDtypeStruct((6 * LANES, 2 * LANES), jnp.bfloat16)
    row = jax.ShapeDtypeStruct((tall, 3 * wide // 2), jnp.bfloat16)
    return pl.pallas_call(
        functools.partial(bands_kernel, layout),
        out_shape=[col, row, row],
        in_specs=[SMEM, SMEM],
        out_specs=[VMEM] * 3,
        compiler_params=pltpu.CompilerParams(vmem_limit_bytes=8 * 2**20),
        cost_estimate=pl.CostEstimate(flops=10**9, bytes_accessed=2 * 10**7, transcendentals=0),
        name="bands",
    )(cut_rows, cut_cols)


def mix_scratch(layout, count):
    return [
        pltpu.VMEM((layout.rows, pl.cdiv(layout.tokens, LANES) * LANES), jnp.float32),
        pltpu.VMEM((layout.span, layout.rows, LANES), jnp.float32),
        pltpu.VMEM((count * layout.lines * layout.channels, 6 * LANES), jnp.bfloat16),
    ]


def early(layout, filters, slots, sources):
    tall = layout.near * layout.lines * layout.channels
    return pl.pallas_call(
        functools.partial(early_kernel, layout, slots),
        out_shape=jax.ShapeDtypeStruct((tall, 2 * LANES), jnp.float32),
        in_specs=[VMEM] * (2 + len(slots)),
        out_specs=VMEM,
        scratch_shapes=mix_scratch(layout, len(slots)),
        compiler_params=pltpu.CompilerParams(vmem_limit_bytes=8 * 2**20),
        cost_estimate=pl.CostEstimate(flops=10**9, bytes_accessed=10**6, transcendentals=0),
        name="early",
    )(*filters, *sources)


def mix_first(layout, filters, carry, slots, sources, m):
    wide = len(slots) * layout.lines * layout.channels
    return pl.pallas_call(
        functools.partial(first_kernel, layout, slots, m),
        out_shape=[
            jax.ShapeDtypeStruct((layout.rows, layout.tokens), jnp.float32),
            jax.ShapeDtypeStruct((3 * wide, 2 * LANES), jnp.bfloat16),
        ],
        in_specs=[VMEM] * (3 + len(slots)),
        out_specs=[VMEM] * 2,
        scratch_shapes=mix_scratch(layout, len(slots)),
        compiler_params=pltpu.CompilerParams(vmem_limit_bytes=8 * 2**20),
        cost_estimate=pl.CostEstimate(flops=10**9, bytes_accessed=10**6, transcendentals=0),
        name="mix_first",
    )(*filters, carry, *sources)


def mix_rest(layout, row_filter, carry, data, others):
    shape = jax.ShapeDtypeStruct((layout.rows, layout.tokens), jnp.float32)
    return pl.pallas_call(
        functools.partial(rest_kernel, layout, others),
        out_shape=[shape] * len(others),
        in_specs=[VMEM] * 3,
        out_specs=[VMEM] * len(others),
        compiler_params=pltpu.CompilerParams(vmem_limit_bytes=8 * 2**20),
        cost_estimate=pl.CostEstimate(flops=10**9, bytes_accessed=10**6, transcendentals=0),
        name="mix_rest",
    )(row_filter, carry, data)


def head(layout, hidden, modulation, head_weight, head_bias, residual, gain, flags, step_index):
    first = hidden.shape[0] // LANES * LANES
    scale = pltpu.VMEM((1, hidden.shape[1]), jnp.float32)
    normed = pl.pallas_call(
        norm_kernel,
        out_shape=jax.ShapeDtypeStruct((first, hidden.shape[1]), jnp.bfloat16),
        in_specs=[VMEM] * 2,
        out_specs=VMEM,
        scratch_shapes=[scale],
        compiler_params=pltpu.CompilerParams(vmem_limit_bytes=8 * 2**20),
        cost_estimate=pl.CostEstimate(
            flops=10 * hidden.size, bytes_accessed=10**7, transcendentals=0
        ),
        name="norm",
    )(hidden, modulation)
    return pl.pallas_call(
        functools.partial(project_kernel, layout),
        out_shape=[
            jax.ShapeDtypeStruct(residual.shape, jnp.float32),
            jax.ShapeDtypeStruct((layout.rows, LANES), jnp.float32),
            jax.ShapeDtypeStruct((8, LANES), jnp.float32),
        ],
        in_specs=[VMEM] * 8 + [SMEM],
        out_specs=[VMEM] * 3,
        scratch_shapes=[
            pltpu.VMEM((hidden.shape[0] - first, hidden.shape[1]), jnp.bfloat16),
            scale,
        ],
        compiler_params=pltpu.CompilerParams(vmem_limit_bytes=8 * 2**20),
        cost_estimate=pl.CostEstimate(
            flops=2 * hidden.size * layout.rows, bytes_accessed=3 * 10**6, transcendentals=0
        ),
        name="project",
    )(
        normed,
        hidden,
        modulation,
        head_weight.T,
        head_bias.reshape(1, -1),
        residual,
        gain,
        flags.reshape(1, -1),
        step_index,
    )


def head_in_parts(
    layout, hidden, modulation, head_weight, head_bias, residual, gain, flags, step_index
):
    values = hidden.astype(jnp.float32)
    moments = lax.psum((jnp.sum(values, axis=1), jnp.sum(values * values, axis=1)), "mp")
    average = moments[0] / D
    scale_inv = lax.rsqrt(moments[1] / D - average * average + EPSILON)
    normed = (
        (values - average[:, None]) * scale_inv[:, None] * (1.0 + modulation[1]) + modulation[0]
    ).astype(jnp.bfloat16)
    conditional = (
        lax.psum_scatter(
            lax.dot_general(
                head_weight, normed, (((0,), (1,)), ((), ())), preferred_element_type=jnp.float32
            ),
            "mp",
            scatter_dimension=0,
            tiled=True,
        )
        + head_bias[:, None]
    )
    w_low, w_high = band_weights(flags, step_index, gain)
    row_high = GUIDE_EXTRA * jnp.repeat(w_high, 4)[:, None]
    row_low = GUIDE_EXTRA * jnp.repeat(w_low - w_high, 4)[:, None]
    current = step_index[0]
    return (
        conditional + row_high * residual,
        jnp.broadcast_to(row_low, (layout.rows, LANES)),
        jnp.broadcast_to(sigma_at(current + 1) - sigma_at(current), (8, LANES)),
    )


def finish(layout, parts, base, row_low, step, latent):
    shape = jax.ShapeDtypeStruct((layout.rows, layout.tokens), jnp.float32)
    return pl.pallas_call(
        functools.partial(finish_kernel, layout),
        out_shape=[shape, shape],
        in_specs=[VMEM] * (layout.near + 4),
        out_specs=[VMEM, VMEM],
        scratch_shapes=[
            pltpu.VMEM((pl.cdiv(layout.tokens, LANES), layout.rows, LANES), jnp.float32)
        ],
        compiler_params=pltpu.CompilerParams(vmem_limit_bytes=8 * 2**20),
        name="finish",
    )(*parts, base, row_low, step, latent)


def body(
    hidden,
    modulation,
    head_weight,
    head_bias,
    residual,
    latent,
    band_gain,
    cut_rows,
    cut_cols,
    skip_flags,
    step_index,
):
    layout = Layout(*residual.shape)
    places = lax.axis_size("seq")

    def exchange(values, masks):
        swapped = [values[0]]
        for turn, mask in enumerate(masks[1:]):
            pairs = [(s, s ^ mask) for s in range(places)]
            swapped.append(lax.ppermute(values[turn + 1], "seq", pairs))
        return swapped

    masks = [k * layout.near for k in layout.far_order()]
    sources = exchange([residual] * layout.far, masks)
    col_filter, row_early, row_late = bands(layout, cut_rows, cut_cols)
    run_head = head if lax.axis_size("mp") == 1 else head_in_parts
    base, row_low, step = run_head(
        layout,
        hidden,
        modulation,
        head_weight,
        head_bias,
        residual,
        band_gain,
        skip_flags,
        step_index,
    )
    slots = list(range(layout.far))
    half = layout.far // 2
    carry = early(layout, (col_filter, row_early), slots[:half], sources[:half])
    filters = (col_filter, row_late)
    part, data = mix_first(layout, filters, carry, slots[half:], sources[half:], 1)
    own, *rest = mix_rest(layout, row_late, carry, data, [0, *range(2, layout.near)])
    parts = exchange([own, part, *rest], layout.near_order())
    return finish(layout, parts, base, row_low, step, latent)


def solution(mesh):
    in_specs = (
        P(("groups", "seq"), "mp"),
        P("groups", "mp"),
        P("mp", None),
        P("mp"),
        P("mp", ("groups", "seq")),
        P("mp", ("groups", "seq")),
        P(None, "mp"),
        P("groups"),
        P("groups"),
        P("groups"),
        P("groups"),
    )
    out_specs = (P("mp", ("groups", "seq")), P("mp", ("groups", "seq")))
    return jax.shard_map(body, mesh=mesh, in_specs=in_specs, out_specs=out_specs, check_vma=False)
```

```python
import functools
import math

import jax
import jax.numpy as jnp
from jax import lax
from jax.experimental import pallas as pl
from jax.experimental.pallas import tpu as pltpu
from jax.sharding import PartitionSpec as P


D = 5120
H = 90
W = 160
PH = 45
PW = 80
NSTEP = 50

EPSILON = 1e-06
GUIDE_EXTRA = 4.0
SHIFT_FACTOR = 5.0
LANES = 128


def sigma_at(step_number):
    remain = 1.0 - step_number.astype(jnp.float32) / NSTEP
    return SHIFT_FACTOR * remain / (1.0 + (SHIFT_FACTOR - 1.0) * remain)


def band_weights(skip_flags, step_index, band_gain):
    current = step_index[0]
    counter = jnp.arange(NSTEP, dtype=jnp.int32)
    computed = (skip_flags == 0) & (counter <= current)
    last_full = jnp.max(jnp.where(computed, counter, -1))
    spacing = (current - last_full).astype(jnp.float32)
    gap_ratio = spacing / (spacing + 2.0)
    return (band_gain[0] * (1.0 + gap_ratio), band_gain[1] * (1.0 - 0.5 * gap_ratio))


def split(value):
    high = value.astype(jnp.bfloat16)
    return high, (value - high.astype(jnp.float32)).astype(jnp.bfloat16)


def dot3(left, right, contract=((1,), (0,))):
    (lh, ll), (rh, rl) = left, right

    def dot(one, other):
        return lax.dot_general(
            one, other, (contract, ((), ())), preferred_element_type=jnp.float32
        )

    return dot(lh, rh) + (dot(ll, rh) + dot(lh, rl))


def iota(shape, axis):
    return lax.broadcasted_iota(jnp.int32, shape, axis)


class Layout:
    def __init__(self, local_rows, local_tokens):
        self.rows = local_rows
        self.tokens = local_tokens
        self.channels = local_rows // 4
        self.members = PH * PW // local_tokens
        bits = self.members.bit_length() - 1
        self.near = 1 << (bits // 2)
        self.far = self.members // self.near
        self.span = max(
            (p * local_tokens % PW + local_tokens + PW - 1) // PW
            for p in range(self.members)
        )
        self.lines = 2 * self.span

    def owners(self, position):
        givers = [position ^ (k * self.near) for k in self.far_order()]
        takers = [position ^ m for m in self.near_order()]
        return givers, takers

    def far_order(self):
        return [0, *range(2, self.far), 1][: self.far]

    def near_order(self):
        return [0, *range(self.near - 1, 0, -1)]

    def offset(self, owner):
        return lax.rem(owner * self.tokens, PW)

    def tiles(self, r):
        return range((r * PW - PW + 1) // LANES, (r * PW + PW - 1) // LANES + 1)

    def first_line(self, owner):
        return 2 * (owner * self.tokens // PW)


def cosine_of_turns(turns):
    angle = 2.0 * math.pi * (0.25 - jnp.abs(turns - 0.5))
    square = angle * angle
    series = jnp.full_like(square, -1.0 / math.factorial(11))
    for power in (9, 7, 5, 3, 1):
        series = series * square + (-1.0) ** (power // 2) / math.factorial(power)
    return -angle * series


def waves(places, length):
    phase = (places * iota(places.shape, 1)).astype(jnp.float32)
    phase = phase - length * jnp.floor((phase + 0.5) * (1.0 / length))
    turns = phase * (1.0 / length)
    later = jnp.where(turns < 0.25, turns + 0.75, turns - 0.25)
    return jnp.concatenate([cosine_of_turns(turns), cosine_of_turns(later)], axis=1)


def kept_modes(shape, length, cutoff):
    modes = iota(shape, 1)
    weight = jnp.where((modes == 0) | (2 * modes == length), 1.0, 2.0) / length
    kept = jnp.where((modes <= cutoff) & (2 * modes <= length), weight, 0.0)
    return jnp.concatenate([kept, kept], axis=1)


def bands_kernel(layout, cut_rows, cut_cols, col_filter, *row_filters):
    seq_index = lax.axis_index("seq")
    position = lax.rem(seq_index, layout.members)
    frame = seq_index // layout.members

    column = iota((PW, LANES), 0)
    gap = jnp.zeros((LANES - PW, 2 * LANES), jnp.float32)
    table = jnp.concatenate([waves(2 * column, W), gap, waves(2 * column + 1, W), gap], axis=0)

    def tables(owners):
        line = iota((len(owners) * layout.lines, LANES), 0)
        places = line
        for n, owner in enumerate(owners):
            start = layout.first_line(owner) - n * layout.lines
            places = jnp.where(line >= n * layout.lines, line + start, places)
        return waves(places, H)

    givers, takers = layout.owners(position)
    given = tables(givers)
    taken = tables(takers)
    kept = kept_modes((2 * LANES, LANES), W, cut_cols[frame])
    high, low = split(dot3(split(table * kept), split(table), ((1,), (1,))))
    for n, part in enumerate((high, high, low)):
        col_filter[n * 2 * LANES : (n + 1) * 2 * LANES, :] = part
    kept = kept_modes((given.shape[0], LANES), H, cut_rows[frame])
    small = dot3(split(taken), split(given * kept), ((1,), (1,)))
    wide = given.shape[0]
    size = wide * layout.channels
    spread = (iota((wide, size), 1) // layout.channels == iota((wide, size), 0)).astype(
        jnp.bfloat16
    )
    shape = (layout.channels, size)
    same = lax.rem(iota(shape, 1), layout.channels) == iota(shape, 0)
    each = size // len(row_filters)
    for part, spots in zip(split(small), ((0, 2), (1,))):
        repeated = jnp.dot(part, spread, preferred_element_type=jnp.float32)
        for n in range(taken.shape[0]):
            block = jnp.where(same, repeated[n : n + 1], 0.0).astype(jnp.bfloat16)
            place = slice(n * layout.channels, (n + 1) * layout.channels)
            for half, out in enumerate(row_filters):
                for spot in spots:
                    out[place, spot * each : (spot + 1) * each] = block[
                        :, half * each : (half + 1) * each
                    ]


def product(left, right):
    return jnp.dot(left, right, preferred_element_type=jnp.float32)


def filtered(layout, slots, sources, col_filter, scratch):
    span, channels, tokens = layout.span, layout.channels, layout.tokens
    window, lines, data = scratch
    givers, _ = layout.owners(lax.rem(lax.axis_index("seq"), layout.members))
    lane = iota((layout.rows, LANES), 1)
    chunks = window.shape[1] // LANES
    blank = jnp.zeros((layout.rows, LANES), jnp.float32)
    window[...] = jnp.zeros_like(window)
    for k, (slot, source) in enumerate(zip(slots, sources)):
        window[:, :tokens] = source[...]
        tiles = [window[:, g * LANES : (g + 1) * LANES] for g in range(chunks)]
        for r in range(span):
            start = r * PW - layout.offset(givers[slot])
            line = None
            for g in layout.tiles(r):
                if 0 <= g < chunks:
                    turned = pltpu.roll(tiles[g], lax.rem(layout.span * LANES - start, LANES), 1)
                else:
                    turned = blank
                line = turned if line is None else jnp.where(lane >= g * LANES - start, turned, line)
            lines[r] = line
        for r in range(span):
            for dy in range(2):
                first = ((k * span + r) * 2 + dy) * channels
                for dx in range(2):
                    high, low = split(lines[r, pl.ds(2 * dy + dx, channels, stride=4), :])
                    for n, part in enumerate((high, low, high)):
                        left = (2 * n + dx) * LANES
                        data[first : first + channels, left : left + LANES] = part
    each = layout.lines * channels
    halves = [
        split(product(data[k * each : (k + 1) * each, :], col_filter[...]))
        for k in range(len(slots))
    ]
    high, low = (jnp.concatenate(h, axis=0) for h in zip(*halves))
    return jnp.concatenate([high, high, low], axis=0)


def early_kernel(layout, slots, col_filter, row_filter, *refs):
    sources, carry = refs[: len(slots)], refs[len(slots)]
    data = filtered(layout, slots, sources, col_filter, refs[len(slots) + 1 :])
    carry[...] = product(row_filter[...], data)


def place_part(layout, mixed, taker, out):
    span, channels, tokens = layout.span, layout.channels, layout.tokens
    lane = iota((channels, LANES), 1)
    starts = [r * PW - layout.offset(taker) for r in range(span)]
    for dy in range(2):
        for dx in range(2):
            placed = [None] * pl.cdiv(tokens, LANES)
            for r, start in enumerate(starts):
                first = (r * 2 + dy) * channels
                line = mixed[first : first + channels, dx * LANES : (dx + 1) * LANES]
                line = pltpu.roll(line, lax.rem(start + LANES, LANES), 1)
                for g in layout.tiles(r):
                    if 0 <= g < len(placed):
                        place = lane + (g * LANES - start)
                        value = jnp.where((place >= 0) & (place < LANES), line, 0.0)
                        placed[g] = value if placed[g] is None else placed[g] + value
            first = (dy * 2 + dx) * channels
            for g, value in enumerate(placed):
                last = min(tokens, (g + 1) * LANES)
                out[first : first + channels, g * LANES : last] = value[:, : last - g * LANES]


def first_kernel(layout, slots, m, col_filter, row_filter, carry, *refs):
    sources = refs[: len(slots)]
    out, data = refs[len(slots) : len(slots) + 2]
    found = filtered(layout, slots, sources, col_filter, refs[len(slots) + 2 :])
    data[...] = found
    each = layout.lines * layout.channels
    _, takers = layout.owners(lax.rem(lax.axis_index("seq"), layout.members))
    rows = slice(m * each, (m + 1) * each)
    place_part(layout, carry[rows, :] + product(row_filter[rows, :], found), takers[m], out)


def rest_kernel(layout, others, row_filter, carry, data, *outs):
    _, takers = layout.owners(lax.rem(lax.axis_index("seq"), layout.members))
    each = layout.lines * layout.channels
    for m, out in zip(others, outs):
        rows = slice(m * each, (m + 1) * each)
        mixed = carry[rows, :] + product(row_filter[rows, :], data[...])
        place_part(layout, mixed, takers[m], out)


def norm_rows(hidden, modulation, scale, normed, start, stop, unroll=False):
    tiles = [slice(t, t + LANES) for t in range(0, hidden.shape[1], LANES)]
    block, pair = 16, 2
    scale[...] = 1.0 + modulation[1:2, :]

    def moments(rows, count):
        sums = [jnp.zeros((count, LANES), jnp.float32) for _ in range(2)]
        squares = list(sums)
        for t, columns in enumerate(tiles):
            value = hidden[rows, columns].astype(jnp.float32)
            sums[t % 2] += value
            squares[t % 2] += value * value
        average = jnp.sum(sums[0] + sums[1], axis=1, keepdims=True) / D
        square = jnp.sum(squares[0] + squares[1], axis=1, keepdims=True) / D
        scale_inv = lax.rsqrt(square - average * average + EPSILON)
        return [jnp.broadcast_to(v, (count, LANES)) for v in (average, scale_inv)]

    def norm(rows, place, average, scale_inv):
        for columns in tiles:
            value = hidden[rows, columns].astype(jnp.float32)
            value = (value - average) * scale_inv
            value = value * scale[:, columns] + modulation[0:1, columns]
            normed[place, columns] = value.astype(jnp.bfloat16)

    whole = (stop - start) // (block * pair)

    @pl.loop(0, whole, unroll=unroll)
    def _(n):
        first = pl.multiple_of(n * (block * pair), block)
        rows = [pl.ds(start + first + p * block, block) for p in range(pair)]
        found = [moments(r, block) for r in rows]
        for p in range(pair):
            norm(rows[p], pl.ds(first + p * block, block), *found[p])

    for first in range(start + whole * block * pair, stop, block):
        rows = slice(first, min(stop, first + block))
        found = moments(rows, rows.stop - first)
        norm(rows, slice(first - start, rows.stop - start), *found)


def norm_kernel(hidden, modulation, normed, scale):
    norm_rows(hidden, modulation, scale, normed, 0, normed.shape[0], unroll=True)


def project_kernel(
    layout,
    early_normed,
    hidden,
    modulation,
    weight,
    bias,
    residual,
    band_gain,
    skip_flags,
    step_index,
    base,
    row_low,
    step,
    normed,
    scale,
):
    tokens, first = hidden.shape[0], early_normed.shape[0]
    current = jnp.full((1, 1), step_index[0], jnp.int32)
    counter = iota(skip_flags.shape, 1)
    computed = (skip_flags[...] == 0) & (counter <= current)
    last_full = jnp.max(jnp.where(computed, counter, -1), axis=1, keepdims=True)
    spacing = (current - last_full).astype(jnp.float32)
    gap_ratio = spacing / (spacing + 2.0)
    shape = (layout.rows, layout.channels)
    own = iota(shape, 0) // 4 == iota(shape, 1)
    w_low, w_high = (
        jnp.sum(jnp.where(own, band_gain[n : n + 1, :], 0.0), axis=1, keepdims=True) * factor
        for n, factor in enumerate((1.0 + gap_ratio, 1.0 - 0.5 * gap_ratio))
    )

    def project(rows, columns):
        conditional = lax.dot_general(
            rows[...], weight[...], (((1,), (1,)), ((), ())), preferred_element_type=jnp.float32
        )
        conditional = (conditional + bias[...]).T
        base[:, columns] = conditional + GUIDE_EXTRA * w_high * residual[:, columns]

    if first:
        project(early_normed, slice(0, first))
    norm_rows(hidden, modulation, scale, normed, first, tokens, unroll=True)
    project(normed, slice(first, tokens))
    row_low[...] = jnp.broadcast_to(GUIDE_EXTRA * (w_low - w_high), row_low.shape)
    step[...] = jnp.broadcast_to(sigma_at(current + 1) - sigma_at(current), step.shape)


def finish_kernel(layout, *refs):
    near, channels, tokens = layout.near, layout.channels, layout.tokens
    parts = refs[:near]
    base, row_low, step, latent, velocity, latent_next, total = refs[near:]
    for g in range(total.shape[0]):
        last = min(tokens, (g + 1) * LANES)
        columns = slice(g * LANES, last)
        width = slice(0, last - g * LANES)
        low_band = parts[0][:, columns]
        for m in range(1, near):
            low_band += parts[m][:, columns]
        total[g, :, width] = low_band
        for c in range(channels):
            rows = slice(4 * c, 4 * c + 4)
            low_band = total[g, pl.ds(c, 4, stride=channels), :][:, width]
            value = base[rows, columns] + row_low[rows, width] * low_band
            velocity[rows, columns] = value
            latent_next[rows, columns] = latent[rows, columns] + step[:4, width] * value


VMEM = pl.BlockSpec(memory_space=pltpu.VMEM)
SMEM = pl.BlockSpec(memory_space=pltpu.SMEM)


def bands(layout, cut_rows, cut_cols):
    wide = layout.far * layout.lines * layout.channels
    tall = layout.near * layout.lines * layout.channels
    col = jax.ShapeDtypeStruct((6 * LANES, 2 * LANES), jnp.bfloat16)
    row = jax.ShapeDtypeStruct((tall, 3 * wide // 2), jnp.bfloat16)
    return pl.pallas_call(
        functools.partial(bands_kernel, layout),
        out_shape=[col, row, row],
        in_specs=[SMEM, SMEM],
        out_specs=[VMEM] * 3,
        compiler_params=pltpu.CompilerParams(vmem_limit_bytes=8 * 2**20),
        cost_estimate=pl.CostEstimate(flops=10**9, bytes_accessed=2 * 10**7, transcendentals=0),
        name="bands",
    )(cut_rows, cut_cols)


def mix_scratch(layout, count):
    return [
        pltpu.VMEM((layout.rows, pl.cdiv(layout.tokens, LANES) * LANES), jnp.float32),
        pltpu.VMEM((layout.span, layout.rows, LANES), jnp.float32),
        pltpu.VMEM((count * layout.lines * layout.channels, 6 * LANES), jnp.bfloat16),
    ]


def early(layout, filters, slots, sources):
    tall = layout.near * layout.lines * layout.channels
    return pl.pallas_call(
        functools.partial(early_kernel, layout, slots),
        out_shape=jax.ShapeDtypeStruct((tall, 2 * LANES), jnp.float32),
        in_specs=[VMEM] * (2 + len(slots)),
        out_specs=VMEM,
        scratch_shapes=mix_scratch(layout, len(slots)),
        compiler_params=pltpu.CompilerParams(vmem_limit_bytes=8 * 2**20),
        cost_estimate=pl.CostEstimate(flops=10**9, bytes_accessed=10**6, transcendentals=0),
        name="early",
    )(*filters, *sources)


def mix_first(layout, filters, carry, slots, sources, m):
    wide = len(slots) * layout.lines * layout.channels
    return pl.pallas_call(
        functools.partial(first_kernel, layout, slots, m),
        out_shape=[
            jax.ShapeDtypeStruct((layout.rows, layout.tokens), jnp.float32),
            jax.ShapeDtypeStruct((3 * wide, 2 * LANES), jnp.bfloat16),
        ],
        in_specs=[VMEM] * (3 + len(slots)),
        out_specs=[VMEM] * 2,
        scratch_shapes=mix_scratch(layout, len(slots)),
        compiler_params=pltpu.CompilerParams(vmem_limit_bytes=8 * 2**20),
        cost_estimate=pl.CostEstimate(flops=10**9, bytes_accessed=10**6, transcendentals=0),
        name="mix_first",
    )(*filters, carry, *sources)


def mix_rest(layout, row_filter, carry, data, others):
    shape = jax.ShapeDtypeStruct((layout.rows, layout.tokens), jnp.float32)
    return pl.pallas_call(
        functools.partial(rest_kernel, layout, others),
        out_shape=[shape] * len(others),
        in_specs=[VMEM] * 3,
        out_specs=[VMEM] * len(others),
        compiler_params=pltpu.CompilerParams(vmem_limit_bytes=8 * 2**20),
        cost_estimate=pl.CostEstimate(flops=10**9, bytes_accessed=10**6, transcendentals=0),
        name="mix_rest",
    )(row_filter, carry, data)


def head(layout, hidden, modulation, head_weight, head_bias, residual, gain, flags, step_index):
    first = hidden.shape[0] // LANES * LANES
    scale = pltpu.VMEM((1, hidden.shape[1]), jnp.float32)
    normed = pl.pallas_call(
        norm_kernel,
        out_shape=jax.ShapeDtypeStruct((first, hidden.shape[1]), jnp.bfloat16),
        in_specs=[VMEM] * 2,
        out_specs=VMEM,
        scratch_shapes=[scale],
        compiler_params=pltpu.CompilerParams(vmem_limit_bytes=8 * 2**20),
        cost_estimate=pl.CostEstimate(
            flops=10 * hidden.size, bytes_accessed=10**7, transcendentals=0
        ),
        name="norm",
    )(hidden, modulation)
    return pl.pallas_call(
        functools.partial(project_kernel, layout),
        out_shape=[
            jax.ShapeDtypeStruct(residual.shape, jnp.float32),
            jax.ShapeDtypeStruct((layout.rows, LANES), jnp.float32),
            jax.ShapeDtypeStruct((8, LANES), jnp.float32),
        ],
        in_specs=[VMEM] * 8 + [SMEM],
        out_specs=[VMEM] * 3,
        scratch_shapes=[
            pltpu.VMEM((hidden.shape[0] - first, hidden.shape[1]), jnp.bfloat16),
            scale,
        ],
        compiler_params=pltpu.CompilerParams(vmem_limit_bytes=8 * 2**20),
        cost_estimate=pl.CostEstimate(
            flops=2 * hidden.size * layout.rows, bytes_accessed=3 * 10**6, transcendentals=0
        ),
        name="project",
    )(
        normed,
        hidden,
        modulation,
        head_weight.T,
        head_bias.reshape(1, -1),
        residual,
        gain,
        flags.reshape(1, -1),
        step_index,
    )


def head_in_parts(
    layout, hidden, modulation, head_weight, head_bias, residual, gain, flags, step_index
):
    values = hidden.astype(jnp.float32)
    moments = lax.psum((jnp.sum(values, axis=1), jnp.sum(values * values, axis=1)), "mp")
    average = moments[0] / D
    scale_inv = lax.rsqrt(moments[1] / D - average * average + EPSILON)
    normed = (
        (values - average[:, None]) * scale_inv[:, None] * (1.0 + modulation[1]) + modulation[0]
    ).astype(jnp.bfloat16)
    conditional = (
        lax.psum_scatter(
            lax.dot_general(
                head_weight, normed, (((0,), (1,)), ((), ())), preferred_element_type=jnp.float32
            ),
            "mp",
            scatter_dimension=0,
            tiled=True,
        )
        + head_bias[:, None]
    )
    w_low, w_high = band_weights(flags, step_index, gain)
    row_high = GUIDE_EXTRA * jnp.repeat(w_high, 4)[:, None]
    row_low = GUIDE_EXTRA * jnp.repeat(w_low - w_high, 4)[:, None]
    current = step_index[0]
    return (
        conditional + row_high * residual,
        jnp.broadcast_to(row_low, (layout.rows, LANES)),
        jnp.broadcast_to(sigma_at(current + 1) - sigma_at(current), (8, LANES)),
    )


def finish(layout, parts, base, row_low, step, latent):
    shape = jax.ShapeDtypeStruct((layout.rows, layout.tokens), jnp.float32)
    return pl.pallas_call(
        functools.partial(finish_kernel, layout),
        out_shape=[shape, shape],
        in_specs=[VMEM] * (layout.near + 4),
        out_specs=[VMEM, VMEM],
        scratch_shapes=[
            pltpu.VMEM((pl.cdiv(layout.tokens, LANES), layout.rows, LANES), jnp.float32)
        ],
        compiler_params=pltpu.CompilerParams(vmem_limit_bytes=8 * 2**20),
        name="finish",
    )(*parts, base, row_low, step, latent)


def body(
    hidden,
    modulation,
    head_weight,
    head_bias,
    residual,
    latent,
    band_gain,
    cut_rows,
    cut_cols,
    skip_flags,
    step_index,
):
    layout = Layout(*residual.shape)
    places = lax.axis_size("seq")

    def exchange(values, masks):
        swapped = [values[0]]
        for turn, mask in enumerate(masks[1:]):
            pairs = [(s, s ^ mask) for s in range(places)]
            swapped.append(lax.ppermute(values[turn + 1], "seq", pairs))
        return swapped

    masks = [k * layout.near for k in layout.far_order()]
    sources = exchange([residual] * layout.far, masks)
    col_filter, row_early, row_late = bands(layout, cut_rows, cut_cols)
    run_head = head if lax.axis_size("mp") == 1 else head_in_parts
    base, row_low, step = run_head(
        layout,
        hidden,
        modulation,
        head_weight,
        head_bias,
        residual,
        band_gain,
        skip_flags,
        step_index,
    )
    slots = list(range(layout.far))
    half = layout.far // 2
    carry = early(layout, (col_filter, row_early), slots[:half], sources[:half])
    filters = (col_filter, row_late)
    part, data = mix_first(layout, filters, carry, slots[half:], sources[half:], 1)
    own, *rest = mix_rest(layout, row_late, carry, data, [0, *range(2, layout.near)])
    parts = exchange([own, part, *rest], layout.near_order())
    return finish(layout, parts, base, row_low, step, latent)


def solution(mesh):
    in_specs = (
        P(("groups", "seq"), "mp"),
        P("groups", "mp"),
        P("mp", None),
        P("mp"),
        P("mp", ("groups", "seq")),
        P("mp", ("groups", "seq")),
        P(None, "mp"),
        P("groups"),
        P("groups"),
        P("groups"),
        P("groups"),
    )
    out_specs = (P("mp", ("groups", "seq")), P("mp", ("groups", "seq")))
    return jax.shard_map(body, mesh=mesh, in_specs=in_specs, out_specs=out_specs, check_vma=False)
```

```python
import functools
import math

import jax
import jax.numpy as jnp
from jax import lax
from jax.experimental import pallas as pl
from jax.experimental.pallas import tpu as pltpu
from jax.sharding import PartitionSpec as P


D = 5120
H = 90
W = 160
PH = 45
PW = 80
NSTEP = 50

EPSILON = 1e-06
GUIDE_EXTRA = 4.0
SHIFT_FACTOR = 5.0
LANES = 128


def sigma_at(step_number):
    remain = 1.0 - step_number.astype(jnp.float32) / NSTEP
    return SHIFT_FACTOR * remain / (1.0 + (SHIFT_FACTOR - 1.0) * remain)


def band_weights(skip_flags, step_index, band_gain):
    current = step_index[0]
    counter = jnp.arange(NSTEP, dtype=jnp.int32)
    computed = (skip_flags == 0) & (counter <= current)
    last_full = jnp.max(jnp.where(computed, counter, -1))
    spacing = (current - last_full).astype(jnp.float32)
    gap_ratio = spacing / (spacing + 2.0)
    return (band_gain[0] * (1.0 + gap_ratio), band_gain[1] * (1.0 - 0.5 * gap_ratio))


def split(value):
    high = value.astype(jnp.bfloat16)
    return high, (value - high.astype(jnp.float32)).astype(jnp.bfloat16)


def dot3(left, right, contract=((1,), (0,))):
    (lh, ll), (rh, rl) = left, right

    def dot(one, other):
        return lax.dot_general(
            one, other, (contract, ((), ())), preferred_element_type=jnp.float32
        )

    return dot(lh, rh) + (dot(ll, rh) + dot(lh, rl))


def iota(shape, axis):
    return lax.broadcasted_iota(jnp.int32, shape, axis)


class Layout:
    def __init__(self, local_rows, local_tokens):
        self.rows = local_rows
        self.tokens = local_tokens
        self.channels = local_rows // 4
        self.members = PH * PW // local_tokens
        bits = self.members.bit_length() - 1
        self.near = 1 << (bits // 2)
        self.far = self.members // self.near
        self.span = max(
            (p * local_tokens % PW + local_tokens + PW - 1) // PW
            for p in range(self.members)
        )
        self.lines = 2 * self.span

    def owners(self, position):
        givers = [position ^ (k * self.near) for k in self.far_order()]
        takers = [position ^ m for m in self.near_order()]
        return givers, takers

    def far_order(self):
        return [0, *range(2, self.far), 1][: self.far]

    def near_order(self):
        return [0, *range(self.near - 1, 0, -1)]

    def offset(self, owner):
        return lax.rem(owner * self.tokens, PW)

    def tiles(self, r):
        return range((r * PW - PW + 1) // LANES, (r * PW + PW - 1) // LANES + 1)

    def first_line(self, owner):
        return 2 * (owner * self.tokens // PW)


def cosine_of_turns(turns):
    angle = 2.0 * math.pi * (0.25 - jnp.abs(turns - 0.5))
    square = angle * angle
    series = jnp.full_like(square, -1.0 / math.factorial(11))
    for power in (9, 7, 5, 3, 1):
        series = series * square + (-1.0) ** (power // 2) / math.factorial(power)
    return -angle * series


def waves(places, length):
    phase = (places * iota(places.shape, 1)).astype(jnp.float32)
    phase = phase - length * jnp.floor((phase + 0.5) * (1.0 / length))
    turns = phase * (1.0 / length)
    later = jnp.where(turns < 0.25, turns + 0.75, turns - 0.25)
    return jnp.concatenate([cosine_of_turns(turns), cosine_of_turns(later)], axis=1)


def kept_modes(shape, length, cutoff):
    modes = iota(shape, 1)
    weight = jnp.where((modes == 0) | (2 * modes == length), 1.0, 2.0) / length
    kept = jnp.where((modes <= cutoff) & (2 * modes <= length), weight, 0.0)
    return jnp.concatenate([kept, kept], axis=1)


def bands_kernel(layout, cut_rows, cut_cols, col_filter, *row_filters):
    seq_index = lax.axis_index("seq")
    position = lax.rem(seq_index, layout.members)
    frame = seq_index // layout.members

    column = iota((PW, LANES), 0)
    gap = jnp.zeros((LANES - PW, 2 * LANES), jnp.float32)
    table = jnp.concatenate([waves(2 * column, W), gap, waves(2 * column + 1, W), gap], axis=0)

    def tables(owners):
        line = iota((len(owners) * layout.lines, LANES), 0)
        places = line
        for n, owner in enumerate(owners):
            start = layout.first_line(owner) - n * layout.lines
            places = jnp.where(line >= n * layout.lines, line + start, places)
        return waves(places, H)

    givers, takers = layout.owners(position)
    given = tables(givers)
    taken = tables(takers)
    kept = kept_modes((2 * LANES, LANES), W, cut_cols[frame])
    high, low = split(dot3(split(table * kept), split(table), ((1,), (1,))))
    for n, part in enumerate((high, high, low)):
        col_filter[n * 2 * LANES : (n + 1) * 2 * LANES, :] = part
    kept = kept_modes((given.shape[0], LANES), H, cut_rows[frame])
    small = dot3(split(taken), split(given * kept), ((1,), (1,)))
    wide = given.shape[0]
    size = wide * layout.channels
    spread = (iota((wide, size), 1) // layout.channels == iota((wide, size), 0)).astype(
        jnp.bfloat16
    )
    shape = (layout.channels, size)
    same = lax.rem(iota(shape, 1), layout.channels) == iota(shape, 0)
    each = size // len(row_filters)
    for part, spots in zip(split(small), ((0, 2), (1,))):
        repeated = jnp.dot(part, spread, preferred_element_type=jnp.float32)
        for n in range(taken.shape[0]):
            block = jnp.where(same, repeated[n : n + 1], 0.0).astype(jnp.bfloat16)
            place = slice(n * layout.channels, (n + 1) * layout.channels)
            for half, out in enumerate(row_filters):
                for spot in spots:
                    out[place, spot * each : (spot + 1) * each] = block[
                        :, half * each : (half + 1) * each
                    ]


def product(left, right):
    return jnp.dot(left, right, preferred_element_type=jnp.float32)


def filtered(layout, slots, sources, col_filter, scratch):
    span, channels, tokens = layout.span, layout.channels, layout.tokens
    window, lines, data = scratch
    givers, _ = layout.owners(lax.rem(lax.axis_index("seq"), layout.members))
    lane = iota((layout.rows, LANES), 1)
    chunks = window.shape[1] // LANES
    blank = jnp.zeros((layout.rows, LANES), jnp.float32)
    window[...] = jnp.zeros_like(window)
    for k, (slot, source) in enumerate(zip(slots, sources)):
        window[:, :tokens] = source[...]
        tiles = [window[:, g * LANES : (g + 1) * LANES] for g in range(chunks)]
        for r in range(span):
            start = r * PW - layout.offset(givers[slot])
            line = None
            for g in layout.tiles(r):
                if 0 <= g < chunks:
                    turned = pltpu.roll(tiles[g], lax.rem(layout.span * LANES - start, LANES), 1)
                else:
                    turned = blank
                line = turned if line is None else jnp.where(lane >= g * LANES - start, turned, line)
            lines[r] = line
        for r in range(span):
            for dy in range(2):
                first = ((k * span + r) * 2 + dy) * channels
                for dx in range(2):
                    high, low = split(lines[r, pl.ds(2 * dy + dx, channels, stride=4), :])
                    for n, part in enumerate((high, low, high)):
                        left = (2 * n + dx) * LANES
                        data[first : first + channels, left : left + LANES] = part
    each = layout.lines * channels
    halves = [
        split(product(data[k * each : (k + 1) * each, :], col_filter[...]))
        for k in range(len(slots))
    ]
    high, low = (jnp.concatenate(h, axis=0) for h in zip(*halves))
    return jnp.concatenate([high, high, low], axis=0)


def early_kernel(layout, slots, col_filter, row_filter, *refs):
    sources, carry = refs[: len(slots)], refs[len(slots)]
    data = filtered(layout, slots, sources, col_filter, refs[len(slots) + 1 :])
    carry[...] = product(row_filter[...], data)


def place_part(layout, mixed, taker, out):
    span, channels, tokens = layout.span, layout.channels, layout.tokens
    lane = iota((channels, LANES), 1)
    starts = [r * PW - layout.offset(taker) for r in range(span)]
    for dy in range(2):
        for dx in range(2):
            placed = [None] * pl.cdiv(tokens, LANES)
            for r, start in enumerate(starts):
                first = (r * 2 + dy) * channels
                line = mixed[first : first + channels, dx * LANES : (dx + 1) * LANES]
                line = pltpu.roll(line, lax.rem(start + LANES, LANES), 1)
                for g in layout.tiles(r):
                    if 0 <= g < len(placed):
                        place = lane + (g * LANES - start)
                        value = jnp.where((place >= 0) & (place < LANES), line, 0.0)
                        placed[g] = value if placed[g] is None else placed[g] + value
            first = (dy * 2 + dx) * channels
            for g, value in enumerate(placed):
                last = min(tokens, (g + 1) * LANES)
                out[first : first + channels, g * LANES : last] = value[:, : last - g * LANES]


def first_kernel(layout, slots, m, col_filter, row_filter, carry, *refs):
    sources = refs[: len(slots)]
    out, data = refs[len(slots) : len(slots) + 2]
    found = filtered(layout, slots, sources, col_filter, refs[len(slots) + 2 :])
    data[...] = found
    each = layout.lines * layout.channels
    _, takers = layout.owners(lax.rem(lax.axis_index("seq"), layout.members))
    rows = slice(m * each, (m + 1) * each)
    place_part(layout, carry[rows, :] + product(row_filter[rows, :], found), takers[m], out)


def rest_kernel(layout, others, row_filter, carry, data, *outs):
    _, takers = layout.owners(lax.rem(lax.axis_index("seq"), layout.members))
    each = layout.lines * layout.channels
    for m, out in zip(others, outs):
        rows = slice(m * each, (m + 1) * each)
        mixed = carry[rows, :] + product(row_filter[rows, :], data[...])
        place_part(layout, mixed, takers[m], out)


def norm_rows(hidden, modulation, scale, normed, start, stop, unroll=False):
    tiles = [slice(t, t + LANES) for t in range(0, hidden.shape[1], LANES)]
    block, pair = 16, 2
    scale[...] = 1.0 + modulation[1:2, :]

    def moments(rows, count):
        sums = [jnp.zeros((count, LANES), jnp.float32) for _ in range(2)]
        squares = list(sums)
        for t, columns in enumerate(tiles):
            value = hidden[rows, columns].astype(jnp.float32)
            sums[t % 2] += value
            squares[t % 2] += value * value
        average = jnp.sum(sums[0] + sums[1], axis=1, keepdims=True) / D
        square = jnp.sum(squares[0] + squares[1], axis=1, keepdims=True) / D
        scale_inv = lax.rsqrt(square - average * average + EPSILON)
        return [jnp.broadcast_to(v, (count, LANES)) for v in (average, scale_inv)]

    def norm(rows, place, average, scale_inv):
        for columns in tiles:
            value = hidden[rows, columns].astype(jnp.float32)
            value = (value - average) * scale_inv
            value = value * scale[:, columns] + modulation[0:1, columns]
            normed[place, columns] = value.astype(jnp.bfloat16)

    whole = (stop - start) // (block * pair)

    @pl.loop(0, whole, unroll=unroll)
    def _(n):
        first = pl.multiple_of(n * (block * pair), block)
        rows = [pl.ds(start + first + p * block, block) for p in range(pair)]
        found = [moments(r, block) for r in rows]
        for p in range(pair):
            norm(rows[p], pl.ds(first + p * block, block), *found[p])

    for first in range(start + whole * block * pair, stop, block):
        rows = slice(first, min(stop, first + block))
        found = moments(rows, rows.stop - first)
        norm(rows, slice(first - start, rows.stop - start), *found)


def norm_kernel(hidden, modulation, normed, scale):
    norm_rows(hidden, modulation, scale, normed, 0, normed.shape[0], unroll=True)


def project_kernel(
    layout,
    early_normed,
    hidden,
    modulation,
    weight,
    bias,
    residual,
    band_gain,
    skip_flags,
    step_index,
    base,
    row_low,
    step,
    normed,
    scale,
):
    tokens, first = hidden.shape[0], early_normed.shape[0]
    current = jnp.full((1, 1), step_index[0], jnp.int32)
    counter = iota(skip_flags.shape, 1)
    computed = (skip_flags[...] == 0) & (counter <= current)
    last_full = jnp.max(jnp.where(computed, counter, -1), axis=1, keepdims=True)
    spacing = (current - last_full).astype(jnp.float32)
    gap_ratio = spacing / (spacing + 2.0)
    shape = (layout.rows, layout.channels)
    own = iota(shape, 0) // 4 == iota(shape, 1)
    w_low, w_high = (
        jnp.sum(jnp.where(own, band_gain[n : n + 1, :], 0.0), axis=1, keepdims=True) * factor
        for n, factor in enumerate((1.0 + gap_ratio, 1.0 - 0.5 * gap_ratio))
    )

    def project(rows, columns):
        conditional = lax.dot_general(
            rows[...], weight[...], (((1,), (1,)), ((), ())), preferred_element_type=jnp.float32
        )
        conditional = (conditional + bias[...]).T
        base[:, columns] = conditional + GUIDE_EXTRA * w_high * residual[:, columns]

    if first:
        project(early_normed, slice(0, first))
    norm_rows(hidden, modulation, scale, normed, first, tokens, unroll=True)
    project(normed, slice(first, tokens))
    row_low[...] = jnp.broadcast_to(GUIDE_EXTRA * (w_low - w_high), row_low.shape)
    step[...] = jnp.broadcast_to(sigma_at(current + 1) - sigma_at(current), step.shape)


def finish_kernel(layout, *refs):
    near, channels, tokens = layout.near, layout.channels, layout.tokens
    parts = refs[:near]
    base, row_low, step, latent, velocity_hbm, latent_next_hbm = refs[near : near + 6]
    total, velocity, latent_next, sems = refs[near + 6 :]
    for g in range(total.shape[0]):
        last = min(tokens, (g + 1) * LANES)
        columns = slice(g * LANES, last)
        low_band = parts[0][:, columns]
        for m in range(1, near):
            low_band += parts[m][:, columns]
        total[g, :, : last - g * LANES] = low_band
    copies = []
    for half in range(2):
        for c in range(half * channels // 2, (half + 1) * channels // 2):
            rows = slice(4 * c, 4 * c + 4)
            for g in range(total.shape[0]):
                last = min(tokens, (g + 1) * LANES)
                columns = slice(g * LANES, last)
                width = slice(0, last - g * LANES)
                low_band = total[g, pl.ds(c, 4, stride=channels), :][:, width]
                value = base[rows, columns] + row_low[rows, width] * low_band
                velocity[rows, columns] = value
                latent_next[rows, columns] = latent[rows, columns] + step[:4, width] * value
        rows = slice(half * 2 * channels, (half + 1) * 2 * channels)
        for n, (here, there) in enumerate(
            ((velocity, velocity_hbm), (latent_next, latent_next_hbm))
        ):
            copy = pltpu.make_async_copy(here.at[rows], there.at[rows], sems.at[half, n])
            copy.start()
            copies.append(copy)
    for copy in copies:
        copy.wait()


VMEM = pl.BlockSpec(memory_space=pltpu.VMEM)
HBM = pl.BlockSpec(memory_space=pltpu.HBM)
SMEM = pl.BlockSpec(memory_space=pltpu.SMEM)


def bands(layout, cut_rows, cut_cols):
    wide = layout.far * layout.lines * layout.channels
    tall = layout.near * layout.lines * layout.channels
    col = jax.ShapeDtypeStruct((6 * LANES, 2 * LANES), jnp.bfloat16)
    row = jax.ShapeDtypeStruct((tall, 3 * wide // 2), jnp.bfloat16)
    return pl.pallas_call(
        functools.partial(bands_kernel, layout),
        out_shape=[col, row, row],
        in_specs=[SMEM, SMEM],
        out_specs=[VMEM] * 3,
        compiler_params=pltpu.CompilerParams(vmem_limit_bytes=8 * 2**20),
        cost_estimate=pl.CostEstimate(flops=10**9, bytes_accessed=2 * 10**7, transcendentals=0),
        name="bands",
    )(cut_rows, cut_cols)


def mix_scratch(layout, count):
    return [
        pltpu.VMEM((layout.rows, pl.cdiv(layout.tokens, LANES) * LANES), jnp.float32),
        pltpu.VMEM((layout.span, layout.rows, LANES), jnp.float32),
        pltpu.VMEM((count * layout.lines * layout.channels, 6 * LANES), jnp.bfloat16),
    ]


def early(layout, filters, slots, sources):
    tall = layout.near * layout.lines * layout.channels
    return pl.pallas_call(
        functools.partial(early_kernel, layout, slots),
        out_shape=jax.ShapeDtypeStruct((tall, 2 * LANES), jnp.float32),
        in_specs=[VMEM] * (2 + len(slots)),
        out_specs=VMEM,
        scratch_shapes=mix_scratch(layout, len(slots)),
        compiler_params=pltpu.CompilerParams(vmem_limit_bytes=8 * 2**20),
        cost_estimate=pl.CostEstimate(flops=10**9, bytes_accessed=10**6, transcendentals=0),
        name="early",
    )(*filters, *sources)


def mix_first(layout, filters, carry, slots, sources, m):
    wide = len(slots) * layout.lines * layout.channels
    return pl.pallas_call(
        functools.partial(first_kernel, layout, slots, m),
        out_shape=[
            jax.ShapeDtypeStruct((layout.rows, layout.tokens), jnp.float32),
            jax.ShapeDtypeStruct((3 * wide, 2 * LANES), jnp.bfloat16),
        ],
        in_specs=[VMEM] * (3 + len(slots)),
        out_specs=[VMEM] * 2,
        scratch_shapes=mix_scratch(layout, len(slots)),
        compiler_params=pltpu.CompilerParams(vmem_limit_bytes=8 * 2**20),
        cost_estimate=pl.CostEstimate(flops=10**9, bytes_accessed=10**6, transcendentals=0),
        name="mix_first",
    )(*filters, carry, *sources)


def mix_rest(layout, row_filter, carry, data, others):
    shape = jax.ShapeDtypeStruct((layout.rows, layout.tokens), jnp.float32)
    return pl.pallas_call(
        functools.partial(rest_kernel, layout, others),
        out_shape=[shape] * len(others),
        in_specs=[VMEM] * 3,
        out_specs=[VMEM] * len(others),
        compiler_params=pltpu.CompilerParams(vmem_limit_bytes=8 * 2**20),
        cost_estimate=pl.CostEstimate(flops=10**9, bytes_accessed=10**6, transcendentals=0),
        name="mix_rest",
    )(row_filter, carry, data)


def head(layout, hidden, modulation, head_weight, head_bias, residual, gain, flags, step_index):
    first = hidden.shape[0] // LANES * LANES
    scale = pltpu.VMEM((1, hidden.shape[1]), jnp.float32)
    normed = pl.pallas_call(
        norm_kernel,
        out_shape=jax.ShapeDtypeStruct((first, hidden.shape[1]), jnp.bfloat16),
        in_specs=[VMEM] * 2,
        out_specs=VMEM,
        scratch_shapes=[scale],
        compiler_params=pltpu.CompilerParams(vmem_limit_bytes=8 * 2**20),
        cost_estimate=pl.CostEstimate(
            flops=10 * hidden.size, bytes_accessed=10**7, transcendentals=0
        ),
        name="norm",
    )(hidden, modulation)
    return pl.pallas_call(
        functools.partial(project_kernel, layout),
        out_shape=[
            jax.ShapeDtypeStruct(residual.shape, jnp.float32),
            jax.ShapeDtypeStruct((layout.rows, LANES), jnp.float32),
            jax.ShapeDtypeStruct((8, LANES), jnp.float32),
        ],
        in_specs=[VMEM] * 8 + [SMEM],
        out_specs=[VMEM] * 3,
        scratch_shapes=[
            pltpu.VMEM((hidden.shape[0] - first, hidden.shape[1]), jnp.bfloat16),
            scale,
        ],
        compiler_params=pltpu.CompilerParams(vmem_limit_bytes=8 * 2**20),
        cost_estimate=pl.CostEstimate(
            flops=2 * hidden.size * layout.rows, bytes_accessed=3 * 10**6, transcendentals=0
        ),
        name="project",
    )(
        normed,
        hidden,
        modulation,
        head_weight.T,
        head_bias.reshape(1, -1),
        residual,
        gain,
        flags.reshape(1, -1),
        step_index,
    )


def head_in_parts(
    layout, hidden, modulation, head_weight, head_bias, residual, gain, flags, step_index
):
    values = hidden.astype(jnp.float32)
    moments = lax.psum((jnp.sum(values, axis=1), jnp.sum(values * values, axis=1)), "mp")
    average = moments[0] / D
    scale_inv = lax.rsqrt(moments[1] / D - average * average + EPSILON)
    normed = (
        (values - average[:, None]) * scale_inv[:, None] * (1.0 + modulation[1]) + modulation[0]
    ).astype(jnp.bfloat16)
    conditional = (
        lax.psum_scatter(
            lax.dot_general(
                head_weight, normed, (((0,), (1,)), ((), ())), preferred_element_type=jnp.float32
            ),
            "mp",
            scatter_dimension=0,
            tiled=True,
        )
        + head_bias[:, None]
    )
    w_low, w_high = band_weights(flags, step_index, gain)
    row_high = GUIDE_EXTRA * jnp.repeat(w_high, 4)[:, None]
    row_low = GUIDE_EXTRA * jnp.repeat(w_low - w_high, 4)[:, None]
    current = step_index[0]
    return (
        conditional + row_high * residual,
        jnp.broadcast_to(row_low, (layout.rows, LANES)),
        jnp.broadcast_to(sigma_at(current + 1) - sigma_at(current), (8, LANES)),
    )


def finish(layout, parts, base, row_low, step, latent):
    shape = jax.ShapeDtypeStruct((layout.rows, layout.tokens), jnp.float32)
    return pl.pallas_call(
        functools.partial(finish_kernel, layout),
        out_shape=[shape, shape],
        in_specs=[VMEM] * (layout.near + 4),
        out_specs=[HBM, HBM],
        scratch_shapes=[
            pltpu.VMEM((pl.cdiv(layout.tokens, LANES), layout.rows, LANES), jnp.float32),
            pltpu.VMEM(shape.shape, jnp.float32),
            pltpu.VMEM(shape.shape, jnp.float32),
            pltpu.SemaphoreType.DMA((2, 2)),
        ],
        compiler_params=pltpu.CompilerParams(vmem_limit_bytes=8 * 2**20),
        name="finish",
    )(*parts, base, row_low, step, latent)


def body(
    hidden,
    modulation,
    head_weight,
    head_bias,
    residual,
    latent,
    band_gain,
    cut_rows,
    cut_cols,
    skip_flags,
    step_index,
):
    layout = Layout(*residual.shape)
    places = lax.axis_size("seq")

    def exchange(values, masks):
        swapped = [values[0]]
        for turn, mask in enumerate(masks[1:]):
            pairs = [(s, s ^ mask) for s in range(places)]
            swapped.append(lax.ppermute(values[turn + 1], "seq", pairs))
        return swapped

    masks = [k * layout.near for k in layout.far_order()]
    sources = exchange([residual] * layout.far, masks)
    col_filter, row_early, row_late = bands(layout, cut_rows, cut_cols)
    run_head = head if lax.axis_size("mp") == 1 else head_in_parts
    base, row_low, step = run_head(
        layout,
        hidden,
        modulation,
        head_weight,
        head_bias,
        residual,
        band_gain,
        skip_flags,
        step_index,
    )
    slots = list(range(layout.far))
    half = layout.far // 2
    carry = early(layout, (col_filter, row_early), slots[:half], sources[:half])
    filters = (col_filter, row_late)
    part, data = mix_first(layout, filters, carry, slots[half:], sources[half:], 1)
    own, *rest = mix_rest(layout, row_late, carry, data, [0, *range(2, layout.near)])
    parts = exchange([own, part, *rest], layout.near_order())
    return finish(layout, parts, base, row_low, step, latent)


def solution(mesh):
    in_specs = (
        P(("groups", "seq"), "mp"),
        P("groups", "mp"),
        P("mp", None),
        P("mp"),
        P("mp", ("groups", "seq")),
        P("mp", ("groups", "seq")),
        P(None, "mp"),
        P("groups"),
        P("groups"),
        P("groups"),
        P("groups"),
    )
    out_specs = (P("mp", ("groups", "seq")), P("mp", ("groups", "seq")))
    return jax.shard_map(body, mesh=mesh, in_specs=in_specs, out_specs=out_specs, check_vma=False)
```
